32 devices in a mesh: fsdp: 32 (over z, y, x, core).
Axes of the slice: x: 2, y: 2, z: 4, core: 2. Of those that a mesh axis runs over, the one named last changes fastest.
Arguments:
- tokens: bfloat16 [32768, 1024], P('fsdp'), may hold values from -5 to 5
- cotangent: bfloat16 [32768, 1024], P('fsdp'), may hold values from -6 to 6
- segment: int32 [32768], P('fsdp'), may hold values from -1 to 511, as said below
- w_qkv: bfloat16 [3072, 1024], P('fsdp'), may hold values from -0.09375 to 0.09375
- w_attn_out: bfloat16 [1024, 1024], P('fsdp'), may hold values from -0.75 to 0.75
- w_in: bfloat16 [5248, 1024], P('fsdp'), may hold values from -0.1875 to 0.1875
- w_ff_out: bfloat16 [1024, 2624], P('fsdp'), may hold values from -0.125 to 0.125
- norm_one: bfloat16 [1024], P('fsdp'), may hold values from 0.25 to 1.75
- norm_two: bfloat16 [1024], P('fsdp'), may hold values from 0.25 to 1.75
Outputs:
- output: bfloat16 [32768, 1024], P('fsdp')
- grad_tokens: float32 [32768, 1024], P('fsdp')
- grad_qkv: float32 [3072, 1024], P('fsdp')
- grad_attn_out: float32 [1024, 1024], P('fsdp')
- grad_in: float32 [5248, 1024], P('fsdp')
- grad_ff_out: float32 [1024, 2624], P('fsdp')
- grad_norm_one: float32 [1024], P('fsdp')
- grad_norm_two: float32 [1024], P('fsdp')
The draws below stay inside these ranges and needn't reach their ends.
Inputs may be any that keep to these rules, and one draw needn't show every extreme that they name: `segment`: within each block of 1024 slots the non-negative values start at 0 and rise by one at each new sequence, and the -1 slots, if any, come last; each run of one value other than -1 is at most 1024 long and at least 2 long unless -1 slots follow it; some run is exactly 1024 long, and some block reaches the largest value.
All inputs are finite; a program needn't handle non-finite values.
Results may differ from the reference program's by a relative error of at most 0.0084.
Values may be sent and summed in bfloat16 or wider, within the bound.
No kernel may reach another device: no remote copies, remote signals or barrier semaphores. Data moves between devices by JAX's collectives and lax.ppermute only.
A program may use at most 320 MiB of HBM per device.

```python
import math
import jax
import jax.numpy as jnp
from jax import lax

D = 1024
HD = 64
FF = 2624
TOK_DEV = 1024
MAXLEN = 1024
TOKENS = 32768
N_FSDP = 32


WEIGHT_CLIP = 0.09375


def draw_segment(key, part):
    used_key, cut_key, pick_key, second_key = jax.random.split(key, 4)
    chosen = jax.random.randint(pick_key, (), 0, N_FSDP)
    second = (chosen + 1 + jax.random.randint(second_key, (), 0, N_FSDP - 1)) % N_FSDP
    device_ids = jnp.arange(N_FSDP, dtype=jnp.int32)
    slot_ids = jnp.arange(TOK_DEV, dtype=jnp.int32)
    used = TOK_DEV - jax.random.randint(used_key, (N_FSDP,), 0, TOK_DEV // 2 + 1)
    used = jnp.where((device_ids == chosen) | (device_ids == second), TOK_DEV, used)
    flags = jax.random.randint(cut_key, (N_FSDP, TOK_DEV), 0, max(2, MAXLEN // 4)) == 0
    forced = device_ids[:, None] == chosen
    flags = jnp.where(forced & (slot_ids[None, :] < MAXLEN), False, flags)
    flags = jnp.where(forced & (slot_ids[None, :] == MAXLEN), True, flags)
    flags = jnp.where(device_ids[:, None] == second, True, flags)

    def advance(run_length, flag_column):
        cut = flag_column & (run_length >= 2) | (run_length >= MAXLEN)
        return (jnp.where(cut, 1, run_length + 1).astype(jnp.int32), cut)
    start_run = jnp.full((N_FSDP,), MAXLEN, jnp.int32)
    _, cuts = lax.scan(advance, start_run, flags.T)
    segment = jnp.cumsum(cuts.T.astype(jnp.int32), axis=1) - 1
    segment = jnp.where(slot_ids[None, :] < used[:, None], segment, -1)
    return segment.reshape(-1).astype(jnp.int32)


def draw_tokens(key, part):
    base_key = jax.random.fold_in(jax.random.fold_in(key, 7), 0)
    base_field = jax.random.normal(base_key, (TOKENS, D), jnp.float32)
    return jnp.clip(base_field, -5.0, 5.0).astype(jnp.bfloat16)


def draw_w_qkv(key, part):
    base_key = jax.random.fold_in(key, 11)
    base_field = jax.random.normal(base_key, (3 * D, D), jnp.float32) * D ** (-0.5)
    base_field = jnp.clip(base_field, -WEIGHT_CLIP, WEIGHT_CLIP)
    return base_field.astype(jnp.bfloat16)


def block_levels(own_key, shape, cuts, least, high):
    loudness, own = 1.0, jax.random.fold_in(own_key, 6)
    for dim, blocks in cuts:
        steps = jnp.exp(jax.random.uniform(jax.random.fold_in(own, dim), (blocks,), jnp.float32, least / len(cuts), high / len(cuts)))
        loudness = loudness * jnp.repeat(steps, shape[dim] // blocks).reshape([-1 if axis == dim else 1 for axis in range(len(shape))])
    return loudness


def gaussian(key, shape, spread, limit, cuts=(), held_as=jnp.bfloat16):
    level = block_levels(key, shape, cuts, -0.22, 0.18) if cuts else 1.0
    values = jax.random.normal(key, shape, jnp.float32) * spread * level
    return jnp.minimum(jnp.maximum(values, -limit), limit).astype(held_as)


def setup_inputs(seed: int = 0) -> dict:
    splits = jax.random.split(jax.random.key(seed), 10)
    tokens = draw_tokens(jax.random.fold_in(splits[9], 71), 0)
    cotangent = gaussian(splits[1], (TOKENS, D), 1.0, 6.0, ((0, 32),))
    segment = draw_segment(jax.random.fold_in(splits[9], 71), 0)
    w_qkv = draw_w_qkv(jax.random.fold_in(splits[9], 71), 0)
    w_attn_out = gaussian(splits[4], (D, D), (D // 16) ** -0.5, 0.75, ((0, 32),))
    w_in = gaussian(splits[5], (2 * FF, D), D ** -0.5, 0.1875, ((0, 32),))
    w_ff_out = gaussian(splits[6], (D, FF), FF ** -0.5, 0.125, ((0, 32),))
    norm_one = jnp.clip(1.0 + 0.15 * jax.random.normal(splits[7], (D,), jnp.float32), 0.25, 1.75).astype(jnp.bfloat16)
    norm_two = jnp.clip(1.0 + 0.15 * jax.random.normal(splits[8], (D,), jnp.float32), 0.25, 1.75).astype(jnp.bfloat16)
    return dict(tokens=tokens, cotangent=cotangent, segment=segment, w_qkv=w_qkv, w_attn_out=w_attn_out, w_in=w_in, w_ff_out=w_ff_out, norm_one=norm_one, norm_two=norm_two)


EPS = 1e-05
THETA = 160000.0

def matmul_nt(left, right):
    return lax.dot_general(left, right, (((1,), (1,)), ((), ())), preferred_element_type=jnp.float32)

def matmul_tn(left, right):
    return lax.dot_general(left, right, (((0,), (0,)), ((), ())), preferred_element_type=jnp.float32)

def heads_first(flat):
    return flat.reshape(flat.shape[0], -1, HD).transpose(1, 0, 2)

def heads_last(split):
    return split.transpose(1, 0, 2).reshape(split.shape[1], -1)

def rotate(field):
    half = field.shape[-1] // 2
    return jnp.concatenate([-field[..., half:], field[..., :half]], axis=-1)

def unrotate(field):
    half = field.shape[-1] // 2
    return jnp.concatenate([field[..., half:], -field[..., :half]], axis=-1)

def rope_tables(segment):
    count = segment.shape[0]
    slots = jnp.arange(count, dtype=jnp.int32)
    begins = jnp.concatenate([jnp.ones((1,), dtype=jnp.bool_), segment[1:] != segment[:-1]])
    starts = lax.cummax(jnp.where(begins, slots, 0).astype(jnp.int32), axis=0)
    positions = (slots - starts).astype(jnp.float32)
    half = HD // 2
    freqs = THETA ** (-2.0 * jnp.arange(half, dtype=jnp.float32) / HD)
    angles = positions[:, None] * freqs[None, :]
    cosine = jnp.concatenate([jnp.cos(angles), jnp.cos(angles)], axis=1)[None]
    sine = jnp.concatenate([jnp.sin(angles), jnp.sin(angles)], axis=1)[None]
    same = (segment[:, None] == segment[None, :]) & (segment[:, None] >= 0)
    allowed = same | (slots[:, None] == slots[None, :])
    return (cosine, sine, allowed)

def layer_norm(field):
    centre = lax.optimization_barrier(jnp.mean(field, axis=-1, keepdims=True))
    centered = field - centre
    variance = lax.optimization_barrier(jnp.mean(centered * centered, axis=-1, keepdims=True))
    inverse = lax.rsqrt(variance + EPS)
    return (centered * inverse, inverse)

def norm_backward(grad_normed, normed, inverse, gain):
    grad_hat = grad_normed * gain.astype(jnp.float32)
    first = lax.optimization_barrier(jnp.mean(grad_hat, axis=-1, keepdims=True))
    second = lax.optimization_barrier(jnp.mean(grad_hat * normed, axis=-1, keepdims=True))
    return (inverse * (grad_hat - first - normed * second), lax.optimization_barrier(jnp.sum(grad_normed * normed, axis=0)))

def gelu_parts(pre):
    cdf = 0.5 * (1.0 + lax.erf(pre * 0.7071067811865476))
    density = jnp.exp(-0.5 * pre * pre) * 0.3989422804014327
    return (pre * cdf, cdf + pre * density)

def attend_forward(query_rot, key_rot, value_all, allowed):
    scale = 1.0 / math.sqrt(HD)

    def per_head(operands):
        query_head, key_head, value_head = operands
        scores = matmul_nt(query_head, key_head) * scale
        scores = jnp.where(allowed, scores, -1e+30)
        top_score = lax.optimization_barrier(jnp.max(scores, axis=1, keepdims=True))
        totals = lax.optimization_barrier(jnp.sum(jnp.exp(scores - top_score), axis=1, keepdims=True))
        log_total = top_score + jnp.log(totals)
        weights = jnp.exp(scores - log_total).astype(jnp.bfloat16)
        result = jnp.dot(weights, value_head, preferred_element_type=jnp.float32)
        return (result.astype(jnp.bfloat16), log_total[:, 0])
    return lax.map(per_head, (query_rot, key_rot, value_all))

def attend_backward(query_rot, key_rot, value_all, head_out, grad_heads, log_totals, allowed):
    scale = 1.0 / math.sqrt(HD)

    def per_head(operands):
        query_head, key_head, value_head, out_head, grad_head, log_head = operands
        scores = matmul_nt(query_head, key_head) * scale
        scores = jnp.where(allowed, scores, -1e+30)
        weights = jnp.where(allowed, jnp.exp(scores - log_head[:, None]), 0.0)
        grad_value = matmul_tn(weights.astype(jnp.bfloat16), grad_head)
        grad_weights = matmul_nt(grad_head, value_head)
        delta = lax.optimization_barrier(jnp.sum(grad_head.astype(jnp.float32) * out_head.astype(jnp.float32), axis=1, keepdims=True))
        grad_scores = (weights * (grad_weights - delta)).astype(jnp.bfloat16)
        grad_query = jnp.dot(grad_scores, key_head, preferred_element_type=jnp.float32) * scale
        grad_key = matmul_tn(grad_scores, query_head) * scale
        return (grad_query, grad_key, grad_value)
    return lax.map(per_head, (query_rot, key_rot, value_all, head_out, grad_heads, log_totals))

def forward_part(tokens, segment, w_qkv, w_attn_out, w_in, w_ff_out, norm_one, norm_two):
    width = tokens.shape[1]
    hidden_units = w_ff_out.shape[1]
    cosine, sine, allowed = rope_tables(segment)
    resid_in = tokens.astype(jnp.float32)
    normed_one, inverse_one = layer_norm(resid_in)
    hidden_one = (normed_one * norm_one.astype(jnp.float32)).astype(jnp.bfloat16)
    projected = matmul_nt(hidden_one, w_qkv)
    query_all = heads_first(projected[:, :width])
    key_all = heads_first(projected[:, width:2 * width])
    value_all = heads_first(projected[:, 2 * width:]).astype(jnp.bfloat16)
    query_rot = (query_all * cosine + rotate(query_all) * sine).astype(jnp.bfloat16)
    key_rot = (key_all * cosine + rotate(key_all) * sine).astype(jnp.bfloat16)
    head_out, log_totals = attend_forward(query_rot, key_rot, value_all, allowed)
    attn_out = heads_last(head_out)
    resid_mid = resid_in + matmul_nt(attn_out, w_attn_out)
    normed_two, inverse_two = layer_norm(resid_mid)
    hidden_two = (normed_two * norm_two.astype(jnp.float32)).astype(jnp.bfloat16)
    inner = matmul_nt(hidden_two, w_in)
    gelu_value, gelu_slope = gelu_parts(inner[:, :hidden_units])
    gate_half = inner[:, hidden_units:]
    mixed = (gelu_value * gate_half).astype(jnp.bfloat16)
    output = (resid_mid + matmul_nt(mixed, w_ff_out)).astype(jnp.bfloat16)
    saved = (cosine, sine, allowed, normed_one, inverse_one, hidden_one, query_rot, key_rot, value_all, head_out, log_totals, attn_out, normed_two, inverse_two, hidden_two, gelu_value, gelu_slope, gate_half, mixed)
    return (output, saved)

def ffn_backward(cotangent, saved, w_in, w_ff_out, norm_two):
    normed_two, inverse_two, hidden_two = (saved[12], saved[13], saved[14])
    gelu_value, gelu_slope, gate_half, mixed = (saved[15], saved[16], saved[17], saved[18])
    grad_ff_out = matmul_tn(cotangent, mixed)
    grad_mixed = jnp.dot(cotangent, w_ff_out, preferred_element_type=jnp.float32)
    grad_inner = jnp.concatenate([grad_mixed * gate_half * gelu_slope, grad_mixed * gelu_value], axis=1).astype(jnp.bfloat16)
    grad_in = matmul_tn(grad_inner, hidden_two)
    grad_hidden_two = jnp.dot(grad_inner, w_in, preferred_element_type=jnp.float32)
    grad_mid_norm, grad_norm_two = norm_backward(grad_hidden_two, normed_two, inverse_two, norm_two)
    grad_mid = cotangent.astype(jnp.float32) + grad_mid_norm
    return (grad_in, grad_ff_out, grad_norm_two, grad_mid)

def attn_backward(grad_mid, saved, w_qkv, w_attn_out, norm_one):
    cosine, sine, allowed, normed_one, inverse_one, hidden_one = saved[:6]
    query_rot, key_rot, value_all, head_out, log_totals, attn_out = saved[6:12]
    grad_mid_low = grad_mid.astype(jnp.bfloat16)
    grad_attn_out = matmul_tn(grad_mid_low, attn_out)
    grad_heads = heads_first(jnp.dot(grad_mid_low, w_attn_out, preferred_element_type=jnp.float32).astype(jnp.bfloat16))
    grad_query, grad_key, grad_value = attend_backward(query_rot, key_rot, value_all, head_out, grad_heads, log_totals, allowed)
    grad_query = grad_query * cosine + unrotate(grad_query * sine)
    grad_key = grad_key * cosine + unrotate(grad_key * sine)
    grad_projected = jnp.concatenate([heads_last(grad_query), heads_last(grad_key), heads_last(grad_value)], axis=1).astype(jnp.bfloat16)
    grad_qkv = matmul_tn(grad_projected, hidden_one)
    grad_hidden_one = jnp.dot(grad_projected, w_qkv, preferred_element_type=jnp.float32)
    grad_in_norm, grad_norm_one = norm_backward(grad_hidden_one, normed_one, inverse_one, norm_one)
    grad_tokens = grad_mid + grad_in_norm
    return (grad_qkv, grad_attn_out, grad_norm_one, grad_tokens)

def reference(tokens, cotangent, segment, w_qkv, w_attn_out, w_in, w_ff_out, norm_one, norm_two):
    blocks = (tokens.reshape(N_FSDP, TOK_DEV, D), cotangent.reshape(N_FSDP, TOK_DEV, D), segment.reshape(N_FSDP, TOK_DEV))
    zeros = (jnp.zeros((3 * D, D), jnp.float32), jnp.zeros((D, D), jnp.float32), jnp.zeros((2 * FF, D), jnp.float32), jnp.zeros((D, FF), jnp.float32), jnp.zeros((D,), jnp.float32), jnp.zeros((D,), jnp.float32))

    def advance(totals, block):
        tok_block, cot_block, seg_block = block
        output, saved = forward_part(tok_block, seg_block, w_qkv, w_attn_out, w_in, w_ff_out, norm_one, norm_two)
        grad_in, grad_ff_out, grad_norm_two, grad_mid = ffn_backward(cot_block, saved, w_in, w_ff_out, norm_two)
        grad_qkv, grad_attn_out, grad_norm_one, grad_tokens = attn_backward(grad_mid, saved, w_qkv, w_attn_out, norm_one)
        terms = (grad_qkv, grad_attn_out, grad_in, grad_ff_out, grad_norm_one, grad_norm_two)
        totals = tuple((left + right for left, right in zip(totals, terms)))
        return (totals, (output, grad_tokens))
    totals, (outputs, grads) = lax.scan(advance, zeros, blocks)
    return (outputs.reshape(TOKENS, D), grads.reshape(TOKENS, D), totals[0], totals[1], totals[2], totals[3], totals[4], totals[5])
```

```python
import functools
import math

import jax
import jax.numpy as jnp
from jax import lax
from jax.experimental import pallas as pl
from jax.experimental.pallas import tpu as pltpu
from jax.sharding import PartitionSpec as P

HD = 64
EPS = 1e-05
THETA = 160000.0
NEG = -1e30
LANES = 128
F32 = jnp.float32
BF16 = jnp.bfloat16
VMEM_BYTES = 60 << 20


def dot_nt(left, right):
    return lax.dot_general(left, right, (((1,), (1,)), ((), ())), preferred_element_type=F32)


def dot_nn(left, right):
    return lax.dot_general(left, right, (((1,), (0,)), ((), ())), preferred_element_type=F32)


def dot_tn(left, right):
    return lax.dot_general(left, right, (((0,), (0,)), ((), ())), preferred_element_type=F32)


def call(kernel, *, name, grid, in_specs, out_specs, out_shape, scratch=(), flops=0, nbytes=0, aliases=None):
    return pl.pallas_call(
        kernel,
        name=name,
        grid=grid,
        in_specs=in_specs,
        out_specs=out_specs,
        out_shape=out_shape,
        scratch_shapes=list(scratch),
        input_output_aliases=aliases or {},
        compiler_params=pltpu.CompilerParams(
            dimension_semantics=("arbitrary",) * len(grid), vmem_limit_bytes=VMEM_BYTES
        ),
        cost_estimate=pl.CostEstimate(flops=flops, transcendentals=0, bytes_accessed=nbytes),
    )


def sds(shape, dtype):
    return jax.ShapeDtypeStruct(shape, dtype)


def whole(shape):
    zeros = (0,) * len(shape)
    return pl.BlockSpec(shape, lambda *_: zeros)


def normalise(field):
    centre = jnp.mean(field, axis=-1, keepdims=True)
    centered = field - centre
    variance = jnp.mean(centered * centered, axis=-1, keepdims=True)
    inverse = lax.rsqrt(variance + EPS)
    return centered * inverse, inverse


def minus_row(field, row):
    return (field.reshape(-1, *row.shape) - row[None]).reshape(field.shape)


def swap_halves(field):
    lane = lax.broadcasted_iota(jnp.int32, field.shape, 1)
    first = (lane & (HD - 1)) < HD // 2
    return jnp.where(
        first, pltpu.roll(field, LANES - HD // 2, 1), pltpu.roll(field, HD // 2, 1)
    )


def fetch(weights, at, rows, target, sem):
    order_ref, pieces = weights
    i = 0
    for piece in pieces:
        for slot in range(piece.shape[0]):
            start = pl.multiple_of(order_ref[i] * rows, rows)
            pltpu.make_async_copy(
                piece.at[slot, pl.ds(at, rows), :], target.at[pl.ds(start, rows), :], sem
            ).start()
            i += 1


def arrive(target, sem):
    pltpu.make_async_copy(target, target, sem).wait()


def fetching_call(
    kernel, weights, *, name, grid, in_specs, out_specs, out_shape, scratch=(), flops=0, nbytes=0
):
    number = len(weights)

    def run(*refs):
        orders, rest, sets = refs[:number], refs[number:], []
        for order, (_, pieces) in zip(orders, weights, strict=True):
            sets.append((order, rest[: len(pieces)]))
            rest = rest[len(pieces) :]
        kernel(*sets, *rest)

    pieces = [piece for _, some in weights for piece in some]
    made = pl.pallas_call(
        run,
        name=name,
        grid_spec=pltpu.PrefetchScalarGridSpec(
            num_scalar_prefetch=number,
            grid=grid,
            in_specs=[pl.BlockSpec(memory_space=pl.ANY)] * len(pieces) + in_specs,
            out_specs=out_specs,
            scratch_shapes=list(scratch),
        ),
        out_shape=out_shape,
        compiler_params=pltpu.CompilerParams(
            dimension_semantics=("arbitrary",) * len(grid), vmem_limit_bytes=VMEM_BYTES
        ),
        cost_estimate=pl.CostEstimate(flops=flops, transcendentals=0, bytes_accessed=nbytes),
    )
    return lambda *args: made(*[order for order, _ in weights], *pieces, *args)


def project_kernel(
    rope_blocks, query_blocks, rows, weights,
    tok_ref, gain_ref, cos_ref, sin_ref, out_ref, hid_ref, w_ref, sem,
):
    step = pl.program_id(0)
    block = out_ref.shape[1]

    @pl.when(step == 0)
    def _():
        fetch(weights, 0, rows, w_ref, sem)
        normed, _ = normalise(tok_ref[...].astype(F32))
        hid_ref[...] = (normed * gain_ref[...]).astype(BF16)
        arrive(w_ref, sem)

    acc = dot_nt(hid_ref[...], w_ref[pl.ds(pl.multiple_of(step * block, block), block), :])

    @pl.when(step < rope_blocks)
    def _():
        scale = jnp.where(step < query_blocks, 1.0 / math.sqrt(HD), 1.0).astype(F32)
        cosine, sine = cos_ref[...], sin_ref[...]
        for s in range(acc.shape[1] // LANES):
            part = acc[:, s * LANES : (s + 1) * LANES]
            turned = part * cosine + swap_halves(part) * sine
            out_ref[:, s * LANES : (s + 1) * LANES] = (turned * scale).astype(BF16)

    @pl.when(step >= rope_blocks)
    def _():
        out_ref[...] = acc.astype(BF16)


def project(tokens, gain, cosine, sine, weights, rows):
    count, width = tokens.shape
    total = 3 * width
    block = 512
    return fetching_call(
        functools.partial(project_kernel, 2 * width // block, width // block, rows),
        [weights],
        name="norm_project",
        grid=(total // block,),
        in_specs=[
            whole((count, width)),
            whole((1, width)),
            whole((count, LANES)),
            whole((count, LANES)),
        ],
        out_specs=[pl.BlockSpec((count, block), lambda j, *_: (0, j)), whole((count, width))],
        out_shape=[sds((count, total), BF16), sds((count, width), BF16)],
        scratch=[pltpu.VMEM((total, width), BF16), pltpu.SemaphoreType.DMA],
        flops=2 * count * width * total,
        nbytes=2 * (2 * count * width + total * width + total * count),
    )(tokens, gain, cosine, sine)


def attend_kernel(chunk, q_ref, k_ref, v_ref, segc_ref, segr_ref, out_ref, lse_ref, vt_ref, ot_ref):
    count = q_ref.shape[0]
    vt_ref[...] = v_ref[...].T
    keys = k_ref[...]
    lane = lax.broadcasted_iota(jnp.int32, (chunk, LANES), 1)

    def body(c, _):
        at = pl.ds(pl.multiple_of(c * chunk, chunk), chunk)
        query = q_ref[at, :]
        column = segc_ref[...]
        allowed = jnp.concatenate([column] * (chunk // LANES), axis=1) == segr_ref[:, at]
        for h in range(2):
            picked = jnp.where((lane >= h * HD) & (lane < (h + 1) * HD), query, jnp.zeros_like(query))
            scores = jnp.where(allowed, dot_nt(keys, picked), NEG)
            top = jnp.max(scores, axis=0, keepdims=True)
            powers = jnp.exp(scores - top)
            total = jnp.sum(powers, axis=0, keepdims=True)
            lse_ref[0, pl.ds(h, 1), at] = top + jnp.log(total)
            mixed = dot_nn(vt_ref[h * HD : (h + 1) * HD, :], powers.astype(BF16))
            ot_ref[h * HD : (h + 1) * HD, at] = mixed / total
        return 0

    lax.fori_loop(0, count // chunk, body, 0)
    out_ref[...] = ot_ref[...].T.astype(BF16)


def attend(qkv, seg_column, seg_row, width, first, number, before=None):
    count = qkv.shape[0]
    pairs = width // LANES
    chunk = 256
    kept = () if before is None else tuple(before)

    def kernel(*refs):
        attend_kernel(chunk, *refs[:5], *refs[5 + len(kept) :])

    tall = lambda offset: pl.BlockSpec((count, LANES), lambda p: (0, offset + first + p))
    return call(
        kernel,
        name="attend",
        grid=(number,),
        in_specs=[tall(0), tall(pairs), tall(2 * pairs), whole((count, LANES)), whole((1, count))]
        + [pl.BlockSpec(memory_space=pl.ANY)] * len(kept),
        out_specs=[tall(0), pl.BlockSpec((1, 2, count), lambda p: (first + p, 0, 0))],
        out_shape=[sds((count, width), BF16), sds((pairs, 2, count), F32)],
        scratch=[pltpu.VMEM((LANES, count), BF16), pltpu.VMEM((LANES, count), F32)],
        flops=16 * count * count * LANES * number,
        nbytes=2 * 4 * count * LANES * number,
        aliases={5: 0, 6: 1} if kept else None,
    )(qkv, qkv, qkv, seg_column, seg_row, *kept)


def attend_back_kernel(
    chunk, q_ref, k_ref, v_ref, o_ref, g_ref, lse_ref, segc_ref, segr_ref, cos_ref, sin_ref,
    out_ref, kt_ref, dk_ref, dv_ref, dqt_ref, delta_ref, total_ref,
):
    count = q_ref.shape[0]
    kt_ref[...] = k_ref[...].T
    keys, values = k_ref[...], v_ref[...]
    product = (g_ref[...].astype(F32) * o_ref[...].astype(F32)).T
    for h in range(2):
        row = jnp.sum(product[h * HD : (h + 1) * HD, :], axis=0, keepdims=True)
        delta_ref[h] = jnp.broadcast_to(row, (8, count))
        total_ref[h] = jnp.broadcast_to(lse_ref[0, h : h + 1, :], (8, count))
    dk_ref[...] = jnp.zeros_like(dk_ref)
    dv_ref[...] = jnp.zeros_like(dv_ref)
    lane = lax.broadcasted_iota(jnp.int32, (chunk, LANES), 1)

    def body(c, _):
        at = pl.ds(pl.multiple_of(c * chunk, chunk), chunk)
        query, grad = q_ref[at, :], g_ref[at, :]
        column = segc_ref[...]
        allowed = jnp.concatenate([column] * (chunk // LANES), axis=1) == segr_ref[:, at]
        turned = []
        for h in range(2):
            mine = (lane >= h * HD) & (lane < (h + 1) * HD)
            query_h = jnp.where(mine, query, jnp.zeros_like(query))
            grad_h = jnp.where(mine, grad, jnp.zeros_like(grad))
            scores = jnp.where(allowed, dot_nt(keys, query_h), NEG)
            weights = jnp.exp(minus_row(scores, total_ref[h, :, at]))
            dv_ref[...] += dot_nn(weights.astype(BF16), grad_h)
            spread = minus_row(dot_nt(values, grad_h), delta_ref[h, :, at])
            grad_scores = (weights * spread).astype(BF16)
            dk_ref[...] += dot_nn(grad_scores, query_h)
            turned.append(dot_nn(kt_ref[...], grad_scores))
        row = lax.broadcasted_iota(jnp.int32, (LANES, chunk), 0)
        dqt_ref[:, at] = jnp.where(row < HD, turned[0], turned[1])
        return 0

    lax.fori_loop(0, count // chunk, body, 0)
    cosine, sine = cos_ref[...], sin_ref[...]
    grad_query = dqt_ref[...].T * (1.0 / math.sqrt(HD))
    out_ref[0] = (grad_query * cosine - swap_halves(grad_query) * sine).astype(BF16)
    grad_key = dk_ref[...]
    out_ref[1] = (grad_key * cosine - swap_halves(grad_key) * sine).astype(BF16)
    out_ref[2] = dv_ref[...].astype(BF16)


def attend_back(qkv, attn_out, grad_heads, lse, seg_column, seg_row, cosine, sine, first, number, before=None):
    count, width = attn_out.shape
    pairs = width // LANES
    chunk = 256
    kept = () if before is None else (before,)

    def kernel(*refs):
        attend_back_kernel(chunk, *refs[:10], *refs[10 + len(kept) :])

    tall = lambda offset: pl.BlockSpec((count, LANES), lambda p: (0, offset + first + p))
    return call(
        kernel,
        name="attend_back",
        grid=(number,),
        in_specs=[
            tall(0),
            tall(pairs),
            tall(2 * pairs),
            tall(0),
            tall(0),
            pl.BlockSpec((1, 2, count), lambda p: (first + p, 0, 0)),
            whole((count, LANES)),
            whole((1, count)),
            whole((count, LANES)),
            whole((count, LANES)),
        ]
        + [pl.BlockSpec(memory_space=pl.ANY)] * len(kept),
        out_specs=pl.BlockSpec((3, count, LANES), lambda p: (0, 0, first + p)),
        out_shape=sds((3, count, width), BF16),
        scratch=[
            pltpu.VMEM((LANES, count), BF16),
            pltpu.VMEM((count, LANES), F32),
            pltpu.VMEM((count, LANES), F32),
            pltpu.VMEM((LANES, count), F32),
            pltpu.VMEM((2, 8, count), F32),
            pltpu.VMEM((2, 8, count), F32),
        ],
        flops=40 * count * count * LANES * number,
        nbytes=2 * 8 * count * LANES * number,
        aliases={10: 0} if kept else None,
    )(qkv, qkv, qkv, attn_out, grad_heads, lse, seg_column, seg_row, cosine, sine, *kept)


def join_kernel(rows, weights, tok_ref, attn_ref, gain_ref, resid_ref, hid_ref, w_ref, sem):
    @pl.when(pl.program_id(0) == 0)
    def _():
        fetch(weights, 0, rows, w_ref, sem)
        arrive(w_ref, sem)

    resid = tok_ref[...].astype(F32) + dot_nt(attn_ref[...], w_ref[...])
    resid_ref[...] = resid
    normed, _ = normalise(resid)
    hid_ref[...] = (normed * gain_ref[...]).astype(BF16)


def join(tokens, attn_out, gain, weights, rows_out):
    count, width = tokens.shape
    block = 256
    rows = pl.BlockSpec((block, width), lambda i, *_: (i, 0))
    return fetching_call(
        functools.partial(join_kernel, rows_out),
        [weights],
        name="attn_out_norm",
        grid=(count // block,),
        in_specs=[rows, rows, whole((1, width))],
        out_specs=[rows, rows],
        out_shape=[sds((count, width), F32), sds((count, width), BF16)],
        scratch=[pltpu.VMEM((width, width), BF16), pltpu.SemaphoreType.DMA],
        flops=2 * count * width * width,
        nbytes=2 * 6 * count * width,
    )(tokens, attn_out, gain)


def ffn_kernel(
    rows_in, at, rows_ff, weights_in, weights_rest,
    resid_ref, hid_ref, cot_ref, gain_ref,
    out_ref, mid_ref, low_ref, gnorm_ref, g_in_ref, g_out_ref,
    cot_t_ref, out_acc, hid_acc, w_in_ref, w_ff_ref, sem_in, sem_ff,
):
    step = pl.program_id(0)
    block = g_out_ref.shape[1]
    units = w_in_ref.shape[0] // 2
    width = hid_ref.shape[1]

    @pl.when(step == 0)
    def _():
        fetch(weights_in, 0, rows_in, w_in_ref, sem_in)
        for b in range(w_ff_ref.shape[0]):
            fetch(weights_rest, at + b * rows_ff, rows_ff, w_ff_ref.at[b], sem_ff)
        cot_t_ref[...] = cot_ref[...].T
        out_acc[...] = jnp.zeros_like(out_acc)
        hid_acc[...] = jnp.zeros_like(hid_acc)
        arrive(w_in_ref, sem_in)
        arrive(w_ff_ref, sem_ff)

    hidden = hid_ref[...]
    w_pre = w_in_ref[pl.ds(pl.multiple_of(step * block, block), block), :]
    w_gate = w_in_ref[pl.ds(pl.multiple_of(units + step * block, block), block), :]
    per = width // block
    w_out = w_ff_ref[step // per, :, pl.ds(pl.multiple_of(step % per * block, block), block)]
    pre = dot_nt(hidden, w_pre)
    gate = dot_nt(hidden, w_gate)
    grad_mixed = dot_nn(cot_ref[...], w_out)
    cdf = 0.5 * (1.0 + lax.erf(pre * 0.7071067811865476))
    density = jnp.exp(-0.5 * pre * pre) * 0.3989422804014327
    gelu = pre * cdf
    mixed = (gelu * gate).astype(BF16)
    out_acc[...] += dot_nt(mixed, w_out)
    g_out_ref[...] = dot_nn(cot_t_ref[...], mixed).astype(BF16)
    grad_pre = (grad_mixed * gate * (cdf + pre * density)).astype(BF16)
    grad_gate = (grad_mixed * gelu).astype(BF16)
    g_in_ref[0] = dot_tn(grad_pre, hidden).astype(BF16)
    g_in_ref[1] = dot_tn(grad_gate, hidden).astype(BF16)
    hid_acc[...] += dot_nn(grad_pre, w_pre) + dot_nn(grad_gate, w_gate)

    @pl.when(step == pl.num_programs(0) - 1)
    def _():
        rows = 256
        gnorm = jnp.zeros_like(gnorm_ref)
        for i in range(resid_ref.shape[0] // rows):
            at = slice(i * rows, (i + 1) * rows)
            resid = resid_ref[at, :]
            out_ref[at, :] = (resid + out_acc[at, :]).astype(BF16)
            normed, inverse = normalise(resid)
            grad = hid_acc[at, :]
            gnorm += jnp.sum(grad * normed, axis=0, keepdims=True)
            hat = grad * gain_ref[...]
            first = jnp.mean(hat, axis=-1, keepdims=True)
            second = jnp.mean(hat * normed, axis=-1, keepdims=True)
            mid = cot_ref[at, :].astype(F32) + inverse * (hat - first - normed * second)
            mid_ref[at, :] = mid
            low_ref[at, :] = mid.astype(BF16)
        gnorm_ref[...] = gnorm


def ffn(resid, hidden, cotangent, gain, w_in, w_rest, units, rows_in, at, rows_ff):
    count, width = resid.shape
    block = 256
    spans = -(-units // width)
    once = pl.BlockSpec((count, width), lambda *_: (0, 0), pipeline_mode=pl.Buffered(1))
    return fetching_call(
        functools.partial(ffn_kernel, rows_in, at, rows_ff),
        [w_in, w_rest],
        name="ffn_forward_backward",
        grid=(units // block,),
        in_specs=[once, once, once, whole((1, width))],
        out_specs=[
            once,
            once,
            once,
            whole((1, width)),
            pl.BlockSpec((2, block, width), lambda j, *_: (0, j, 0)),
            pl.BlockSpec((width, block), lambda j, *_: (0, j)),
        ],
        out_shape=[
            sds((count, width), BF16),
            sds((count, width), F32),
            sds((count, width), BF16),
            sds((1, width), F32),
            sds((2, units, width), BF16),
            sds((width, units), BF16),
        ],
        scratch=[
            pltpu.VMEM((width, count), BF16),
            pltpu.VMEM((count, width), F32),
            pltpu.VMEM((count, width), F32),
            pltpu.VMEM((2 * units, width), BF16),
            pltpu.VMEM((spans, width, width), BF16),
            pltpu.SemaphoreType.DMA,
            pltpu.SemaphoreType.DMA,
        ],
        flops=18 * count * width * units,
        nbytes=2 * (10 * count * width + 6 * units * width),
    )(resid, hidden, cotangent, gain)


def join_back_kernel(rows, weights, low_ref, attn_ref, heads_ref, gw_ref, w_ref, sem):
    step = pl.program_id(0)
    block = heads_ref.shape[1]

    @pl.when(step == 0)
    def _():
        fetch(weights, 0, rows, w_ref, sem)
        arrive(w_ref, sem)

    span = pl.ds(pl.multiple_of(step * block, block), block)
    heads_ref[...] = dot_nn(low_ref[...], w_ref[:, span]).astype(BF16)
    gw_ref[...] = dot_tn(low_ref[:, span], attn_ref[...]).astype(BF16)


def join_back(low, attn_out, weights, rows):
    count, width = low.shape
    block = 256
    return fetching_call(
        functools.partial(join_back_kernel, rows),
        [weights],
        name="attn_out_back",
        grid=(width // block,),
        in_specs=[whole((count, width)), whole((count, width))],
        out_specs=[pl.BlockSpec((count, block), lambda j, *_: (0, j)), pl.BlockSpec((block, width), lambda j, *_: (j, 0))],
        out_shape=[sds((count, width), BF16), sds((width, width), BF16)],
        scratch=[pltpu.VMEM((width, width), BF16), pltpu.SemaphoreType.DMA],
        flops=4 * count * width * width,
        nbytes=2 * 5 * count * width,
    )(low, attn_out)


def project_grad_kernel(gp_ref, hid_ref, out_ref):
    out_ref[...] = dot_tn(gp_ref[0], hid_ref[...]).astype(BF16)


def project_grad(grad_projected, hidden):
    count, width = hidden.shape
    block = 512
    per = width // block
    return call(
        project_grad_kernel,
        name="grad_qkv",
        grid=(3 * per,),
        in_specs=[pl.BlockSpec((1, count, block), lambda j: (j // per, 0, j % per)), whole((count, width))],
        out_specs=pl.BlockSpec((block, width), lambda j: (j, 0)),
        out_shape=sds((3 * width, width), BF16),
        flops=6 * count * width * width,
        nbytes=2 * 7 * count * width,
    )(grad_projected, hidden)


def project_back_kernel(
    rows_qkv, weights, gp_ref, tok_ref, mid_ref, gain_ref, out_ref, gnorm_ref, acc_ref, w_ref, sem
):
    step = pl.program_id(0)
    width = gp_ref.shape[2]

    @pl.when(step == 0)
    def _():
        fetch(weights, 0, rows_qkv, w_ref, sem)
        arrive(w_ref, sem)

    term = dot_nn(gp_ref[0], w_ref[pl.ds(pl.multiple_of(step * width, width), width), :])

    @pl.when(step == 0)
    def _():
        acc_ref[...] = term

    @pl.when(step > 0)
    def _():
        acc_ref[...] += term

    @pl.when(step == pl.num_programs(0) - 1)
    def _():
        rows = 256
        gnorm = jnp.zeros_like(gnorm_ref)
        for i in range(tok_ref.shape[0] // rows):
            at = slice(i * rows, (i + 1) * rows)
            normed, inverse = normalise(tok_ref[at, :].astype(F32))
            grad = acc_ref[at, :]
            gnorm += jnp.sum(grad * normed, axis=0, keepdims=True)
            hat = grad * gain_ref[...]
            first = jnp.mean(hat, axis=-1, keepdims=True)
            second = jnp.mean(hat * normed, axis=-1, keepdims=True)
            out_ref[at, :] = mid_ref[at, :] + inverse * (hat - first - normed * second)
        gnorm_ref[...] = gnorm


def project_back(grad_projected, weights, rows_qkv, tokens, mid, gain):
    count, width = tokens.shape
    full = whole((count, width))
    return fetching_call(
        functools.partial(project_back_kernel, rows_qkv),
        [weights],
        name="grad_tokens",
        grid=(3,),
        in_specs=[
            pl.BlockSpec((1, count, width), lambda j, *_: (j, 0, 0)),
            full,
            full,
            whole((1, width)),
        ],
        out_specs=[full, whole((1, width))],
        out_shape=[sds((count, width), F32), sds((1, width), F32)],
        scratch=[
            pltpu.VMEM((count, width), F32),
            pltpu.VMEM((3 * width, width), BF16),
            pltpu.SemaphoreType.DMA,
        ],
        flops=6 * count * width * width,
        nbytes=2 * 12 * count * width,
    )(grad_projected, tokens, mid, gain)


Z, Y, X = 4, 2, 2
UP, DOWN, IN_Y, IN_X = (1, 0, 0), (-1, 0, 0), (0, 1, 0), (0, 0, 1)
CROSSED, LEVEL = ("planes", "lines"), ("planes", "planes")
SPREAD = {
    CROSSED: (((UP, IN_X), (DOWN, IN_Y), (UP, IN_Y)), ((IN_Y, UP), (IN_X, DOWN), (IN_X, UP))),
    LEVEL: (((UP, UP), (DOWN, DOWN), (UP, UP)), ((IN_Y, IN_X), (IN_X, IN_Y), (IN_X, IN_Y))),
}
REDUCE = {
    CROSSED: (((IN_X, DOWN), (IN_X, UP), (IN_Y, DOWN)), ((DOWN, IN_Y), (UP, IN_Y), (DOWN, IN_X))),
    LEVEL: (((IN_X, IN_Y), (IN_X, IN_Y), (IN_Y, IN_X)), ((DOWN, DOWN), (UP, UP), (DOWN, DOWN))),
}


def ident(z, y, x, c):
    return (((z % Z) * Y + y % Y) * X + x % X) * 2 + c


def plus(*moves):
    return tuple(sum(m[i] for m in moves) for i in range(3))


def minus(move):
    return tuple(-m for m in move)


def hop(array, axis, moves):
    pairs = [
        (ident(z, y, x, c), ident(z + m[0], y + m[1], x + m[2], c))
        for z in range(Z) for y in range(Y) for x in range(X)
        for c, m in enumerate(moves)
    ]
    return lax.ppermute(array, axis, pairs)


def swap_cores(array, axis):
    return lax.ppermute(array, axis, [(i, i ^ 1) for i in range(2 * Z * Y * X)])


def place(axis):
    me = lax.axis_index(axis)
    return (me // (2 * Y * X), me // (2 * X) % Y, me // 2 % X), me % 2


def by_core(c, zero, one):
    return jnp.where(c == 0, jnp.stack(zero), jnp.stack(one)).astype(jnp.int32)


def tie(*values):
    return lax.optimization_barrier(values)


class Spread:
    def __init__(self, shard, axis, route):
        self.shard, self.axis, self.route = shard, axis, route

    def near(self):
        short, _ = SPREAD[self.route]
        self.first = hop(self.shard, self.axis, short[0])
        self.third = hop(self.shard, self.axis, short[1])

    def nearer(self):
        short, _ = SPREAD[self.route]
        second = hop(self.first, self.axis, short[2])
        self.block = jnp.stack([self.shard, self.first, second, self.third])

    def far(self):
        _, far = SPREAD[self.route]
        self.one = hop(self.block, self.axis, far[0])
        self.three = hop(self.block, self.axis, far[1])

    def farther(self):
        _, far = SPREAD[self.route]
        self.two = hop(self.one, self.axis, far[2])

    def result(self):
        short, far = SPREAD[self.route]
        mine = (self.block, self.one, self.two, self.three)
        pieces = mine + tuple(swap_cores(b, self.axis) for b in mine)
        at, c = place(self.axis)
        froms = []
        for core in range(2):
            s, f = [m[core] for m in short], [m[core] for m in far]
            close = [(0, 0, 0), s[0], plus(s[0], s[2]), s[1]]
            long = [(0, 0, 0), f[0], plus(f[0], f[2]), f[1]]
            froms.append([ident(*plus(at, minus(a), minus(b)), core) for a in long for b in close])
        order = jnp.concatenate([by_core(c, *froms), by_core(c, *froms[::-1])])
        return order, pieces


def lay_out(grad, wide):
    spans = [(b, min(b + wide, grad.shape[2])) for b in range(0, grad.shape[2], wide)]
    return spans, grad.shape[1] * len(spans)


def collect(grads, twins, extras, chosen, lines, wide, dtype):
    four = chosen.shape[1]
    total = sum(lay_out(g, wide)[1] for g in grads)
    k, number = len(grads) * four, len(lines)

    def kernel(chosen_ref, *refs):
        mine, theirs, more, outs = refs[:k], refs[k : 2 * k], refs[2 * k : -number], refs[-number:]

        def fill(out):
            for i in range(four):
                at = 0
                for g, t in zip(mine[i::four], theirs[i::four], strict=True):
                    rows = g.shape[1]
                    for a, b in lay_out(g, wide)[0]:
                        value = g[0, :, a:b].astype(F32) + t[0, :, a:b].astype(F32)
                        for m in more:
                            value = value + m[i, at : at + rows, : b - a].astype(F32)
                        out[i, at : at + rows, : b - a] = value.astype(dtype)
                        if b - a < wide:
                            out[i, at : at + rows, b - a :] = jnp.zeros((rows, wide - (b - a)), dtype)
                        at += rows

        for j, out in enumerate(outs):
            pl.when(pl.program_id(0) == j)(functools.partial(fill, out))

    def by_device(g, i):
        def index(j, chosen_ref):
            device = chosen_ref[lines[0], i]
            for step, which in enumerate(lines[1:], 1):
                device = jnp.where(j == step, chosen_ref[which, i], device)
            return device, 0, 0

        return pl.BlockSpec((1, *g.shape[1:]), index)

    devices = [by_device(g, i) for g in grads for i in range(four)]
    every = [g for g in grads for _ in range(four)]
    pairs = [t for t in twins for _ in range(four)]
    block = whole((four, total, wide))
    return pl.pallas_call(
        kernel,
        name="collect_grads",
        grid_spec=pltpu.PrefetchScalarGridSpec(
            num_scalar_prefetch=1,
            grid=(number,),
            in_specs=devices * 2 + [block] * len(extras),
            out_specs=[block] * number,
        ),
        out_shape=[sds((four, total, wide), dtype)] * number,
        compiler_params=pltpu.CompilerParams(
            dimension_semantics=("arbitrary",), vmem_limit_bytes=VMEM_BYTES
        ),
        cost_estimate=pl.CostEstimate(
            flops=number * four * total * wide * (1 + len(extras)),
            transcendentals=0,
            bytes_accessed=2 * number * four * total * wide * (3 + len(extras)),
        ),
    )(chosen, *every, *pairs, *extras)


class Reduce:
    def __init__(self, axis, route, wide):
        self.axis, self.route, self.wide = axis, route, wide
        far, short = REDUCE[route]
        at, c = place(axis)
        both = lambda a, b: tuple(plus(i, j) for i, j in zip(a, b, strict=True))
        here = ((0, 0, 0), (0, 0, 0))

        def line(step):
            lists = []
            for core, kind in enumerate(route):
                z, y, x = plus(at, step[core])
                if kind == "planes":
                    lists.append([ident(k, y, x, core) for k in range(Z)])
                else:
                    lists.append([ident(z, j, k, core) for j in range(Y) for k in range(X)])
            return by_core(c, *lists)

        def slot(step):
            places = []
            for core, kind in enumerate(route):
                z, y, x = plus(at, step[core])
                places.append(z % Z if kind == "planes" else y % Y * X + x % X)
            return jnp.where(c == 0, places[0], places[1])

        self.chosen = jnp.stack([line(s) for s in (both(far[0], far[2]), far[1], far[2], here)])
        self.slots = [slot(s) for s in (both(short[0], short[2]), short[1], short[2], here)]

    def pair(self, grads):
        self.grads = grads
        self.twins = tuple(swap_cores(g, self.axis) for g in grads)

    def pack(self):
        self.one, self.two = collect(self.grads, self.twins, (), self.chosen, (0, 1), self.wide, BF16)

    def far(self):
        far, _ = REDUCE[self.route]
        self.one, self.two = hop(self.one, self.axis, far[0]), hop(self.two, self.axis, far[1])

    def repack(self):
        (self.three,) = collect(self.grads, self.twins, (self.one,), self.chosen, (2,), self.wide, BF16)

    def farther(self):
        far, _ = REDUCE[self.route]
        self.three = hop(self.three, self.axis, far[2])

    def pick(self, which):
        return lax.dynamic_index_in_dim(self.block, self.slots[which], 0, keepdims=False)

    def gather(self):
        (self.block,) = collect(self.grads, self.twins, (self.two, self.three), self.chosen, (3,), self.wide, F32)

    def near(self):
        _, short = REDUCE[self.route]
        self.one = hop(self.pick(0).astype(BF16), self.axis, short[0])
        self.two = hop(self.pick(1).astype(BF16), self.axis, short[1])

    def nearer(self):
        _, short = REDUCE[self.route]
        self.three = hop((self.pick(2) + self.one.astype(F32)).astype(BF16), self.axis, short[2])

    def result(self):
        return self.pick(3) + self.two.astype(F32) + self.three.astype(F32)


def gains_kernel(at, number, weights, out_ref, rows_ref, sem):
    fetch(weights, at, 8, rows_ref, sem)
    arrive(rows_ref, sem)
    total, width = rows_ref.shape
    devices = total // 8
    owner = lax.broadcasted_iota(jnp.int32, (devices, total), 0)
    row = lax.broadcasted_iota(jnp.int32, (devices, total), 1)
    found = dot_nn((row == owner * 8).astype(BF16), rows_ref[:, :LANES]).astype(BF16)
    place_in = lax.broadcasted_iota(jnp.int32, (LANES, width), 0)
    lane = lax.broadcasted_iota(jnp.int32, (LANES, width), 1)
    mine = lax.broadcasted_iota(jnp.int32, (devices, width), 1) // number
    mine = mine == lax.broadcasted_iota(jnp.int32, (devices, width), 0)
    for which in range(2):
        tiled = dot_nn(found, (place_in == lane % number + which * number).astype(BF16))
        out_ref[which : which + 1, :] = jnp.sum(jnp.where(mine, tiled, 0.0), axis=0, keepdims=True)


def find_gains(weights, at, width):
    devices = weights[0].shape[0]
    return fetching_call(
        functools.partial(gains_kernel, at, width // devices),
        [weights],
        name="norm_scales",
        grid=(1,),
        in_specs=[],
        out_specs=[whole((2, width))],
        out_shape=[sds((2, width), F32)],
        scratch=[pltpu.VMEM((devices * 8, width), BF16), pltpu.SemaphoreType.DMA],
        nbytes=2 * devices * 8 * width,
    )()[0]


def tables(segment):
    count = segment.shape[0]
    slots = jnp.arange(count, dtype=jnp.int32)
    order = jnp.where(segment < 0, count, segment)
    starts = jnp.sum((order[None, :] < order[:, None]).astype(jnp.int32), axis=1)
    positions = (slots - starts).astype(F32)
    half = HD // 2
    freqs = THETA ** (-2.0 * jnp.arange(half, dtype=F32) / HD)
    angles = positions[:, None] * freqs[None, :]
    cosine, sine = jnp.cos(angles), jnp.sin(angles)
    cosine = jnp.concatenate([cosine] * 4, axis=1)
    sine = jnp.concatenate([-sine, sine] * 2, axis=1)
    group = jnp.where(segment < 0, -1 - slots, segment)
    return cosine, sine, jnp.broadcast_to(group[:, None], (count, LANES)), group[None, :]


def spans_of(matrix, wide):
    rows, columns = matrix.shape
    count = -(-columns // wide)
    matrix = jnp.pad(matrix, ((0, 0), (0, count * wide - columns)))
    return matrix.reshape(rows, count, wide).transpose(1, 0, 2).reshape(count * rows, wide)


def finish(g_in, g_ff, rows_in, padded, n, axis, g_one, g_two):
    g_in = g_in[:rows_in]
    g_ff = g_ff.reshape(-1, n // 2, padded)[:, :, :rows_in].reshape(-1, n // 2 * rows_in)
    g_norms = jnp.stack([g_one.reshape(n, -1), g_two.reshape(n, -1)], axis=1)
    g_norms = jnp.sum(lax.all_to_all(g_norms, axis, 0, 0, tiled=True), axis=0)
    return g_in, g_ff, g_norms


def by_collectives(tokens, cotangent, segment, w_qkv, w_attn_out, w_in, w_ff_out, gains, padded, axis):
    n = lax.axis_size(axis)
    width = tokens.shape[1]
    units = n // 2 * padded
    pairs = width // LANES
    gather = lambda shard: lax.all_gather(shard, axis, axis=0, tiled=True)
    at_once = lambda matrix: (jnp.zeros((1,), jnp.int32), (matrix[None],))
    w_qkv, w_in = at_once(gather(w_qkv)), at_once(gather(w_in))
    w_rest = at_once(jnp.concatenate([gather(w_attn_out), spans_of(gather(w_ff_out), width)]))
    gains = gather(gains[None]).astype(F32)
    gain_one, gain_two = (g.reshape(1, width) for g in jnp.split(gains, 2, axis=1))
    cosine, sine, seg_column, seg_row = tables(segment)
    qkv, hidden_one = project(tokens, gain_one, cosine, sine, w_qkv, 3 * width)
    attn_out, lse = attend(qkv, seg_column, seg_row, width, 0, pairs)
    resid, hidden_two = join(tokens, attn_out, gain_two, w_rest, width)
    output, mid, low, g_two, g_in, g_ff = ffn(
        resid, hidden_two, cotangent, gain_two, w_in, w_rest, units, 2 * units, width, width
    )
    grad_heads, g_out = join_back(low, attn_out, w_rest, width)
    grad_projected = attend_back(qkv, attn_out, grad_heads, lse, seg_column, seg_row, cosine, sine, 0, pairs)
    g_qkv = project_grad(grad_projected, hidden_one)
    grad_tokens, g_one = project_back(grad_projected, w_qkv, 3 * width, tokens, mid, gain_one)
    scatter = lambda grad: lax.psum_scatter(grad, axis, scatter_dimension=0, tiled=True).astype(F32)
    g_in = g_in.reshape(2 * units, width)
    return output, grad_tokens, scatter(g_qkv), scatter(g_out), scatter(g_in), scatter(g_ff), g_one, g_two


def by_links(tokens, cotangent, segment, w_qkv, w_attn_out, w_in, w_ff_out, gains, padded, axis):
    n = lax.axis_size(axis)
    width = tokens.shape[1]
    units = n // 2 * padded
    pairs = width // LANES
    rows_qkv, rows_out, rows_ff = w_qkv.shape[0], w_attn_out.shape[0], w_ff_out.shape[0]
    gain_rows = jnp.pad(gains[None], ((0, 7), (0, width - gains.shape[0])))
    s_qkv = Spread(jnp.concatenate([w_qkv, gain_rows]), axis, LEVEL)
    s_rest = Spread(jnp.concatenate([w_attn_out, spans_of(w_ff_out, width)]), axis, CROSSED)
    s_in = Spread(w_in, axis, LEVEL)
    r_ff, r_in, r_qkv = Reduce(axis, CROSSED, width), Reduce(axis, LEVEL, width), Reduce(axis, CROSSED, width)
    cosine, sine, seg_column, seg_row = tables(segment)

    s_qkv.near()
    s_qkv.nearer()
    s_qkv.block, s_rest.shard, s_in.shard, cosine, sine, seg_column, seg_row = tie(
        s_qkv.block, s_rest.shard, s_in.shard, cosine, sine, seg_column, seg_row
    )
    s_qkv.far()
    s_rest.near()
    s_in.near()
    s_rest.nearer()
    s_in.nearer()
    s_qkv.farther()
    w_qkv = s_qkv.result()
    gains = find_gains(w_qkv, rows_qkv, width)
    gain_one, gain_two = gains[:1], gains[1:]
    gain_one, s_rest.block, s_in.block = tie(gain_one, s_rest.block, s_in.block)
    s_rest.far()
    s_in.far()
    qkv, hidden_one = project(tokens, gain_one, cosine, sine, w_qkv, rows_qkv)
    done = attend(qkv, seg_column, seg_row, width, 0, pairs // 4)
    done = attend(qkv, seg_column, seg_row, width, pairs // 4, pairs // 4, done)
    done, s_rest.one, s_rest.three, s_in.one, s_in.three = tie(done, s_rest.one, s_rest.three, s_in.one, s_in.three)
    s_rest.farther()
    s_in.farther()
    done = attend(qkv, seg_column, seg_row, width, pairs // 2, pairs // 4, done)
    done = attend(qkv, seg_column, seg_row, width, 3 * pairs // 4, pairs // 4, done)
    done, s_rest.two, s_in.two = tie(done, s_rest.two, s_in.two)
    attn_out, lse = done
    w_rest, w_in = s_rest.result(), s_in.result()
    resid, hidden_two = join(tokens, attn_out, gain_two, w_rest, rows_out)
    output, mid, low, g_two, g_in, g_ff = ffn(
        resid, hidden_two, cotangent, gain_two, w_in, w_rest, units, padded, rows_out, rows_ff
    )

    rows_of = lambda grad: grad.reshape(n, -1, grad.shape[-1])
    calls = pairs
    back = lambda k, heads, before=None: attend_back(
        qkv, attn_out, heads, lse, seg_column, seg_row, cosine, sine, k * pairs // calls, pairs // calls, before
    )
    r_ff.pair((rows_of(g_ff),))
    grad_heads, g_out = join_back(low, attn_out, w_rest, rows_out)
    r_in.pair((rows_of(g_in), rows_of(g_out)))
    grad_heads, r_ff.twins = tie(grad_heads, r_ff.twins)
    r_ff.pack()
    grad_heads, r_ff.one, r_ff.two = tie(grad_heads, r_ff.one, r_ff.two)
    r_ff.far()
    some = back(1, grad_heads, back(0, grad_heads))
    some, r_in.twins, r_ff.one, r_ff.two = tie(some, r_in.twins, r_ff.one, r_ff.two)
    r_in.pack()
    r_ff.repack()
    some, r_in.one, r_in.two, r_ff.three = tie(some, r_in.one, r_in.two, r_ff.three)
    r_in.far()
    r_ff.farther()
    for k in (2, 3, 4, 5):
        some = back(k, grad_heads, some)
    some, r_in.one, r_in.two, r_ff.three = tie(some, r_in.one, r_in.two, r_ff.three)
    r_in.repack()
    r_ff.gather()
    some, r_in.three, r_ff.block = tie(some, r_in.three, r_ff.block)
    r_in.farther()
    r_ff.near()
    grad_projected = back(7, grad_heads, back(6, grad_heads, some))
    grad_projected, r_in.three, r_ff.one, r_ff.two = tie(grad_projected, r_in.three, r_ff.one, r_ff.two)
    r_in.gather()
    grad_projected, r_in.block = tie(grad_projected, r_in.block)
    r_in.near()
    r_ff.nearer()
    g_qkv = project_grad(grad_projected, hidden_one)
    r_qkv.pair((rows_of(g_qkv),))
    r_qkv.twins, r_in.one, r_in.two, r_ff.three = tie(r_qkv.twins, r_in.one, r_in.two, r_ff.three)
    r_qkv.pack()
    r_in.nearer()
    mid, r_qkv.one, r_qkv.two = tie(mid, r_qkv.one, r_qkv.two)
    r_qkv.far()
    grad_tokens, g_one = project_back(grad_projected, w_qkv, rows_qkv, tokens, mid, gain_one)
    grad_tokens, r_qkv.one, r_qkv.two, r_in.three = tie(grad_tokens, r_qkv.one, r_qkv.two, r_in.three)
    r_qkv.repack()
    r_qkv.farther()
    r_qkv.gather()
    r_qkv.near()
    r_qkv.nearer()
    rest = r_in.result()
    g_ff = r_ff.result()
    g_ff = g_ff.reshape(-1, rows_ff, width).transpose(1, 0, 2).reshape(rows_ff, -1)[:, :units]
    return output, grad_tokens, r_qkv.result(), rest[padded:], rest[:padded], g_ff, g_one, g_two


def body(tokens, cotangent, segment, w_qkv, w_attn_out, w_in, w_ff_out, norm_one, norm_two):
    axis = "fsdp"
    n = lax.axis_size(axis)
    rows_in = w_in.shape[0]
    padded = -(-rows_in // 16) * 16
    w_in = jnp.pad(w_in, ((0, padded - rows_in), (0, 0)))
    w_ff_out = jnp.pad(
        w_ff_out.reshape(-1, n // 2, rows_in), ((0, 0), (0, 0), (0, padded - rows_in))
    ).reshape(-1, n // 2 * padded)
    aligned = not any(w.shape[0] % 16 for w in (w_qkv, w_attn_out, w_ff_out))
    way = by_links if aligned and n == 2 * Z * Y * X else by_collectives
    output, grad_tokens, g_qkv, g_out, g_in, g_ff, g_one, g_two = way(
        tokens, cotangent, segment, w_qkv, w_attn_out, w_in, w_ff_out, jnp.concatenate([norm_one, norm_two]), padded, axis
    )
    g_in, g_ff, g_norms = finish(g_in, g_ff, rows_in, padded, n, axis, g_one, g_two)
    return (output, grad_tokens, g_qkv, g_out, g_in, g_ff, g_norms[0], g_norms[1])


def solution(mesh):
    rows, flat = P("fsdp", None), P("fsdp")
    return jax.shard_map(
        body,
        mesh=mesh,
        in_specs=(rows, rows, flat, rows, rows, rows, rows, flat, flat),
        out_specs=(rows, rows, rows, rows, rows, rows, flat, flat),
        check_vma=False,
    )
```

```python
import functools
import math

import jax
import jax.numpy as jnp
from jax import lax
from jax.experimental import pallas as pl
from jax.experimental.pallas import tpu as pltpu
from jax.sharding import PartitionSpec as P

HD = 64
EPS = 1e-05
THETA = 160000.0
NEG = -1e30
LANES = 128
F32 = jnp.float32
BF16 = jnp.bfloat16
VMEM_BYTES = 60 << 20


def dot_nt(left, right):
    return lax.dot_general(left, right, (((1,), (1,)), ((), ())), preferred_element_type=F32)


def dot_nn(left, right):
    return lax.dot_general(left, right, (((1,), (0,)), ((), ())), preferred_element_type=F32)


def dot_tn(left, right):
    return lax.dot_general(left, right, (((0,), (0,)), ((), ())), preferred_element_type=F32)


def call(kernel, *, name, grid, in_specs, out_specs, out_shape, scratch=(), flops=0, nbytes=0, aliases=None):
    return pl.pallas_call(
        kernel,
        name=name,
        grid=grid,
        in_specs=in_specs,
        out_specs=out_specs,
        out_shape=out_shape,
        scratch_shapes=list(scratch),
        input_output_aliases=aliases or {},
        compiler_params=pltpu.CompilerParams(
            dimension_semantics=("arbitrary",) * len(grid), vmem_limit_bytes=VMEM_BYTES
        ),
        cost_estimate=pl.CostEstimate(flops=flops, transcendentals=0, bytes_accessed=nbytes),
    )


def sds(shape, dtype):
    return jax.ShapeDtypeStruct(shape, dtype)


def whole(shape):
    zeros = (0,) * len(shape)
    return pl.BlockSpec(shape, lambda *_: zeros)


def normalise(field):
    centre = jnp.mean(field, axis=-1, keepdims=True)
    centered = field - centre
    variance = jnp.mean(centered * centered, axis=-1, keepdims=True)
    inverse = lax.rsqrt(variance + EPS)
    return centered * inverse, inverse


def minus_row(field, row):
    return (field.reshape(-1, *row.shape) - row[None]).reshape(field.shape)


def swap_halves(field):
    lane = lax.broadcasted_iota(jnp.int32, field.shape, 1)
    first = (lane & (HD - 1)) < HD // 2
    return jnp.where(
        first, pltpu.roll(field, LANES - HD // 2, 1), pltpu.roll(field, HD // 2, 1)
    )


def fetch(weights, at, rows, target, sem):
    order_ref, pieces = weights
    i = 0
    for piece in pieces:
        for slot in range(piece.shape[0]):
            start = pl.multiple_of(order_ref[i] * rows, rows)
            pltpu.make_async_copy(
                piece.at[slot, pl.ds(at, rows), :], target.at[pl.ds(start, rows), :], sem
            ).start()
            i += 1


def arrive(target, sem):
    pltpu.make_async_copy(target, target, sem).wait()


def fetching_call(
    kernel, weights, *, name, grid, in_specs, out_specs, out_shape, scratch=(), flops=0, nbytes=0
):
    number = len(weights)

    def run(*refs):
        orders, rest, sets = refs[:number], refs[number:], []
        for order, (_, pieces) in zip(orders, weights, strict=True):
            sets.append((order, rest[: len(pieces)]))
            rest = rest[len(pieces) :]
        kernel(*sets, *rest)

    pieces = [piece for _, some in weights for piece in some]
    made = pl.pallas_call(
        run,
        name=name,
        grid_spec=pltpu.PrefetchScalarGridSpec(
            num_scalar_prefetch=number,
            grid=grid,
            in_specs=[pl.BlockSpec(memory_space=pl.ANY)] * len(pieces) + in_specs,
            out_specs=out_specs,
            scratch_shapes=list(scratch),
        ),
        out_shape=out_shape,
        compiler_params=pltpu.CompilerParams(
            dimension_semantics=("arbitrary",) * len(grid), vmem_limit_bytes=VMEM_BYTES
        ),
        cost_estimate=pl.CostEstimate(flops=flops, transcendentals=0, bytes_accessed=nbytes),
    )
    return lambda *args: made(*[order for order, _ in weights], *pieces, *args)


def unpack_gains(rows_ref, number, out_ref):
    total, width = rows_ref.shape
    devices = total // 8
    owner = lax.broadcasted_iota(jnp.int32, (devices, total), 0)
    row = lax.broadcasted_iota(jnp.int32, (devices, total), 1)
    found = dot_nn((row == owner * 8).astype(BF16), rows_ref[:, :LANES]).astype(BF16)
    place_in = lax.broadcasted_iota(jnp.int32, (LANES, width), 0)
    lane = lax.broadcasted_iota(jnp.int32, (LANES, width), 1)
    mine = lax.broadcasted_iota(jnp.int32, (devices, width), 1) // number
    mine = mine == lax.broadcasted_iota(jnp.int32, (devices, width), 0)
    for which in range(2):
        tiled = dot_nn(found, (place_in == lane % number + which * number).astype(BF16))
        out_ref[which : which + 1, :] = jnp.sum(jnp.where(mine, tiled, 0.0), axis=0, keepdims=True)


def project_kernel(rope_blocks, query_blocks, rows, given, weights, tok_ref, cos_ref, sin_ref, *refs):
    if given:
        gains_in, out_ref, hid_ref, gains_ref, w_ref, sem = refs
    else:
        out_ref, hid_ref, gains_ref, w_ref, sem, rows_ref, rows_sem = refs
    step = pl.program_id(0)
    block = out_ref.shape[1]

    @pl.when(step == 0)
    def _():
        if given:
            gains_ref[...] = gains_in[...]
        else:
            fetch(weights, rows, 8, rows_ref, rows_sem)
        fetch(weights, 0, rows, w_ref, sem)
        if not given:
            arrive(rows_ref, rows_sem)
            unpack_gains(rows_ref, w_ref.shape[1] * 8 // rows_ref.shape[0], gains_ref)
        normed, _ = normalise(tok_ref[...].astype(F32))
        hid_ref[...] = (normed * gains_ref[:1, :]).astype(BF16)
        arrive(w_ref, sem)

    acc = dot_nt(hid_ref[...], w_ref[pl.ds(pl.multiple_of(step * block, block), block), :])

    @pl.when(step < rope_blocks)
    def _():
        scale = jnp.where(step < query_blocks, 1.0 / math.sqrt(HD), 1.0).astype(F32)
        cosine, sine = cos_ref[...], sin_ref[...]
        for s in range(acc.shape[1] // LANES):
            part = acc[:, s * LANES : (s + 1) * LANES]
            turned = part * cosine + swap_halves(part) * sine
            out_ref[:, s * LANES : (s + 1) * LANES] = (turned * scale).astype(BF16)

    @pl.when(step >= rope_blocks)
    def _():
        out_ref[...] = acc.astype(BF16)


def project(tokens, cosine, sine, weights, rows, gains=None):
    count, width = tokens.shape
    total = 3 * width
    block = 512
    given = gains is not None
    own = [] if given else [pltpu.VMEM((weights[0].shape[0] * 8, width), BF16), pltpu.SemaphoreType.DMA]
    return fetching_call(
        functools.partial(project_kernel, 2 * width // block, width // block, rows, given),
        [weights],
        name="norm_project",
        grid=(total // block,),
        in_specs=[whole((count, width)), whole((count, LANES)), whole((count, LANES))]
        + [whole((2, width))] * given,
        out_specs=[
            pl.BlockSpec((count, block), lambda j, *_: (0, j)),
            whole((count, width)),
            whole((2, width)),
        ],
        out_shape=[sds((count, total), BF16), sds((count, width), BF16), sds((2, width), F32)],
        scratch=[pltpu.VMEM((total, width), BF16), pltpu.SemaphoreType.DMA] + own,
        flops=2 * count * width * total,
        nbytes=2 * (2 * count * width + total * width + total * count),
    )(tokens, cosine, sine, *([gains] if given else []))


def attend_kernel(q_ref, k_ref, v_ref, segc_ref, segr_ref, out_ref, lse_ref, vt_ref, ot_ref):
    count = q_ref.shape[0]
    vt_ref[...] = v_ref[...].T
    keys, query = k_ref[...], q_ref[...]
    lane = lax.broadcasted_iota(jnp.int32, query.shape, 1)
    allowed = jnp.concatenate([segc_ref[...]] * (count // LANES), axis=1) == segr_ref[...]
    for h in range(2):
        picked = jnp.where((lane >= h * HD) & (lane < (h + 1) * HD), query, jnp.zeros_like(query))
        scores = jnp.where(allowed, dot_nt(keys, picked), NEG)
        top = jnp.max(scores, axis=0, keepdims=True)
        powers = jnp.exp(scores - top)
        total = jnp.sum(powers, axis=0, keepdims=True)
        lse_ref[0, h : h + 1, :] = top + jnp.log(total)
        ot_ref[h * HD : (h + 1) * HD, :] = dot_nn(vt_ref[h * HD : (h + 1) * HD, :], powers.astype(BF16)) / total
    out_ref[...] = ot_ref[...].T.astype(BF16)


def attend(qkv, seg_column, seg_row, width, first, number, before=None):
    count = qkv.shape[0]
    pairs = width // LANES
    kept = () if before is None else tuple(before)

    def kernel(*refs):
        attend_kernel(*refs[:5], *refs[5 + len(kept) :])

    tall = lambda offset: pl.BlockSpec((count, LANES), lambda p: (0, offset + first + p))
    return call(
        kernel,
        name="attend",
        grid=(number,),
        in_specs=[tall(0), tall(pairs), tall(2 * pairs), whole((count, LANES)), whole((1, count))]
        + [pl.BlockSpec(memory_space=pl.ANY)] * len(kept),
        out_specs=[tall(0), pl.BlockSpec((1, 2, count), lambda p: (first + p, 0, 0))],
        out_shape=[sds((count, width), BF16), sds((pairs, 2, count), F32)],
        scratch=[pltpu.VMEM((LANES, count), BF16), pltpu.VMEM((LANES, count), F32)],
        flops=16 * count * count * LANES * number,
        nbytes=2 * 4 * count * LANES * number,
        aliases={5: 0, 6: 1} if kept else None,
    )(qkv, qkv, qkv, seg_column, seg_row, *kept)


def attend_back_kernel(
    chunk, q_ref, k_ref, v_ref, o_ref, g_ref, lse_ref, segc_ref, segr_ref, cos_ref, sin_ref,
    out_ref, kt_ref, dk_ref, dv_ref, dqt_ref, delta_ref, total_ref,
):
    count = q_ref.shape[0]
    kt_ref[...] = k_ref[...].T
    keys, values = k_ref[...], v_ref[...]
    product = (g_ref[...].astype(F32) * o_ref[...].astype(F32)).T
    for h in range(2):
        row = jnp.sum(product[h * HD : (h + 1) * HD, :], axis=0, keepdims=True)
        delta_ref[h] = jnp.broadcast_to(row, (8, count))
        total_ref[h] = jnp.broadcast_to(lse_ref[0, h : h + 1, :], (8, count))
    lane = lax.broadcasted_iota(jnp.int32, (chunk, LANES), 1)
    upper = lax.broadcasted_iota(jnp.int32, (LANES, chunk), 0) < HD
    for c in range(count // chunk):
        at = slice(c * chunk, (c + 1) * chunk)
        query, grad = q_ref[at, :], g_ref[at, :]
        allowed = jnp.concatenate([segc_ref[...]] * (chunk // LANES), axis=1) == segr_ref[:, at]
        grads = []
        for h in range(2):
            mine = (lane >= h * HD) & (lane < (h + 1) * HD)
            query_h = jnp.where(mine, query, jnp.zeros_like(query))
            grad_h = jnp.where(mine, grad, jnp.zeros_like(grad))
            scores = jnp.where(allowed, dot_nt(keys, query_h), NEG)
            weights = jnp.exp(minus_row(scores, total_ref[h, :, at]))
            grad_value = dot_nn(weights.astype(BF16), grad_h)
            spread = minus_row(dot_nt(values, grad_h), delta_ref[h, :, at])
            grad_scores = (weights * spread).astype(BF16)
            grads.append((dot_nn(grad_scores, query_h), grad_value, dot_nn(kt_ref[...], grad_scores)))
        (key_0, value_0, query_0), (key_1, value_1, query_1) = grads
        dqt_ref[:, at] = jnp.where(upper, query_0, query_1)
        if c == 0:
            dk_ref[...] = key_0 + key_1
            dv_ref[...] = value_0 + value_1
        else:
            dk_ref[...] += key_0 + key_1
            dv_ref[...] += value_0 + value_1

    cosine, sine = cos_ref[...], sin_ref[...]
    grad_query = dqt_ref[...].T * (1.0 / math.sqrt(HD))
    out_ref[0] = (grad_query * cosine - swap_halves(grad_query) * sine).astype(BF16)
    grad_key = dk_ref[...]
    out_ref[1] = (grad_key * cosine - swap_halves(grad_key) * sine).astype(BF16)
    out_ref[2] = dv_ref[...].astype(BF16)


def attend_back(qkv, attn_out, grad_heads, lse, seg_column, seg_row, cosine, sine, first, number, before=None):
    count, width = attn_out.shape
    pairs = width // LANES
    chunk = 256
    kept = () if before is None else (before,)

    def kernel(*refs):
        attend_back_kernel(chunk, *refs[:10], *refs[10 + len(kept) :])

    tall = lambda offset: pl.BlockSpec((count, LANES), lambda p: (0, offset + first + p))
    return call(
        kernel,
        name="attend_back",
        grid=(number,),
        in_specs=[
            tall(0),
            tall(pairs),
            tall(2 * pairs),
            tall(0),
            tall(0),
            pl.BlockSpec((1, 2, count), lambda p: (first + p, 0, 0)),
            whole((count, LANES)),
            whole((1, count)),
            whole((count, LANES)),
            whole((count, LANES)),
        ]
        + [pl.BlockSpec(memory_space=pl.ANY)] * len(kept),
        out_specs=pl.BlockSpec((3, count, LANES), lambda p: (0, 0, first + p)),
        out_shape=sds((3, count, width), BF16),
        scratch=[
            pltpu.VMEM((LANES, count), BF16),
            pltpu.VMEM((count, LANES), F32),
            pltpu.VMEM((count, LANES), F32),
            pltpu.VMEM((LANES, count), F32),
            pltpu.VMEM((2, 8, count), F32),
            pltpu.VMEM((2, 8, count), F32),
        ],
        flops=40 * count * count * LANES * number,
        nbytes=2 * 8 * count * LANES * number,
        aliases={10: 0} if kept else None,
    )(qkv, qkv, qkv, attn_out, grad_heads, lse, seg_column, seg_row, cosine, sine, *kept)


def ffn_kernel(
    rows_in, rows_out, rows_ff, weights_in, weights_ff,
    tok_ref, attn_ref, cot_ref, gain_ref,
    out_ref, mid_ref, low_ref, gnorm_ref, g_in_ref, g_out_ref,
    resid_ref, hid_ref, cot_t_ref, out_acc, w_attn_ref, w_in_ref, w_ff_ref, sem_attn, sem_in, sem_ff,
):
    step = pl.program_id(0)
    count = resid_ref.shape[0]
    block = g_out_ref.shape[1]
    units = w_in_ref.shape[0] // 2
    width = hid_ref.shape[1]
    some = 256

    @pl.when(step == 0)
    def _():
        fetch(weights_in, rows_in, rows_out, w_attn_ref, sem_attn)
        fetch(weights_in, 0, rows_in, w_in_ref, sem_in)
        for b in range(w_ff_ref.shape[0]):
            fetch(weights_ff, b * rows_ff, rows_ff, w_ff_ref.at[b], sem_ff)
        cot_t_ref[...] = cot_ref[...].T
        out_acc[...] = jnp.zeros_like(out_acc)
        mid_ref[...] = jnp.zeros_like(mid_ref)
        arrive(w_attn_ref, sem_attn)
        for i in range(count // some):
            at = slice(i * some, (i + 1) * some)
            resid = tok_ref[at, :].astype(F32) + dot_nt(attn_ref[at, :], w_attn_ref[...])
            resid_ref[at, :] = resid
            normed, _ = normalise(resid)
            hid_ref[at, :] = (normed * gain_ref[1:, :]).astype(BF16)
        arrive(w_in_ref, sem_in)
        arrive(w_ff_ref, sem_ff)

    hidden = hid_ref[...]
    w_pre = w_in_ref[pl.ds(pl.multiple_of(step * block, block), block), :]
    w_gate = w_in_ref[pl.ds(pl.multiple_of(units + step * block, block), block), :]
    per = width // block
    w_out = w_ff_ref[step // per, :, pl.ds(pl.multiple_of(step % per * block, block), block)]
    pre = dot_nt(hidden, w_pre)
    gate = dot_nt(hidden, w_gate)
    grad_mixed = dot_nn(cot_ref[...], w_out)
    cdf = 0.5 * (1.0 + lax.erf(pre * 0.7071067811865476))
    density = jnp.exp(-0.5 * pre * pre) * 0.3989422804014327
    gelu = pre * cdf
    mixed = (gelu * gate).astype(BF16)
    out_acc[...] += dot_nt(mixed, w_out)
    g_out_ref[...] = dot_nn(cot_t_ref[...], mixed).astype(BF16)
    grad_pre = (grad_mixed * gate * (cdf + pre * density)).astype(BF16)
    grad_gate = (grad_mixed * gelu).astype(BF16)
    g_in_ref[0] = dot_tn(grad_pre, hidden).astype(BF16)
    g_in_ref[1] = dot_tn(grad_gate, hidden).astype(BF16)
    mid_ref[...] += dot_nn(grad_pre, w_pre) + dot_nn(grad_gate, w_gate)

    @pl.when(step == pl.num_programs(0) - 1)
    def _():
        gnorm = jnp.zeros_like(gnorm_ref)
        for i in range(count // some):
            at = slice(i * some, (i + 1) * some)
            resid = resid_ref[at, :]
            out_ref[at, :] = (resid + out_acc[at, :]).astype(BF16)
            normed, inverse = normalise(resid)
            grad = mid_ref[at, :]
            gnorm += jnp.sum(grad * normed, axis=0, keepdims=True)
            hat = grad * gain_ref[1:, :]
            first = jnp.mean(hat, axis=-1, keepdims=True)
            second = jnp.mean(hat * normed, axis=-1, keepdims=True)
            mid = cot_ref[at, :].astype(F32) + inverse * (hat - first - normed * second)
            mid_ref[at, :] = mid
            low_ref[at, :] = mid.astype(BF16)
        gnorm_ref[...] = gnorm


def ffn(tokens, attn_out, cotangent, gains, w_in, w_ff, units, rows_in, rows_out, rows_ff):
    count, width = tokens.shape
    block = 256
    spans = -(-units // width)
    once = pl.BlockSpec((count, width), lambda *_: (0, 0), pipeline_mode=pl.Buffered(1))
    return fetching_call(
        functools.partial(ffn_kernel, rows_in, rows_out, rows_ff),
        [w_in, w_ff],
        name="ffn_forward_backward",
        grid=(units // block,),
        in_specs=[once, once, once, whole((2, width))],
        out_specs=[
            once,
            once,
            once,
            whole((1, width)),
            pl.BlockSpec((2, block, width), lambda j, *_: (0, j, 0)),
            pl.BlockSpec((width, block), lambda j, *_: (0, j)),
        ],
        out_shape=[
            sds((count, width), BF16),
            sds((count, width), F32),
            sds((count, width), BF16),
            sds((1, width), F32),
            sds((2, units, width), BF16),
            sds((width, units), BF16),
        ],
        scratch=[
            pltpu.VMEM((count, width), F32),
            pltpu.VMEM((count, width), BF16),
            pltpu.VMEM((width, count), BF16),
            pltpu.VMEM((count, width), F32),
            pltpu.VMEM((width, width), BF16),
            pltpu.VMEM((2 * units, width), BF16),
            pltpu.VMEM((spans, width, width), BF16),
            pltpu.SemaphoreType.DMA,
            pltpu.SemaphoreType.DMA,
            pltpu.SemaphoreType.DMA,
        ],
        flops=18 * count * width * units,
        nbytes=2 * (10 * count * width + 6 * units * width),
    )(tokens, attn_out, cotangent, gains)


def join_back_kernel(at, rows, weights, low_ref, attn_ref, heads_ref, gw_ref, w_ref, sem):
    step = pl.program_id(0)
    block = heads_ref.shape[1]

    @pl.when(step == 0)
    def _():
        fetch(weights, at, rows, w_ref, sem)
        arrive(w_ref, sem)

    span = pl.ds(pl.multiple_of(step * block, block), block)
    heads_ref[...] = dot_nn(low_ref[...], w_ref[:, span]).astype(BF16)
    gw_ref[...] = dot_tn(low_ref[:, span], attn_ref[...]).astype(BF16)


def join_back(low, attn_out, weights, at, rows):
    count, width = low.shape
    block = 256
    return fetching_call(
        functools.partial(join_back_kernel, at, rows),
        [weights],
        name="attn_out_back",
        grid=(width // block,),
        in_specs=[whole((count, width)), whole((count, width))],
        out_specs=[pl.BlockSpec((count, block), lambda j, *_: (0, j)), pl.BlockSpec((block, width), lambda j, *_: (j, 0))],
        out_shape=[sds((count, width), BF16), sds((width, width), BF16)],
        scratch=[pltpu.VMEM((width, width), BF16), pltpu.SemaphoreType.DMA],
        flops=4 * count * width * width,
        nbytes=2 * 5 * count * width,
    )(low, attn_out)


def project_grad_kernel(gp_ref, hid_ref, out_ref):
    out_ref[...] = dot_tn(gp_ref[0], hid_ref[...]).astype(BF16)


def project_grad(grad_projected, hidden):
    count, width = hidden.shape
    block = 512
    per = width // block
    return call(
        project_grad_kernel,
        name="grad_qkv",
        grid=(3 * per,),
        in_specs=[pl.BlockSpec((1, count, block), lambda j: (j // per, 0, j % per)), whole((count, width))],
        out_specs=pl.BlockSpec((block, width), lambda j: (j, 0)),
        out_shape=sds((3 * width, width), BF16),
        flops=6 * count * width * width,
        nbytes=2 * 7 * count * width,
    )(grad_projected, hidden)


def hidden_back_kernel(rows_qkv, weights, gp_ref, out_ref, w_ref, sem):
    step = pl.program_id(0)
    width = gp_ref.shape[2]

    @pl.when(step == 0)
    def _():
        fetch(weights, 0, rows_qkv, w_ref, sem)
        arrive(w_ref, sem)

    term = dot_nn(gp_ref[0], w_ref[pl.ds(pl.multiple_of(step * width, width), width), :])

    @pl.when(step == 0)
    def _():
        out_ref[...] = term

    @pl.when(step > 0)
    def _():
        out_ref[...] += term


def hidden_back(grad_projected, weights, rows_qkv):
    _, count, width = grad_projected.shape
    return fetching_call(
        functools.partial(hidden_back_kernel, rows_qkv),
        [weights],
        name="grad_hidden_one",
        grid=(3,),
        in_specs=[pl.BlockSpec((1, count, width), lambda j, *_: (j, 0, 0))],
        out_specs=[whole((count, width))],
        out_shape=[sds((count, width), F32)],
        scratch=[pltpu.VMEM((3 * width, width), BF16), pltpu.SemaphoreType.DMA],
        flops=6 * count * width * width,
        nbytes=2 * 8 * count * width,
    )(grad_projected)[0]


def norm_back_kernel(grad_ref, tok_ref, mid_ref, gain_ref, out_ref, gnorm_ref):
    normed, inverse = normalise(tok_ref[...].astype(F32))
    grad = grad_ref[...]
    part = jnp.sum(grad * normed, axis=0, keepdims=True)
    hat = grad * gain_ref[:1, :]
    first = jnp.mean(hat, axis=-1, keepdims=True)
    second = jnp.mean(hat * normed, axis=-1, keepdims=True)
    out_ref[...] = mid_ref[...] + inverse * (hat - first - normed * second)

    @pl.when(pl.program_id(0) == 0)
    def _():
        gnorm_ref[...] = part

    @pl.when(pl.program_id(0) > 0)
    def _():
        gnorm_ref[...] += part


def norm_back(grad, tokens, mid, gain):
    count, width = tokens.shape
    rows = pl.BlockSpec((128, width), lambda i: (i, 0))
    return call(
        norm_back_kernel,
        name="grad_tokens",
        grid=(count // 128,),
        in_specs=[rows, rows, rows, whole((2, width))],
        out_specs=[rows, whole((1, width))],
        out_shape=[sds((count, width), F32), sds((1, width), F32)],
        flops=20 * count * width,
        nbytes=14 * count * width,
    )(grad, tokens, mid, gain)


Z, Y, X = 4, 2, 2
UP, DOWN, IN_Y, IN_X = (1, 0, 0), (-1, 0, 0), (0, 1, 0), (0, 0, 1)
CROSSED, LEVEL, UPRIGHT = ("planes", "lines"), ("planes", "planes"), ("lines", "lines")
SPREAD = {
    CROSSED: (((UP, IN_X), (DOWN, IN_Y), (UP, IN_Y)), ((IN_Y, UP), (IN_X, DOWN), (IN_X, UP))),
    LEVEL: (((UP, UP), (DOWN, DOWN), (UP, UP)), ((IN_Y, IN_X), (IN_X, IN_Y), (IN_X, IN_Y))),
    UPRIGHT: (((IN_X, IN_Y), (IN_Y, IN_X), (IN_Y, IN_X)), ((UP, UP), (DOWN, DOWN), (UP, UP))),
}
REDUCE = {
    CROSSED: (((IN_X, DOWN), (IN_X, UP), (IN_Y, DOWN)), ((DOWN, IN_Y), (UP, IN_Y), (DOWN, IN_X))),
    LEVEL: (((IN_X, IN_Y), (IN_X, IN_Y), (IN_Y, IN_X)), ((DOWN, DOWN), (UP, UP), (DOWN, DOWN))),
    UPRIGHT: (((DOWN, DOWN), (UP, UP), (DOWN, DOWN)), ((IN_Y, IN_X), (IN_Y, IN_X), (IN_X, IN_Y))),
}


def ident(z, y, x, c):
    return (((z % Z) * Y + y % Y) * X + x % X) * 2 + c


def plus(*moves):
    return tuple(sum(m[i] for m in moves) for i in range(3))


def minus(move):
    return tuple(-m for m in move)


def hop(array, axis, moves):
    pairs = [
        (ident(z, y, x, c), ident(z + m[0], y + m[1], x + m[2], c))
        for z in range(Z) for y in range(Y) for x in range(X)
        for c, m in enumerate(moves)
    ]
    return lax.ppermute(array, axis, pairs)


def swap_cores(array, axis):
    return lax.ppermute(array, axis, [(i, i ^ 1) for i in range(2 * Z * Y * X)])


def place(axis):
    me = lax.axis_index(axis)
    return (me // (2 * Y * X), me // (2 * X) % Y, me // 2 % X), me % 2


def by_core(c, zero, one):
    return jnp.where(c == 0, jnp.stack(zero), jnp.stack(one)).astype(jnp.int32)


def together(*places):
    values = lax.optimization_barrier(tuple(getattr(owner, name) for owner, name in places))
    for (owner, name), value in zip(places, values, strict=True):
        setattr(owner, name, value)


def tie(*values):
    return lax.optimization_barrier(values)


class Spread:
    def __init__(self, shard, axis, route):
        self.shard, self.axis, self.route = shard, axis, route

    def near(self):
        short, _ = SPREAD[self.route]
        self.first = hop(self.shard, self.axis, short[0])
        self.third = hop(self.shard, self.axis, short[1])

    def nearer(self):
        short, _ = SPREAD[self.route]
        second = hop(self.first, self.axis, short[2])
        self.block = jnp.stack([self.shard, self.first, second, self.third])

    def far_one(self):
        self.one = hop(self.block, self.axis, SPREAD[self.route][1][0])

    def far_three(self):
        self.three = hop(self.block, self.axis, SPREAD[self.route][1][1])

    def farther(self):
        _, far = SPREAD[self.route]
        self.two = hop(self.one, self.axis, far[2])

    def swap(self, *names):
        for name in names:
            setattr(self, "other_" + name, swap_cores(getattr(self, name), self.axis))

    def result(self):
        short, far = SPREAD[self.route]
        names = ("block", "one", "two", "three")
        pieces = tuple(getattr(self, kind + name) for kind in ("", "other_") for name in names)
        at, c = place(self.axis)
        froms = []
        for core in range(2):
            s, f = [m[core] for m in short], [m[core] for m in far]
            close = [(0, 0, 0), s[0], plus(s[0], s[2]), s[1]]
            long = [(0, 0, 0), f[0], plus(f[0], f[2]), f[1]]
            froms.append([ident(*plus(at, minus(a), minus(b)), core) for a in long for b in close])
        order = jnp.concatenate([by_core(c, *froms), by_core(c, *froms[::-1])])
        return order, pieces


def lay_out(grad, wide):
    spans = [(b, min(b + wide, grad.shape[2])) for b in range(0, grad.shape[2], wide)]
    return spans, grad.shape[1] * len(spans)


def collect(grads, twins, extras, chosen, lines, wide, dtype):
    four = chosen.shape[1]
    total = sum(lay_out(g, wide)[1] for g in grads)
    k, number = len(grads) * four, len(lines)

    def kernel(chosen_ref, *refs):
        mine, theirs, more, outs = refs[:k], refs[k : 2 * k], refs[2 * k : -number], refs[-number:]

        def fill(out):
            for i in range(four):
                at = 0
                for g, t in zip(mine[i::four], theirs[i::four], strict=True):
                    rows = g.shape[1]
                    for a, b in lay_out(g, wide)[0]:
                        value = g[0, :, a:b].astype(F32) + t[0, :, a:b].astype(F32)
                        for m in more:
                            value = value + m[i, at : at + rows, : b - a].astype(F32)
                        out[i, at : at + rows, : b - a] = value.astype(dtype)
                        if b - a < wide:
                            out[i, at : at + rows, b - a :] = jnp.zeros((rows, wide - (b - a)), dtype)
                        at += rows

        for j, out in enumerate(outs):
            pl.when(pl.program_id(0) == j)(functools.partial(fill, out))

    def by_device(g, i):
        def index(j, chosen_ref):
            device = chosen_ref[lines[0], i]
            for step, which in enumerate(lines[1:], 1):
                device = jnp.where(j == step, chosen_ref[which, i], device)
            return device, 0, 0

        return pl.BlockSpec((1, *g.shape[1:]), index)

    devices = [by_device(g, i) for g in grads for i in range(four)]
    every = [g for g in grads for _ in range(four)]
    pairs = [t for t in twins for _ in range(four)]
    block = whole((four, total, wide))
    return pl.pallas_call(
        kernel,
        name="collect_grads",
        grid_spec=pltpu.PrefetchScalarGridSpec(
            num_scalar_prefetch=1,
            grid=(number,),
            in_specs=devices * 2 + [block] * len(extras),
            out_specs=[block] * number,
        ),
        out_shape=[sds((four, total, wide), dtype)] * number,
        compiler_params=pltpu.CompilerParams(
            dimension_semantics=("arbitrary",), vmem_limit_bytes=VMEM_BYTES
        ),
        cost_estimate=pl.CostEstimate(
            flops=number * four * total * wide * (1 + len(extras)),
            transcendentals=0,
            bytes_accessed=2 * number * four * total * wide * (3 + len(extras)),
        ),
    )(chosen, *every, *pairs, *extras)


def collect_last(grads, twins, extras, chosen, wide):
    four = chosen.shape[1]
    total = sum(lay_out(g, wide)[1] for g in grads)
    k = len(grads) * four

    def kernel(chosen_ref, *refs):
        mine, theirs, more, outs = refs[:k], refs[k : 2 * k], refs[2 * k : -3], refs[-3:]
        targets = [outs[0], outs[1], outs[2].at[0], outs[2].at[1]]
        for i, out in enumerate(targets):
            at = 0
            for g, t in zip(mine[i::four], theirs[i::four], strict=True):
                rows = g.shape[1]
                for a, b in lay_out(g, wide)[0]:
                    value = g[0, :, a:b].astype(F32) + t[0, :, a:b].astype(F32)
                    for m in more[i::four]:
                        value = value + m[0, at : at + rows, : b - a].astype(F32)
                    out[at : at + rows, : b - a] = value.astype(out.dtype)
                    if b - a < wide:
                        out[at : at + rows, b - a :] = jnp.zeros((rows, wide - (b - a)), out.dtype)
                    at += rows

    def pick(shape, line, i):
        return pl.BlockSpec((1, *shape[1:]), lambda j, chosen_ref: (chosen_ref[line, i], 0, 0))

    devices = [pick(g.shape, 3, i) for g in grads for i in range(four)]
    places = [pick(m.shape, 4, i) for m in extras for i in range(four)]
    flat, two = whole((total, wide)), whole((2, total, wide))
    return pl.pallas_call(
        kernel,
        name="collect_last_grads",
        grid_spec=pltpu.PrefetchScalarGridSpec(
            num_scalar_prefetch=1,
            grid=(1,),
            in_specs=devices * 2 + places,
            out_specs=[flat, flat, two],
        ),
        out_shape=[sds((total, wide), BF16), sds((total, wide), BF16), sds((2, total, wide), F32)],
        compiler_params=pltpu.CompilerParams(
            dimension_semantics=("arbitrary",), vmem_limit_bytes=VMEM_BYTES
        ),
        cost_estimate=pl.CostEstimate(
            flops=four * total * wide * (1 + len(extras)),
            transcendentals=0,
            bytes_accessed=2 * four * total * wide * (4 + len(extras)),
        ),
    )(chosen, *[a for a in (*grads, *twins, *extras) for _ in range(four)])


class Reduce:
    def __init__(self, axis, route, wide):
        self.axis, self.route, self.wide = axis, route, wide
        far, short = REDUCE[route]
        at, c = place(axis)
        both = lambda a, b: tuple(plus(i, j) for i, j in zip(a, b, strict=True))
        here = ((0, 0, 0), (0, 0, 0))

        def line(step):
            lists = []
            for core, kind in enumerate(route):
                z, y, x = plus(at, step[core])
                if kind == "planes":
                    lists.append([ident(k, y, x, core) for k in range(Z)])
                else:
                    lists.append([ident(z, j, k, core) for j in range(Y) for k in range(X)])
            return by_core(c, *lists)

        def slot(step):
            places = []
            for core, kind in enumerate(route):
                z, y, x = plus(at, step[core])
                places.append(z % Z if kind == "planes" else y % Y * X + x % X)
            return jnp.where(c == 0, places[0], places[1])

        ends = (both(short[0], short[2]), short[1], short[2], here)
        slots = jnp.stack([slot(step) for step in ends]).astype(jnp.int32)
        lines = [line(step) for step in (both(far[0], far[2]), far[1], far[2])]
        last = []
        for core in range(2):
            last.append([ident(*plus(at, step[core]), core) for step in ends])
        self.chosen = jnp.stack([*lines, by_core(c, *last), slots])

    def pair(self, grads):
        self.grads = grads
        self.twins = tuple(swap_cores(g, self.axis) for g in grads)

    def pack(self):
        self.one, self.two = collect(self.grads, self.twins, (), self.chosen, (0, 1), self.wide, BF16)

    def far(self):
        far, _ = REDUCE[self.route]
        self.one, self.two = hop(self.one, self.axis, far[0]), hop(self.two, self.axis, far[1])

    def repack(self):
        (self.three,) = collect(self.grads, self.twins, (self.one,), self.chosen, (2,), self.wide, BF16)

    def farther(self):
        far, _ = REDUCE[self.route]
        self.three = hop(self.three, self.axis, far[2])

    def gather(self):
        self.one, self.two, self.rest = collect_last(
            self.grads, self.twins, (self.two, self.three), self.chosen, self.wide
        )

    def near(self):
        _, short = REDUCE[self.route]
        self.one, self.two = hop(self.one, self.axis, short[0]), hop(self.two, self.axis, short[1])

    def nearer(self):
        _, short = REDUCE[self.route]
        self.three = hop((self.rest[0] + self.one.astype(F32)).astype(BF16), self.axis, short[2])

    def result(self):
        return self.rest[1] + self.two.astype(F32) + self.three.astype(F32)


def tables(segment):
    count = segment.shape[0]
    slots = jnp.arange(count, dtype=jnp.int32)
    order = jnp.where(segment < 0, count, segment)
    starts = jnp.sum((order[None, :] < order[:, None]).astype(jnp.int32), axis=1)
    positions = (slots - starts).astype(F32)
    half = HD // 2
    freqs = THETA ** (-2.0 * jnp.arange(half, dtype=F32) / HD)
    angles = positions[:, None] * freqs[None, :]
    cosine, sine = jnp.cos(angles), jnp.sin(angles)
    cosine = jnp.concatenate([cosine] * 4, axis=1)
    sine = jnp.concatenate([-sine, sine] * 2, axis=1)
    group = jnp.where(segment < 0, -1 - slots, segment)
    return cosine, sine, jnp.broadcast_to(group[:, None], (count, LANES)), group[None, :]


def spans_of(matrix, wide):
    rows, columns = matrix.shape
    count = -(-columns // wide)
    matrix = jnp.pad(matrix, ((0, 0), (0, count * wide - columns)))
    return matrix.reshape(rows, count, wide).transpose(1, 0, 2).reshape(count * rows, wide)


def finish(g_in, g_ff, rows_in, padded, n, axis, g_one, g_two):
    g_in = g_in[:rows_in]
    g_ff = g_ff.reshape(-1, n // 2, padded)[:, :, :rows_in].reshape(-1, n // 2 * rows_in)
    g_norms = jnp.stack([g_one.reshape(n, -1), g_two.reshape(n, -1)], axis=1)
    g_norms = jnp.sum(lax.all_to_all(g_norms, axis, 0, 0, tiled=True), axis=0)
    return g_in, g_ff, g_norms


def by_collectives(tokens, cotangent, segment, w_qkv, w_attn_out, w_in, w_ff_out, gains, padded, axis):
    n = lax.axis_size(axis)
    width = tokens.shape[1]
    units = n // 2 * padded
    pairs = width // LANES
    gather = lambda shard: lax.all_gather(shard, axis, axis=0, tiled=True)
    at_once = lambda matrix: (jnp.zeros((1,), jnp.int32), (matrix[None],))
    w_qkv, w_ff = at_once(gather(w_qkv)), at_once(spans_of(gather(w_ff_out), width))
    w_in = at_once(jnp.concatenate([gather(w_in), gather(w_attn_out)]))
    gains = gather(gains.reshape(1, 2, -1)).astype(F32).transpose(1, 0, 2).reshape(2, width)
    cosine, sine, seg_column, seg_row = tables(segment)
    qkv, hidden_one, gains = project(tokens, cosine, sine, w_qkv, 3 * width, gains)
    attn_out, lse = attend(qkv, seg_column, seg_row, width, 0, pairs)
    output, mid, low, g_two, g_in, g_ff = ffn(
        tokens, attn_out, cotangent, gains, w_in, w_ff, units, 2 * units, width, width
    )
    grad_heads, g_out = join_back(low, attn_out, w_in, 2 * units, width)
    grad_projected = attend_back(qkv, attn_out, grad_heads, lse, seg_column, seg_row, cosine, sine, 0, pairs)
    g_qkv = project_grad(grad_projected, hidden_one)
    grad_tokens, g_one = norm_back(hidden_back(grad_projected, w_qkv, 3 * width), tokens, mid, gains)
    scatter = lambda grad: lax.psum_scatter(grad, axis, scatter_dimension=0, tiled=True).astype(F32)
    g_in = g_in.reshape(2 * units, width)
    return output, grad_tokens, scatter(g_qkv), scatter(g_out), scatter(g_in), scatter(g_ff), g_one, g_two


class Box:
    pass


def by_links(tokens, cotangent, segment, w_qkv, w_attn_out, w_in, w_ff_out, gains, padded, axis):
    n = lax.axis_size(axis)
    width = tokens.shape[1]
    units = n // 2 * padded
    pairs = width // LANES
    rows_qkv, rows_out, rows_ff = w_qkv.shape[0], w_attn_out.shape[0], w_ff_out.shape[0]
    v = Box()
    gain_rows = jnp.pad(gains[None], ((0, 7), (0, width - gains.shape[0])))
    s_qkv = Spread(jnp.concatenate([w_qkv, gain_rows]), axis, LEVEL)
    s_in = Spread(jnp.concatenate([w_in, w_attn_out]), axis, LEVEL)
    s_ff = Spread(spans_of(w_ff_out, width), axis, UPRIGHT)
    r_ff, r_in, r_qkv = Reduce(axis, UPRIGHT, width), Reduce(axis, LEVEL, width), Reduce(axis, LEVEL, width)
    v.cosine, v.sine, v.seg_column, v.seg_row = tables(segment)

    s_qkv.near()
    s_ff.near()
    s_qkv.nearer()
    s_ff.nearer()
    together((s_qkv, "block"), (s_in, "shard"), (s_ff, "block"), *((v, k) for k in vars(v)))
    s_qkv.far_one()
    s_qkv.far_three()
    s_in.near()
    s_qkv.swap("block")
    together((s_qkv, "one"), (s_qkv, "three"), (s_qkv, "other_block"), (s_in, "first"), (s_in, "third"))
    s_qkv.farther()
    s_in.nearer()
    s_qkv.swap("one", "three")
    together((s_qkv, "two"), (s_qkv, "other_three"), (s_qkv, "other_one"), (s_in, "block"), (s_ff, "block"))
    s_in.far_one()
    s_in.far_three()
    s_ff.far_one()
    s_qkv.swap("two")
    s_ff.swap("block")
    w_qkv = s_qkv.result()
    v.qkv, v.hidden_one, v.gains = project(tokens, v.cosine, v.sine, w_qkv, rows_qkv)
    together((v, "qkv"), (s_ff, "one"), (s_ff, "block"), (s_in, "block"), (s_ff, "other_block"))
    s_ff.far_three()
    s_ff.swap("one")
    s_in.swap("block")
    attend_some = lambda first, number, done=None: attend(v.qkv, v.seg_column, v.seg_row, width, first, number, done)
    v.done = attend_some(0, pairs // 2)
    together(
        (v, "done"), (s_in, "one"), (s_in, "three"), (s_ff, "one"), (s_ff, "three"),
        (s_in, "other_block"), (s_ff, "other_one"),
    )
    s_in.farther()
    s_ff.farther()
    s_in.swap("one", "three")
    s_ff.swap("three")
    v.done = attend_some(pairs // 2, pairs // 2, v.done)
    together(
        (v, "done"), (s_in, "two"), (s_ff, "two"), (s_in, "other_one"), (s_in, "other_three"), (s_ff, "other_three")
    )
    s_in.swap("two")
    s_ff.swap("two")
    attn_out, lse = v.done
    w_in, w_ff = s_in.result(), s_ff.result()
    output, mid, low, g_two, g_in, g_ff = ffn(
        tokens, attn_out, cotangent, v.gains, w_in, w_ff, units, padded, rows_out, rows_ff
    )

    rows_of = lambda grad: grad.reshape(n, -1, grad.shape[-1])
    back = lambda first, number, before=None: attend_back(
        v.qkv, attn_out, v.grad_heads, lse, v.seg_column, v.seg_row, v.cosine, v.sine, first, number, before
    )
    eighth = pairs // 8
    r_ff.pair((rows_of(g_ff),))
    v.grad_heads, g_out = join_back(low, attn_out, w_in, padded, rows_out)
    r_in.pair((rows_of(g_in), rows_of(g_out)))
    v.some = back(0, 2 * eighth)
    together((v, "some"), (r_in, "twins"), (r_ff, "twins"))
    r_in.pack()
    r_ff.pack()
    together((v, "some"), (r_in, "one"), (r_in, "two"), (r_ff, "one"), (r_ff, "two"))
    r_in.far()
    r_ff.far()
    v.some = back(2 * eighth, 4 * eighth, v.some)
    together((v, "some"), (r_in, "one"), (r_in, "two"), (r_ff, "one"), (r_ff, "two"))
    r_in.repack()
    r_ff.repack()
    together((v, "some"), (r_in, "three"), (r_ff, "three"))
    r_in.farther()
    r_ff.farther()
    v.some = back(6 * eighth, 2 * eighth, v.some)
    v.g_qkv = project_grad(v.some, v.hidden_one)
    together((v, "some"), (v, "g_qkv"), (r_in, "three"), (r_ff, "three"))
    r_qkv.pair((rows_of(v.g_qkv),))
    r_ff.gather()
    together((v, "some"), (r_ff, "one"), (r_ff, "two"), (r_in, "three"))
    r_ff.near()
    r_in.gather()
    together((v, "some"), (r_qkv, "twins"), (r_in, "one"), (r_in, "two"), (r_ff, "one"), (r_ff, "two"))
    r_ff.nearer()
    r_in.near()
    r_qkv.pack()
    together((v, "some"), (r_qkv, "one"), (r_qkv, "two"))
    r_qkv.far()
    v.hidden = hidden_back(v.some, w_qkv, rows_qkv)
    together(
        (v, "hidden"), (r_qkv, "one"), (r_qkv, "two"), (r_in, "one"), (r_in, "two"), (r_ff, "three")
    )
    r_qkv.repack()
    together((v, "hidden"), (r_qkv, "three"))
    r_qkv.farther()
    r_in.nearer()
    v.grad_tokens, v.g_one = norm_back(v.hidden, tokens, mid, v.gains)
    together((v, "grad_tokens"), (v, "g_one"), (r_qkv, "three"), (r_in, "three"))
    r_qkv.gather()
    r_qkv.near()
    r_qkv.nearer()
    rest = r_in.result()
    g_ff = r_ff.result()
    g_ff = g_ff.reshape(-1, rows_ff, width).transpose(1, 0, 2).reshape(rows_ff, -1)[:, :units]
    return output, v.grad_tokens, r_qkv.result(), rest[padded:], rest[:padded], g_ff, v.g_one, g_two


def body(tokens, cotangent, segment, w_qkv, w_attn_out, w_in, w_ff_out, norm_one, norm_two):
    axis = "fsdp"
    n = lax.axis_size(axis)
    rows_in = w_in.shape[0]
    padded = -(-rows_in // 16) * 16
    w_in = jnp.pad(w_in, ((0, padded - rows_in), (0, 0)))
    w_ff_out = jnp.pad(
        w_ff_out.reshape(-1, n // 2, rows_in), ((0, 0), (0, 0), (0, padded - rows_in))
    ).reshape(-1, n // 2 * padded)
    aligned = not any(w.shape[0] % 16 for w in (w_qkv, w_attn_out, w_ff_out))
    way = by_links if aligned and n == 2 * Z * Y * X else by_collectives
    output, grad_tokens, g_qkv, g_out, g_in, g_ff, g_one, g_two = way(
        tokens, cotangent, segment, w_qkv, w_attn_out, w_in, w_ff_out, jnp.concatenate([norm_one, norm_two]), padded, axis
    )
    g_in, g_ff, g_norms = finish(g_in, g_ff, rows_in, padded, n, axis, g_one, g_two)
    return (output, grad_tokens, g_qkv, g_out, g_in, g_ff, g_norms[0], g_norms[1])


def solution(mesh):
    rows, flat = P("fsdp", None), P("fsdp")
    return jax.shard_map(
        body,
        mesh=mesh,
        in_specs=(rows, rows, flat, rows, rows, rows, rows, flat, flat),
        out_specs=(rows, rows, rows, rows, rows, rows, flat, flat),
        check_vma=False,
    )
```

```python
import functools
import math

import jax
import jax.numpy as jnp
from jax import lax
from jax.experimental import pallas as pl
from jax.experimental.pallas import tpu as pltpu
from jax.sharding import PartitionSpec as P

HD = 64
EPS = 1e-05
THETA = 160000.0
NEG = -1e30
LANES = 128
F32 = jnp.float32
BF16 = jnp.bfloat16
VMEM_BYTES = 62 << 20


def dot_nt(left, right):
    return lax.dot_general(left, right, (((1,), (1,)), ((), ())), preferred_element_type=F32)


def dot_nn(left, right):
    return lax.dot_general(left, right, (((1,), (0,)), ((), ())), preferred_element_type=F32)


def dot_tn(left, right):
    return lax.dot_general(left, right, (((0,), (0,)), ((), ())), preferred_element_type=F32)


def call(kernel, *, name, grid, in_specs, out_specs, out_shape, scratch=(), flops=0, nbytes=0, aliases=None):
    return pl.pallas_call(
        kernel,
        name=name,
        grid=grid,
        in_specs=in_specs,
        out_specs=out_specs,
        out_shape=out_shape,
        scratch_shapes=list(scratch),
        input_output_aliases=aliases or {},
        compiler_params=pltpu.CompilerParams(
            dimension_semantics=("arbitrary",) * len(grid), vmem_limit_bytes=VMEM_BYTES
        ),
        cost_estimate=pl.CostEstimate(flops=flops, transcendentals=0, bytes_accessed=nbytes),
    )


def sds(shape, dtype):
    return jax.ShapeDtypeStruct(shape, dtype)


def whole(shape, once=False):
    zeros = (0,) * len(shape)
    mode = dict(pipeline_mode=pl.Buffered(1)) if once else {}
    return pl.BlockSpec(shape, lambda *_: zeros, **mode)


def normalise(field):
    centre = jnp.mean(field, axis=-1, keepdims=True)
    centered = field - centre
    variance = jnp.mean(centered * centered, axis=-1, keepdims=True)
    inverse = lax.rsqrt(variance + EPS)
    return centered * inverse, inverse


def minus_row(field, row):
    return (field.reshape(-1, *row.shape) - row[None]).reshape(field.shape)


def swap_halves(field):
    lane = lax.broadcasted_iota(jnp.int32, field.shape, 1)
    first = (lane & (HD - 1)) < HD // 2
    return jnp.where(
        first, pltpu.roll(field, LANES - HD // 2, 1), pltpu.roll(field, HD // 2, 1)
    )


def fetch(weights, at, rows, target, sem, group=None):
    order_ref, pieces = weights
    i = 0
    for piece in pieces:
        for slot in range(piece.shape[0]):
            device = order_ref[i]
            start = pl.multiple_of(device * rows, rows)
            pltpu.make_async_copy(
                piece.at[slot, pl.ds(at, rows), :],
                target.at[pl.ds(start, rows), :],
                sem if group is None else sem.at[device // group],
            ).start()
            i += 1


def arrive(target, sem):
    pltpu.make_async_copy(target, target, sem).wait()


def grouping(weights, group):
    devices = weights[0].shape[0]
    return (group, devices // group) if devices % group == 0 else (devices, 1)


def arrive_in_time(target, sem, rows, groups, block, step):
    for g in groups:
        @pl.when(step == (g - groups[0]) * rows // block)
        def _(g=g):
            arrive(target.at[pl.ds(g * rows, rows), :], sem.at[g])


def fetching_call(
    kernel, weights, *, name, grid, in_specs, out_specs, out_shape, scratch=(), flops=0, nbytes=0
):
    number = len(weights)

    def run(*refs):
        orders, rest, sets = refs[:number], refs[number:], []
        for order, (_, pieces) in zip(orders, weights, strict=True):
            sets.append((order, rest[: len(pieces)]))
            rest = rest[len(pieces) :]
        kernel(*sets, *rest)

    pieces = [piece for _, some in weights for piece in some]
    made = pl.pallas_call(
        run,
        name=name,
        grid_spec=pltpu.PrefetchScalarGridSpec(
            num_scalar_prefetch=number,
            grid=grid,
            in_specs=[pl.BlockSpec(memory_space=pl.ANY)] * len(pieces) + in_specs,
            out_specs=out_specs,
            scratch_shapes=list(scratch),
        ),
        out_shape=out_shape,
        compiler_params=pltpu.CompilerParams(
            dimension_semantics=("arbitrary",) * len(grid), vmem_limit_bytes=VMEM_BYTES
        ),
        cost_estimate=pl.CostEstimate(flops=flops, transcendentals=0, bytes_accessed=nbytes),
    )
    return lambda *args: made(*[order for order, _ in weights], *pieces, *args)


def unpack_gains(rows_ref, number, out_ref):
    total, width = rows_ref.shape
    devices = total // 8
    owner = lax.broadcasted_iota(jnp.int32, (devices, total), 0)
    row = lax.broadcasted_iota(jnp.int32, (devices, total), 1)
    found = dot_nn((row == owner * 8).astype(BF16), rows_ref[:, :LANES]).astype(BF16)
    place_in = lax.broadcasted_iota(jnp.int32, (LANES, width), 0)
    lane = lax.broadcasted_iota(jnp.int32, (LANES, width), 1) & (number - 1)
    first = lax.broadcasted_iota(jnp.int32, (devices, width), 0) * number
    column = lax.broadcasted_iota(jnp.int32, (devices, width), 1)
    mine = (column >= first) & (column < first + number)
    for which in range(2):
        tiled = dot_nn(found, (place_in == lane + which * number).astype(BF16))
        out_ref[which : which + 1, :] = jnp.sum(jnp.where(mine, tiled, 0.0), axis=0, keepdims=True)


def project_kernel(rope_blocks, query_blocks, rows, given, group, groups, weights, tok_ref, cos_ref, sin_ref, *refs):
    if given:
        gains_in, out_ref, hid_ref, gains_ref, w_ref, sem = refs
    else:
        out_ref, hid_ref, gains_ref, w_ref, sem, rows_ref, rows_sem = refs
    step = pl.program_id(0)
    block = out_ref.shape[1]

    @pl.when(step == 0)
    def _():
        if given:
            gains_ref[...] = gains_in[...]
        else:
            fetch(weights, rows, 8, rows_ref, rows_sem)
        fetch(weights, 0, rows, w_ref, sem, group)
        if not given:
            arrive(rows_ref, rows_sem)
            unpack_gains(rows_ref, w_ref.shape[1] * 8 // rows_ref.shape[0], gains_ref)
        normed, _ = normalise(tok_ref[...].astype(F32))
        hid_ref[...] = (normed * gains_ref[:1, :]).astype(BF16)

    arrive_in_time(w_ref, sem, group * rows, range(groups), block, step)
    w_block = w_ref[pl.ds(pl.multiple_of(step * block, block), block), :]
    some = 256

    @pl.when(step < rope_blocks)
    def _():
        scale = jnp.where(step < query_blocks, 1.0 / math.sqrt(HD), 1.0).astype(F32)
        for r in range(hid_ref.shape[0] // some):
            at = slice(r * some, (r + 1) * some)
            acc = dot_nt(hid_ref[at, :], w_block)
            cosine, sine = cos_ref[at, :] * scale, sin_ref[at, :] * scale
            for s in range(block // LANES):
                part = acc[:, s * LANES : (s + 1) * LANES]
                out_ref[at, s * LANES : (s + 1) * LANES] = (part * cosine + swap_halves(part) * sine).astype(BF16)

    @pl.when(step >= rope_blocks)
    def _():
        for r in range(hid_ref.shape[0] // some):
            at = slice(r * some, (r + 1) * some)
            out_ref[at, :] = dot_nt(hid_ref[at, :], w_block).astype(BF16)


def project(tokens, cosine, sine, weights, rows, gains=None):
    count, width = tokens.shape
    total = 3 * width
    block = 512
    given = gains is not None
    group, groups = grouping(weights, 4)
    own = [] if given else [pltpu.VMEM((weights[0].shape[0] * 8, width), BF16), pltpu.SemaphoreType.DMA]
    return fetching_call(
        functools.partial(project_kernel, 2 * width // block, width // block, rows, given, group, groups),
        [weights],
        name="norm_project",
        grid=(total // block,),
        in_specs=[whole((count, width)), whole((count, LANES)), whole((count, LANES))]
        + [whole((2, width))] * given,
        out_specs=[
            pl.BlockSpec((count, block), lambda j, *_: (0, j)),
            whole((count, width)),
            whole((2, width)),
        ],
        out_shape=[sds((count, total), BF16), sds((count, width), BF16), sds((2, width), F32)],
        scratch=[pltpu.VMEM((total, width), BF16), pltpu.SemaphoreType.DMA((groups,))] + own,
        flops=2 * count * width * total,
        nbytes=2 * (2 * count * width + total * width + total * count),
    )(tokens, cosine, sine, *([gains] if given else []))


def attend_kernel(q_ref, k_ref, v_ref, segc_ref, segr_ref, out_ref, lse_ref, vt_ref, ot_ref):
    count = q_ref.shape[0]
    vt_ref[...] = v_ref[...].T
    keys, query = k_ref[...], q_ref[...]
    lane = lax.broadcasted_iota(jnp.int32, query.shape, 1)
    allowed = jnp.concatenate([segc_ref[...]] * (count // LANES), axis=1) == segr_ref[...]
    for h in range(2):
        picked = jnp.where((lane >= h * HD) & (lane < (h + 1) * HD), query, jnp.zeros_like(query))
        scores = jnp.where(allowed, dot_nt(keys, picked), NEG)
        top = jnp.max(scores, axis=0, keepdims=True)
        powers = jnp.exp(scores - top)
        total = jnp.sum(powers, axis=0, keepdims=True)
        lse_ref[0, h : h + 1, :] = top + jnp.log(total)
        ot_ref[h * HD : (h + 1) * HD, :] = dot_nn(vt_ref[h * HD : (h + 1) * HD, :], powers.astype(BF16)) / total
    out_ref[...] = ot_ref[...].T.astype(BF16)


def attend(qkv, seg_column, seg_row, width, first, number, before=None):
    count = qkv.shape[0]
    pairs = width // LANES
    kept = () if before is None else tuple(before)

    def kernel(*refs):
        attend_kernel(*refs[:5], *refs[5 + len(kept) :])

    tall = lambda offset: pl.BlockSpec((count, LANES), lambda p: (0, offset + first + p))
    return call(
        kernel,
        name="attend",
        grid=(number,),
        in_specs=[tall(0), tall(pairs), tall(2 * pairs), whole((count, LANES)), whole((1, count))]
        + [pl.BlockSpec(memory_space=pl.ANY)] * len(kept),
        out_specs=[tall(0), pl.BlockSpec((1, 2, count), lambda p: (first + p, 0, 0))],
        out_shape=[sds((count, width), BF16), sds((pairs, 2, count), F32)],
        scratch=[pltpu.VMEM((LANES, count), BF16), pltpu.VMEM((LANES, count), F32)],
        flops=16 * count * count * LANES * number,
        nbytes=2 * 4 * count * LANES * number,
        aliases={5: 0, 6: 1} if kept else None,
    )(qkv, qkv, qkv, seg_column, seg_row, *kept)


def attend_back_kernel(
    chunk, q_ref, k_ref, v_ref, o_ref, g_ref, lse_ref, segc_ref, segr_ref, cos_ref, sin_ref,
    out_ref, kt_ref, dk_ref, dv_ref, dqt_ref, delta_ref, total_ref,
):
    count = q_ref.shape[0]
    kt_ref[...] = k_ref[...].T
    keys, values = k_ref[...], v_ref[...]
    product = (g_ref[...].astype(F32) * o_ref[...].astype(F32)).T
    for h in range(2):
        row = jnp.sum(product[h * HD : (h + 1) * HD, :], axis=0, keepdims=True)
        delta_ref[h] = jnp.broadcast_to(row, (8, count))
        total_ref[h] = jnp.broadcast_to(lse_ref[0, h : h + 1, :], (8, count))
    lane = lax.broadcasted_iota(jnp.int32, (chunk, LANES), 1)
    upper = lax.broadcasted_iota(jnp.int32, (LANES, chunk), 0) < HD
    for c in range(count // chunk):
        at = slice(c * chunk, (c + 1) * chunk)
        query, grad = q_ref[at, :], g_ref[at, :]
        allowed = jnp.concatenate([segc_ref[...]] * (chunk // LANES), axis=1) == segr_ref[:, at]
        grads = []
        for h in range(2):
            mine = (lane >= h * HD) & (lane < (h + 1) * HD)
            query_h = jnp.where(mine, query, jnp.zeros_like(query))
            grad_h = jnp.where(mine, grad, jnp.zeros_like(grad))
            scores = jnp.where(allowed, dot_nt(keys, query_h), NEG)
            weights = jnp.exp(minus_row(scores, total_ref[h, :, at]))
            grad_value = dot_nn(weights.astype(BF16), grad_h)
            spread = minus_row(dot_nt(values, grad_h), delta_ref[h, :, at])
            grad_scores = (weights * spread).astype(BF16)
            grads.append((dot_nn(grad_scores, query_h), grad_value, dot_nn(kt_ref[...], grad_scores)))
        (key_0, value_0, query_0), (key_1, value_1, query_1) = grads
        dqt_ref[:, at] = jnp.where(upper, query_0, query_1)
        if c == 0:
            dk_ref[...] = key_0 + key_1
            dv_ref[...] = value_0 + value_1
        else:
            dk_ref[...] += key_0 + key_1
            dv_ref[...] += value_0 + value_1

    cosine, sine = cos_ref[...], sin_ref[...]
    grad_query = dqt_ref[...].T * (1.0 / math.sqrt(HD))
    out_ref[0] = (grad_query * cosine - swap_halves(grad_query) * sine).astype(BF16)
    grad_key = dk_ref[...]
    out_ref[1] = (grad_key * cosine - swap_halves(grad_key) * sine).astype(BF16)
    out_ref[2] = dv_ref[...].astype(BF16)


def attend_back(qkv, attn_out, grad_heads, lse, seg_column, seg_row, cosine, sine, first, number, before=None):
    count, width = attn_out.shape
    pairs = width // LANES
    chunk = 256
    kept = () if before is None else (before,)

    def kernel(*refs):
        attend_back_kernel(chunk, *refs[:10], *refs[10 + len(kept) :])

    tall = lambda offset: pl.BlockSpec((count, LANES), lambda p: (0, offset + first + p))
    return call(
        kernel,
        name="attend_back",
        grid=(number,),
        in_specs=[
            tall(0),
            tall(pairs),
            tall(2 * pairs),
            tall(0),
            tall(0),
            pl.BlockSpec((1, 2, count), lambda p: (first + p, 0, 0)),
            whole((count, LANES)),
            whole((1, count)),
            whole((count, LANES)),
            whole((count, LANES)),
        ]
        + [pl.BlockSpec(memory_space=pl.ANY)] * len(kept),
        out_specs=pl.BlockSpec((3, count, LANES), lambda p: (0, 0, first + p)),
        out_shape=sds((3, count, width), BF16),
        scratch=[
            pltpu.VMEM((LANES, count), BF16),
            pltpu.VMEM((count, LANES), F32),
            pltpu.VMEM((count, LANES), F32),
            pltpu.VMEM((LANES, count), F32),
            pltpu.VMEM((2, 8, count), F32),
            pltpu.VMEM((2, 8, count), F32),
        ],
        flops=40 * count * count * LANES * number,
        nbytes=2 * 8 * count * LANES * number,
        aliases={10: 0} if kept else None,
    )(qkv, qkv, qkv, attn_out, grad_heads, lse, seg_column, seg_row, cosine, sine, *kept)


def ffn_kernel(
    rows_in, rows_out, rows_ff, group, groups, weights_in, weights_ff,
    tok_ref, attn_ref, cot_ref, gain_ref,
    resid_ref, mixed_ref, mid_ref, heads_ref, g_attn_ref, gnorm_ref, g_in_ref, g_out_ref,
    hid_ref, cot_t_ref, w_attn_ref, w_in_ref, w_ff_ref, sem_attn, sem_in, sem_ff,
):
    step = pl.program_id(0)
    count = resid_ref.shape[0]
    block = g_out_ref.shape[1]
    units = w_in_ref.shape[0] // 2
    width = hid_ref.shape[1]
    some = 256

    @pl.when(step == 0)
    def _():
        fetch(weights_in, rows_in, rows_out, w_attn_ref, sem_attn)
        fetch(weights_ff, 0, rows_ff, w_ff_ref.at[0], sem_ff.at[0])
        fetch(weights_in, 0, rows_in, w_in_ref, sem_in, group)
        for b in range(1, w_ff_ref.shape[0]):
            fetch(weights_ff, b * rows_ff, rows_ff, w_ff_ref.at[b], sem_ff.at[b])
        cot_t_ref[...] = cot_ref[...].T
        mid_ref[...] = jnp.zeros_like(mid_ref)
        arrive(w_attn_ref, sem_attn)
        for i in range(count // some):
            at = slice(i * some, (i + 1) * some)
            resid = tok_ref[at, :].astype(F32) + dot_nt(attn_ref[at, :], w_attn_ref[...])
            resid_ref[at, :] = resid
            normed, _ = normalise(resid)
            hid_ref[at, :] = (normed * gain_ref[1:, :]).astype(BF16)

    half = max(groups // 2, 1)
    for some_groups in (range(half), range(half, groups)):
        if some_groups:
            arrive_in_time(w_in_ref, sem_in, group * rows_in, some_groups, block, step)
    for b in range(w_ff_ref.shape[0]):
        pl.when(step == b * width // block)(functools.partial(arrive, w_ff_ref.at[b], sem_ff.at[b]))
    hidden = hid_ref[...]
    w_pre = w_in_ref[pl.ds(pl.multiple_of(step * block, block), block), :]
    w_gate = w_in_ref[pl.ds(pl.multiple_of(units + step * block, block), block), :]
    per = width // block
    w_out = w_ff_ref[step // per, :, pl.ds(pl.multiple_of(step % per * block, block), block)]
    pre = dot_nt(hidden, w_pre)
    gate = dot_nt(hidden, w_gate)
    grad_mixed = dot_nn(cot_ref[...], w_out)
    cdf = 0.5 * (1.0 + lax.erf(pre * 0.7071067811865476))
    density = jnp.exp(-0.5 * pre * pre) * 0.3989422804014327
    gelu = pre * cdf
    mixed = (gelu * gate).astype(BF16)
    mixed_ref[...] = mixed
    g_out_ref[...] = dot_nn(cot_t_ref[...], mixed).astype(BF16)
    grad_pre = (grad_mixed * gate * (cdf + pre * density)).astype(BF16)
    grad_gate = (grad_mixed * gelu).astype(BF16)
    g_in_ref[0] = dot_tn(grad_pre, hidden).astype(BF16)
    g_in_ref[1] = dot_tn(grad_gate, hidden).astype(BF16)
    mid_ref[...] += dot_nn(grad_pre, w_pre) + dot_nn(grad_gate, w_gate)

    @pl.when(step == pl.num_programs(0) - 1)
    def _():
        gnorm = jnp.zeros_like(gnorm_ref)
        for i in range(count // some):
            at = slice(i * some, (i + 1) * some)
            resid = resid_ref[at, :]
            normed, inverse = normalise(resid)
            grad = mid_ref[at, :]
            gnorm += jnp.sum(grad * normed, axis=0, keepdims=True)
            hat = grad * gain_ref[1:, :]
            first = jnp.mean(hat, axis=-1, keepdims=True)
            second = jnp.mean(hat * normed, axis=-1, keepdims=True)
            mid = cot_ref[at, :].astype(F32) + inverse * (hat - first - normed * second)
            mid_ref[at, :] = mid
            low = mid.astype(BF16)
            cot_t_ref[at, :] = low
            heads_ref[at, :] = dot_nn(low, w_attn_ref[...]).astype(BF16)
        gnorm_ref[...] = gnorm
        for i in range(width // some):
            at = slice(i * some, (i + 1) * some)
            g_attn_ref[at, :] = dot_tn(cot_t_ref[:, at], attn_ref[...]).astype(BF16)


def ffn(tokens, attn_out, cotangent, gains, w_in, w_ff, units, rows_in, rows_out, rows_ff):
    count, width = tokens.shape
    block = 256
    spans = -(-units // width)
    group, groups = grouping(w_in, 2)
    once = whole((count, width), once=True)
    return fetching_call(
        functools.partial(ffn_kernel, rows_in, rows_out, rows_ff, group, groups),
        [w_in, w_ff],
        name="ffn_forward_backward",
        grid=(units // block,),
        in_specs=[once, once, once, whole((2, width))],
        out_specs=[
            once,
            pl.BlockSpec((count, block), lambda j, *_: (0, j)),
            once,
            once,
            whole((width, width), once=True),
            whole((1, width)),
            pl.BlockSpec((2, block, width), lambda j, *_: (0, j, 0)),
            pl.BlockSpec((width, block), lambda j, *_: (0, j)),
        ],
        out_shape=[
            sds((count, width), F32),
            sds((count, units), BF16),
            sds((count, width), F32),
            sds((count, width), BF16),
            sds((width, width), BF16),
            sds((1, width), F32),
            sds((2, units, width), BF16),
            sds((width, units), BF16),
        ],
        scratch=[
            pltpu.VMEM((count, width), BF16),
            pltpu.VMEM((width, count), BF16),
            pltpu.VMEM((width, width), BF16),
            pltpu.VMEM((2 * units, width), BF16),
            pltpu.VMEM((spans, width, width), BF16),
            pltpu.SemaphoreType.DMA,
            pltpu.SemaphoreType.DMA((groups,)),
            pltpu.SemaphoreType.DMA((spans,)),
        ],
        flops=16 * count * width * units,
        nbytes=2 * (10 * count * width + 6 * units * width),
    )(tokens, attn_out, cotangent, gains)


def ffn_out_kernel(rows_ff, weights, resid_ref, mixed_ref, out_ref, w_ref, sem):
    @pl.when(pl.program_id(0) == 0)
    def _():
        for b in range(w_ref.shape[0]):
            fetch(weights, b * rows_ff, rows_ff, w_ref.at[b], sem.at[b])

    units, width = mixed_ref.shape[1], out_ref.shape[1]
    out = resid_ref[...]
    for b in range(w_ref.shape[0]):
        pl.when(pl.program_id(0) == 0)(functools.partial(arrive, w_ref.at[b], sem.at[b]))
        stop = min(width, units - b * width)
        out = out + dot_nt(mixed_ref[:, b * width : b * width + stop], w_ref[b, :, :stop])
    out_ref[...] = out.astype(BF16)


def ffn_out(resid, mixed, weights, rows_ff):
    count, width = resid.shape
    units = mixed.shape[1]
    spans = -(-units // width)
    rows = lambda columns: pl.BlockSpec((256, columns), lambda i, *_: (i, 0))
    return fetching_call(
        functools.partial(ffn_out_kernel, rows_ff),
        [weights],
        name="ffn_output",
        grid=(count // 256,),
        in_specs=[rows(width), rows(units)],
        out_specs=[rows(width)],
        out_shape=[sds((count, width), BF16)],
        scratch=[pltpu.VMEM((spans, width, width), BF16), pltpu.SemaphoreType.DMA((spans,))],
        flops=2 * count * width * units,
        nbytes=2 * (count * units + 3 * count * width + units * width),
    )(resid, mixed)[0]


def project_grad_kernel(gp_ref, hid_ref, out_ref):
    out_ref[...] = dot_tn(gp_ref[0], hid_ref[...]).astype(BF16)


def project_grad(grad_projected, hidden):
    count, width = hidden.shape
    block = 512
    per = width // block
    return call(
        project_grad_kernel,
        name="grad_qkv",
        grid=(3 * per,),
        in_specs=[pl.BlockSpec((1, count, block), lambda j: (j // per, 0, j % per)), whole((count, width))],
        out_specs=pl.BlockSpec((block, width), lambda j: (j, 0)),
        out_shape=sds((3 * width, width), BF16),
        flops=6 * count * width * width,
        nbytes=2 * 7 * count * width,
    )(grad_projected, hidden)


def project_grad_halves_kernel(rows, core_ref, gp_ref, hid_ref, stay_ref, go_ref, acc_ref):
    step = pl.program_id(0)
    block, width = acc_ref.shape

    def product(k):
        parts, at = [], k * block
        while at < (k + 1) * block:
            stop = min((k + 1) * block, (at // width + 1) * width)
            parts.append(gp_ref[at // width, :, at % width : at % width + stop - at])
            at = stop
        acc_ref[...] = dot_tn(jnp.concatenate(parts, axis=1), hid_ref[...])

    for k in range(gp_ref.shape[0] * width // block):
        pl.when(step == k)(functools.partial(product, k))
    mine = core_ref[0]
    for pair in range(block // (2 * rows)):
        to = slice(pair * rows, (pair + 1) * rows)
        for out, core in ((stay_ref, mine), (go_ref, 1 - mine)):
            start = pl.multiple_of((2 * pair + core) * rows, rows)
            out[to, :] = acc_ref[pl.ds(start, rows), :].astype(BF16)


def project_grad_halves(grad_projected, hidden, rows, core):
    count, width = hidden.shape
    total = 3 * width
    block = next(b for b in range(LANES, total + 1, LANES) if b % (2 * rows) == 0 and total % b == 0)
    half = pl.BlockSpec((block // 2, width), lambda j, _: (j, 0))
    return pl.pallas_call(
        functools.partial(project_grad_halves_kernel, rows),
        name="grad_qkv",
        grid_spec=pltpu.PrefetchScalarGridSpec(
            num_scalar_prefetch=1,
            grid=(total // block,),
            in_specs=[whole(grad_projected.shape, once=True), whole((count, width))],
            out_specs=[half, half],
            scratch_shapes=[pltpu.VMEM((block, width), F32)],
        ),
        out_shape=[sds((total // 2, width), BF16)] * 2,
        compiler_params=pltpu.CompilerParams(
            dimension_semantics=("arbitrary",), vmem_limit_bytes=VMEM_BYTES
        ),
        cost_estimate=pl.CostEstimate(
            flops=6 * count * width * width, transcendentals=0, bytes_accessed=14 * count * width
        ),
    )(core.reshape(1).astype(jnp.int32), grad_projected, hidden)


def hidden_back_kernel(rows_qkv, group, groups, weights, gp_ref, out_ref, w_ref, sem):
    step = pl.program_id(0)
    block = gp_ref.shape[2]

    @pl.when(step == 0)
    def _():
        fetch(weights, 0, rows_qkv, w_ref, sem, group)

    arrive_in_time(w_ref, sem, group * rows_qkv, range(groups), block, step)
    term = dot_nn(gp_ref[0], w_ref[pl.ds(pl.multiple_of(step * block, block), block), :])

    @pl.when(step == 0)
    def _():
        out_ref[...] = term

    @pl.when(step > 0)
    def _():
        out_ref[...] += term


def hidden_back(grad_projected, weights, rows_qkv):
    _, count, width = grad_projected.shape
    group, groups = grouping(weights, 4)
    return fetching_call(
        functools.partial(hidden_back_kernel, rows_qkv, group, groups),
        [weights],
        name="grad_hidden_one",
        grid=(3,),
        in_specs=[pl.BlockSpec((1, count, width), lambda j, *_: (j, 0, 0))],
        out_specs=[whole((count, width))],
        out_shape=[sds((count, width), F32)],
        scratch=[pltpu.VMEM((3 * width, width), BF16), pltpu.SemaphoreType.DMA((groups,))],
        flops=6 * count * width * width,
        nbytes=2 * 8 * count * width,
    )(grad_projected)[0]


def norm_back_kernel(grad_ref, tok_ref, mid_ref, gain_ref, out_ref, gnorm_ref):
    normed, inverse = normalise(tok_ref[...].astype(F32))
    grad = grad_ref[...]
    part = jnp.sum(grad * normed, axis=0, keepdims=True)
    hat = grad * gain_ref[:1, :]
    first = jnp.mean(hat, axis=-1, keepdims=True)
    second = jnp.mean(hat * normed, axis=-1, keepdims=True)
    out_ref[...] = mid_ref[...] + inverse * (hat - first - normed * second)

    @pl.when(pl.program_id(0) == 0)
    def _():
        gnorm_ref[...] = part

    @pl.when(pl.program_id(0) > 0)
    def _():
        gnorm_ref[...] += part


def norm_back(grad, tokens, mid, gain):
    count, width = tokens.shape
    rows = pl.BlockSpec((128, width), lambda i: (i, 0))
    return call(
        norm_back_kernel,
        name="grad_tokens",
        grid=(count // 128,),
        in_specs=[rows, rows, rows, whole((2, width))],
        out_specs=[rows, whole((1, width))],
        out_shape=[sds((count, width), F32), sds((1, width), F32)],
        flops=20 * count * width,
        nbytes=14 * count * width,
    )(grad, tokens, mid, gain)


Z, Y, X = 4, 2, 2
UP, DOWN, IN_Y, IN_X = (1, 0, 0), (-1, 0, 0), (0, 1, 0), (0, 0, 1)
CROSSED, LEVEL, UPRIGHT = ("planes", "lines"), ("planes", "planes"), ("lines", "lines")
SPREAD = {
    CROSSED: (((UP, IN_X), (DOWN, IN_Y), (UP, IN_Y)), ((IN_Y, UP), (IN_X, DOWN), (IN_X, UP))),
    LEVEL: (((UP, UP), (DOWN, DOWN), (UP, UP)), ((IN_Y, IN_X), (IN_X, IN_Y), (IN_X, IN_Y))),
    UPRIGHT: (((IN_X, IN_Y), (IN_Y, IN_X), (IN_Y, IN_X)), ((UP, UP), (DOWN, DOWN), (UP, UP))),
}
REDUCE = {
    CROSSED: (((IN_X, DOWN), (IN_X, UP), (IN_Y, DOWN)), ((DOWN, IN_Y), (UP, IN_Y), (DOWN, IN_X))),
    LEVEL: (((IN_X, IN_Y), (IN_X, IN_Y), (IN_Y, IN_X)), ((DOWN, DOWN), (UP, UP), (DOWN, DOWN))),
    UPRIGHT: (((DOWN, DOWN), (UP, UP), (DOWN, DOWN)), ((IN_Y, IN_X), (IN_Y, IN_X), (IN_X, IN_Y))),
}


def ident(z, y, x, c):
    return (((z % Z) * Y + y % Y) * X + x % X) * 2 + c


def plus(*moves):
    return tuple(sum(m[i] for m in moves) for i in range(3))


def minus(move):
    return tuple(-m for m in move)


def hop(array, axis, moves):
    pairs = [
        (ident(z, y, x, c), ident(z + m[0], y + m[1], x + m[2], c))
        for z in range(Z) for y in range(Y) for x in range(X)
        for c, m in enumerate(moves)
    ]
    return lax.ppermute(array, axis, pairs)


def swap_cores(array, axis):
    return lax.ppermute(array, axis, [(i, i ^ 1) for i in range(2 * Z * Y * X)])


def place(axis):
    me = lax.axis_index(axis)
    return (me // (2 * Y * X), me // (2 * X) % Y, me // 2 % X), me % 2


def by_core(c, zero, one):
    return jnp.where(c == 0, jnp.stack(zero), jnp.stack(one)).astype(jnp.int32)


def together(*places):
    values = lax.optimization_barrier(tuple(getattr(owner, name) for owner, name in places))
    for (owner, name), value in zip(places, values, strict=True):
        setattr(owner, name, value)


def tie(*values):
    return lax.optimization_barrier(values)


class Spread:
    def __init__(self, shard, axis, route):
        self.shard, self.axis, self.route = shard, axis, route

    def near(self):
        short, _ = SPREAD[self.route]
        self.first = hop(self.shard, self.axis, short[0])
        self.third = hop(self.shard, self.axis, short[1])

    def nearer(self):
        short, _ = SPREAD[self.route]
        second = hop(self.first, self.axis, short[2])
        self.block = jnp.stack([self.shard, self.first, second, self.third])

    def far_one(self):
        self.one = hop(self.block, self.axis, SPREAD[self.route][1][0])

    def far_three(self):
        self.three = hop(self.block, self.axis, SPREAD[self.route][1][1])

    def farther(self):
        _, far = SPREAD[self.route]
        self.two = hop(self.one, self.axis, far[2])

    def swap(self, *names):
        for name in names:
            setattr(self, "other_" + name, swap_cores(getattr(self, name), self.axis))

    def result(self):
        short, far = SPREAD[self.route]
        names = ("block", "one", "two", "three")
        pieces = tuple(getattr(self, kind + name) for kind in ("", "other_") for name in names)
        at, c = place(self.axis)
        froms = []
        for core in range(2):
            s, f = [m[core] for m in short], [m[core] for m in far]
            close = [(0, 0, 0), s[0], plus(s[0], s[2]), s[1]]
            long = [(0, 0, 0), f[0], plus(f[0], f[2]), f[1]]
            froms.append([ident(*plus(at, minus(a), minus(b)), core) for a in long for b in close])
        order = jnp.concatenate([by_core(c, *froms), by_core(c, *froms[::-1])])
        return order, pieces


def lay_out(grad, wide):
    spans = [(b, min(b + wide, grad.shape[2])) for b in range(0, grad.shape[2], wide)]
    return spans, grad.shape[1] * len(spans)


def gather_rows(mine, theirs, more, out, wide):
    at = 0
    for g, t in zip(mine, theirs, strict=True):
        rows = g.shape[1]
        for a, b in lay_out(g, wide)[0]:
            value = g[0, :, a:b].astype(F32) + t[0, :, a:b].astype(F32)
            for m in more:
                value = value + m[at : at + rows, : b - a].astype(F32)
            out[at : at + rows, : b - a] = value.astype(out.dtype)
            if b - a < wide:
                out[at : at + rows, b - a :] = jnp.zeros((rows, wide - (b - a)), out.dtype)
            at += rows


def collect_call(kernel, name, chosen, lines, splits, in_specs, out_specs, out_shape, nbytes, args):
    return pl.pallas_call(
        kernel,
        name=name,
        grid_spec=pltpu.PrefetchScalarGridSpec(
            num_scalar_prefetch=1, grid=(lines, splits), in_specs=in_specs, out_specs=out_specs
        ),
        out_shape=out_shape,
        compiler_params=pltpu.CompilerParams(
            dimension_semantics=("arbitrary", "arbitrary"), vmem_limit_bytes=VMEM_BYTES
        ),
        cost_estimate=pl.CostEstimate(flops=nbytes, transcendentals=0, bytes_accessed=nbytes),
    )(chosen, *args)


def collect(grads, twins, extras, chosen, lines, wide):
    four = chosen.shape[1]
    total = sum(lay_out(g, wide)[1] for g in grads)
    k, number = len(grads) * four, len(lines)
    splits, part = 1, wide

    def kernel(chosen_ref, *refs):
        mine, theirs, more, outs = refs[:k], refs[k : 2 * k], refs[2 * k : -number], refs[-number:]

        def fill(out):
            for i in range(four):
                gather_rows(mine[i::four], theirs[i::four], [m.at[i] for m in more], out.at[i], part)

        for j, out in enumerate(outs):
            pl.when(pl.program_id(0) == j)(functools.partial(fill, out))

    def by_device(g, i):
        def index(j, q, chosen_ref):
            device = chosen_ref[lines[0], i]
            for step, which in enumerate(lines[1:], 1):
                device = jnp.where(j == step, chosen_ref[which, i], device)
            return device, 0, q

        return pl.BlockSpec((1, g.shape[1], g.shape[2] // splits), index)

    def output(step):
        index = lambda j, q, _: (0, 0, jnp.where(j < step, 0, jnp.where(j > step, splits - 1, q)))
        return pl.BlockSpec((four, total, part), index)

    arrived = pl.BlockSpec((four, total, part), lambda j, q, _: (0, 0, q))
    devices = [by_device(g, i) for g in grads for i in range(four)]
    return collect_call(
        kernel,
        "collect_grads",
        chosen,
        number,
        splits,
        devices * 2 + [arrived] * len(extras),
        [output(j) for j in range(number)],
        [sds((four, total, wide), BF16)] * number,
        2 * number * four * total * wide * (3 + len(extras)),
        [*(g for g in (*grads, *twins) for _ in range(four)), *extras],
    )


def collect_last(grads, twins, extras, chosen, wide, direct):
    four = chosen.shape[1]
    total = sum(lay_out(g, wide)[1] for g in grads)
    k = len(grads) * four

    def kernel(chosen_ref, *refs):
        mine, theirs, more, outs = refs[:k], refs[k : 2 * k], refs[2 * k : -four], refs[-four:]
        for i, out in enumerate(outs):
            gather_rows(mine[i::four], theirs[i::four], [m.at[0] for m in more[i::four]], out, wide)

    def pick(shape, line, i):
        return pl.BlockSpec((1, *shape[1:]), lambda j, q, chosen_ref: (chosen_ref[line, i], 0, 0))

    devices = [pick(g.shape, 3, i) for g in grads for i in range(four)]
    places = [pick(m.shape, 4, i) for m in extras for i in range(four)]
    return collect_call(
        kernel,
        "collect_last_grads",
        chosen,
        1,
        1,
        devices * 2 + places,
        [whole((total, wide))] * four,
        [sds((total, wide), kind) for kind in (BF16, BF16, BF16 if direct else F32, F32)],
        2 * four * total * wide * (4 + len(extras)),
        [a for a in (*grads, *twins, *extras) for _ in range(four)],
    )


class Reduce:
    def __init__(self, axis, route, wide, halves=False, direct=False):
        self.axis, self.route, self.wide, self.halves, self.direct = axis, route, wide, halves, direct
        far, short = REDUCE[route]
        at, c = place(axis)
        both = lambda a, b: tuple(plus(i, j) for i, j in zip(a, b, strict=True))
        here = ((0, 0, 0), (0, 0, 0))

        def line(step):
            lists = []
            for core, kind in enumerate(route):
                z, y, x = plus(at, step[core])
                if kind == "planes":
                    lists.append([ident(k, y, x, core) for k in range(Z)])
                else:
                    lists.append([ident(z, j, k, core) for j in range(Y) for k in range(X)])
            return by_core(c, *lists)

        def slot(step):
            places = []
            for core, kind in enumerate(route):
                z, y, x = plus(at, step[core])
                places.append(z % Z if kind == "planes" else y % Y * X + x % X)
            return jnp.where(c == 0, places[0], places[1])

        ends = (both(short[0], short[2]), short[1], short[2], here)
        slots = jnp.stack([slot(step) for step in ends]).astype(jnp.int32)
        lines = [line(step) for step in (both(far[0], far[2]), far[1], far[2])]
        last = []
        for core in range(2):
            last.append([ident(*plus(at, step[core]), core) for step in ends])
        devices = jnp.stack([*lines, by_core(c, *last)])
        self.chosen = jnp.concatenate([devices // 2 if halves else devices, slots[None]])

    def pair(self, grads, go=None):
        self.grads = grads
        self.twins = tuple(swap_cores(g, self.axis) for g in (go if self.halves else grads))

    def pack(self):
        self.one, self.two = collect(self.grads, self.twins, (), self.chosen, (0, 1), self.wide)

    def far(self):
        far, _ = REDUCE[self.route]
        self.one, self.two = hop(self.one, self.axis, far[0]), hop(self.two, self.axis, far[1])

    def repack(self):
        (self.three,) = collect(self.grads, self.twins, (self.one,), self.chosen, (2,), self.wide)

    def farther(self):
        far, _ = REDUCE[self.route]
        self.three = hop(self.three, self.axis, far[2])

    def gather(self):
        self.one, self.two, self.three, self.rest = collect_last(
            self.grads, self.twins, (self.two, self.three), self.chosen, self.wide, self.direct
        )

    def near(self):
        _, short = REDUCE[self.route]
        first = short[0]
        if self.direct:
            first = tuple(plus(a, b) for a, b in zip(short[0], short[2], strict=True))
            self.three = hop(self.three, self.axis, short[2])
        self.one, self.two = hop(self.one, self.axis, first), hop(self.two, self.axis, short[1])

    def nearer(self):
        _, short = REDUCE[self.route]
        self.three = hop((self.three + self.one.astype(F32)).astype(BF16), self.axis, short[2])

    def result(self):
        total = self.rest + self.two.astype(F32) + self.three.astype(F32)
        return total + self.one.astype(F32) if self.direct else total


def tables(segment):
    count = segment.shape[0]
    slots = jnp.arange(count, dtype=jnp.int32)
    order = jnp.where(segment < 0, count, segment)
    starts = jnp.sum((order[None, :] < order[:, None]).astype(jnp.int32), axis=1)
    positions = (slots - starts).astype(F32)
    half = HD // 2
    freqs = THETA ** (-2.0 * jnp.arange(half, dtype=F32) / HD)
    angles = positions[:, None] * freqs[None, :]
    cosine, sine = jnp.cos(angles), jnp.sin(angles)
    cosine = jnp.concatenate([cosine] * 4, axis=1)
    sine = jnp.concatenate([-sine, sine] * 2, axis=1)
    group = jnp.where(segment < 0, -1 - slots, segment)
    return cosine, sine, jnp.broadcast_to(group[:, None], (count, LANES)), group[None, :]


def spans_of(matrix, wide):
    rows, columns = matrix.shape
    count = -(-columns // wide)
    matrix = jnp.pad(matrix, ((0, 0), (0, count * wide - columns)))
    return matrix.reshape(rows, count, wide).transpose(1, 0, 2).reshape(count * rows, wide)


def pad_units(w_ff_out, n, padded):
    units = w_ff_out.reshape(w_ff_out.shape[0], n // 2, -1)
    return jnp.pad(units, ((0, 0), (0, 0), (0, padded - units.shape[2]))).reshape(w_ff_out.shape[0], -1)


def drop_units(g_ff, n, padded, rows_in):
    return g_ff.reshape(-1, n // 2, padded)[:, :, :rows_in].reshape(-1, n // 2 * rows_in)


def sum_norms(n, axis, g_one, g_two):
    g_norms = jnp.stack([g_one.reshape(n, -1), g_two.reshape(n, -1)], axis=1)
    g_norms = jnp.sum(lax.all_to_all(g_norms, axis, 0, 0, tiled=True), axis=0)
    return g_norms


def by_collectives(tokens, cotangent, segment, w_qkv, w_attn_out, w_in, w_ff_out, gains, w_in_rows, padded, axis):
    n = lax.axis_size(axis)
    width = tokens.shape[1]
    units = n // 2 * padded
    pairs = width // LANES
    gather = lambda shard: lax.all_gather(shard, axis, axis=0, tiled=True)
    at_once = lambda matrix: (jnp.zeros((1,), jnp.int32), (matrix[None],))
    w_qkv, w_ff = at_once(gather(w_qkv)), at_once(spans_of(gather(pad_units(w_ff_out, n, padded)), width))
    w_in = at_once(jnp.concatenate([gather(w_in), gather(w_attn_out)]))
    gains = gather(gains.reshape(1, 2, -1)).astype(F32).transpose(1, 0, 2).reshape(2, width)
    cosine, sine, seg_column, seg_row = tables(segment)
    qkv, hidden_one, gains = project(tokens, cosine, sine, w_qkv, 3 * width, gains)
    attn_out, lse = attend(qkv, seg_column, seg_row, width, 0, pairs)
    resid, mixed, mid, grad_heads, g_out, g_two, g_in, g_ff = ffn(
        tokens, attn_out, cotangent, gains, w_in, w_ff, units, 2 * units, width, width
    )
    output = ffn_out(resid, mixed, w_ff, width)
    grad_projected = attend_back(qkv, attn_out, grad_heads, lse, seg_column, seg_row, cosine, sine, 0, pairs)
    g_qkv = project_grad(grad_projected, hidden_one)
    grad_tokens, g_one = norm_back(hidden_back(grad_projected, w_qkv, 3 * width), tokens, mid, gains)
    scatter = lambda grad: lax.psum_scatter(grad, axis, scatter_dimension=0, tiled=True).astype(F32)
    g_in = g_in.reshape(2 * units, width)
    g_ff = drop_units(scatter(g_ff), n, padded, w_in_rows)
    return output, grad_tokens, scatter(g_qkv), scatter(g_out), scatter(g_in), g_ff, g_one, g_two


class Box:
    pass


def by_links(tokens, cotangent, segment, w_qkv, w_attn_out, w_in, w_ff_out, gains, w_in_rows, padded, axis):
    n = lax.axis_size(axis)
    width = tokens.shape[1]
    units = n // 2 * padded
    pairs = width // LANES
    rows_qkv, rows_out, rows_ff = w_qkv.shape[0], w_attn_out.shape[0], w_ff_out.shape[0]
    v = Box()
    gain_rows = jnp.pad(gains[None], ((0, 7), (0, width - gains.shape[0])))
    s_qkv = Spread(jnp.concatenate([w_qkv, gain_rows]), axis, LEVEL)
    s_in = Spread(jnp.concatenate([w_in, w_attn_out]), axis, LEVEL)
    s_ff = Spread(spans_of(pad_units(w_ff_out, n, padded), width), axis, UPRIGHT)
    r_ff = Reduce(axis, UPRIGHT, width, direct=True)
    r_in = Reduce(axis, LEVEL, width)
    r_qkv = Reduce(axis, LEVEL, width, halves=True, direct=True)
    v.cosine, v.sine, v.seg_column, v.seg_row = tables(segment)

    s_qkv.near()
    s_ff.near()
    s_qkv.nearer()
    s_ff.nearer()
    together((s_qkv, "block"), (s_in, "shard"), (s_ff, "block"), *((v, k) for k in vars(v)))
    s_qkv.far_one()
    s_qkv.far_three()
    s_in.near()
    s_qkv.swap("block")
    together((s_qkv, "one"), (s_qkv, "three"), (s_qkv, "other_block"), (s_in, "first"), (s_in, "third"))
    s_qkv.farther()
    s_in.nearer()
    s_qkv.swap("one", "three")
    together((s_qkv, "two"), (s_qkv, "other_three"), (s_qkv, "other_one"), (s_in, "block"), (s_ff, "block"))
    s_in.far_one()
    s_in.far_three()
    s_ff.far_one()
    s_qkv.swap("two")
    s_ff.swap("block")
    w_qkv = s_qkv.result()
    v.qkv, v.hidden_one, v.gains = project(tokens, v.cosine, v.sine, w_qkv, rows_qkv)
    together((v, "qkv"), (s_ff, "one"), (s_ff, "block"), (s_in, "block"), (s_ff, "other_block"))
    s_ff.far_three()
    s_ff.swap("one")
    s_in.swap("block")
    attend_some = lambda first, number, done=None: attend(v.qkv, v.seg_column, v.seg_row, width, first, number, done)
    v.done = attend_some(0, pairs // 2)
    together(
        (v, "done"), (s_in, "one"), (s_in, "three"), (s_ff, "one"), (s_ff, "three"),
        (s_in, "other_block"), (s_ff, "other_one"),
    )
    s_in.farther()
    s_ff.farther()
    s_in.swap("one", "three")
    s_ff.swap("three")
    v.done = attend_some(pairs // 2, pairs // 2, v.done)
    together(
        (v, "done"), (s_in, "two"), (s_ff, "two"), (s_in, "other_one"), (s_in, "other_three"), (s_ff, "other_three")
    )
    s_in.swap("two")
    s_ff.swap("two")
    attn_out, lse = v.done
    w_in, w_ff = s_in.result(), s_ff.result()
    rows_of = lambda grad: grad.reshape(n, -1, grad.shape[-1])
    resid, v.mixed, mid, v.heads, v.g_out, g_two, v.g_in, g_ff = ffn(
        tokens, attn_out, cotangent, v.gains, w_in, w_ff, units, padded, rows_out, rows_ff
    )

    def back(first, number):
        v.some = attend_back(
            v.qkv, attn_out, v.heads, lse, v.seg_column, v.seg_row, v.cosine, v.sine,
            first * pairs // 8, number * pairs // 8, v.some,
        )

    v.some = None
    r_ff.pair((rows_of(g_ff),))
    back(0, 1)
    together((v, "some"), (r_ff, "twins"), (v, "g_in"), (v, "g_out"))
    r_in.pair((rows_of(v.g_in), rows_of(v.g_out)))
    r_ff.pack()
    together((v, "some"), (r_ff, "one"), (r_ff, "two"))
    r_ff.far()
    back(1, 2)
    together((v, "some"), (r_in, "twins"))
    r_in.pack()
    together((v, "some"), (r_in, "one"), (r_in, "two"))
    r_in.far()
    back(3, 2)
    together((v, "some"), (r_ff, "one"), (r_ff, "two"))
    r_ff.repack()
    together((v, "some"), (r_ff, "three"))
    r_ff.farther()
    back(5, 2)
    together((v, "some"), (r_in, "one"), (r_in, "two"), (r_ff, "three"))
    r_in.repack()
    together((v, "some"), (r_in, "three"), (r_ff, "three"))
    r_in.farther()
    back(7, 1)
    together((v, "some"), (r_ff, "three"))
    r_ff.gather()
    together((v, "some"), (r_ff, "one"), (r_ff, "two"))
    r_ff.near()
    v.stay, v.go = project_grad_halves(v.some, v.hidden_one, rows_qkv, place(axis)[1])
    together((v, "some"), (v, "stay"), (v, "go"), (r_in, "three"), (r_ff, "one"), (r_ff, "two"), (r_ff, "three"))
    half_of = lambda grad: grad.reshape(n // 2, -1, width)
    r_qkv.pair((half_of(v.stay),), (half_of(v.go),))
    r_in.gather()
    together((v, "some"), (r_qkv, "twins"), (r_in, "one"), (r_in, "two"))
    r_in.near()
    r_qkv.pack()
    together((v, "some"), (r_qkv, "one"), (r_qkv, "two"))
    r_qkv.far()
    v.hidden = hidden_back(v.some, w_qkv, rows_qkv)
    together((v, "hidden"), (r_ff, "one"), (r_ff, "two"), (r_ff, "three"))
    g_ff = r_ff.result().reshape(-1, rows_ff, width).transpose(1, 0, 2).reshape(rows_ff, -1)[:, :units]
    v.g_ff = drop_units(g_ff, n, padded, w_in_rows)
    together((v, "g_ff"), (v, "hidden"), (r_qkv, "one"), (r_qkv, "two"), (r_in, "one"), (r_in, "two"))
    r_qkv.repack()
    together((v, "hidden"), (r_qkv, "three"))
    r_qkv.farther()
    r_in.nearer()
    v.grad_tokens, v.g_one = norm_back(v.hidden, tokens, mid, v.gains)
    together((v, "grad_tokens"), (v, "g_one"), (r_qkv, "three"), (r_in, "three"))
    r_qkv.gather()
    together((v, "mixed"), (r_qkv, "one"), (r_qkv, "two"), (r_qkv, "three"), (r_qkv, "rest"))
    r_qkv.near()
    v.output = ffn_out(resid, v.mixed, w_ff, rows_ff)
    together((v, "output"), (r_qkv, "one"), (r_qkv, "two"), (r_qkv, "three"), (r_in, "three"))
    rest = r_in.result()
    return v.output, v.grad_tokens, r_qkv.result(), rest[padded:], rest[:padded], v.g_ff, v.g_one, g_two


def body(tokens, cotangent, segment, w_qkv, w_attn_out, w_in, w_ff_out, norm_one, norm_two):
    axis = "fsdp"
    n = lax.axis_size(axis)
    rows_in = w_in.shape[0]
    padded = -(-rows_in // 16) * 16
    w_in = jnp.pad(w_in, ((0, padded - rows_in), (0, 0)))
    scales = norm_one.shape[0]
    aligned = not (any(w.shape[0] % 16 for w in (w_qkv, w_attn_out, w_ff_out)) or scales & (scales - 1))
    way = by_links if aligned and n == 2 * Z * Y * X else by_collectives
    output, grad_tokens, g_qkv, g_out, g_in, g_ff, g_one, g_two = way(
        tokens, cotangent, segment, w_qkv, w_attn_out, w_in, w_ff_out, jnp.concatenate([norm_one, norm_two]), rows_in, padded, axis
    )
    g_norms = sum_norms(n, axis, g_one, g_two)
    g_in = g_in[:rows_in]
    return (output, grad_tokens, g_qkv, g_out, g_in, g_ff, g_norms[0], g_norms[1])


def solution(mesh):
    rows, flat = P("fsdp", None), P("fsdp")
    return jax.shard_map(
        body,
        mesh=mesh,
        in_specs=(rows, rows, flat, rows, rows, rows, rows, flat, flat),
        out_specs=(rows, rows, rows, rows, rows, rows, flat, flat),
        check_vma=False,
    )
```

```python
import functools
import math

import jax
import jax.numpy as jnp
from jax import lax
from jax.experimental import pallas as pl
from jax.experimental.pallas import tpu as pltpu
from jax.sharding import PartitionSpec as P

HD = 64
EPS = 1e-05
THETA = 160000.0
NEG = -1e30
LANES = 128
F32 = jnp.float32
BF16 = jnp.bfloat16
VMEM_BYTES = 62 << 20


def dot_nt(left, right):
    return lax.dot_general(left, right, (((1,), (1,)), ((), ())), preferred_element_type=F32)


def dot_nn(left, right):
    return lax.dot_general(left, right, (((1,), (0,)), ((), ())), preferred_element_type=F32)


def dot_tn(left, right):
    return lax.dot_general(left, right, (((0,), (0,)), ((), ())), preferred_element_type=F32)


def call(kernel, *, name, grid, in_specs, out_specs, out_shape, scratch=(), flops=0, nbytes=0, aliases=None):
    return pl.pallas_call(
        kernel,
        name=name,
        grid=grid,
        in_specs=in_specs,
        out_specs=out_specs,
        out_shape=out_shape,
        scratch_shapes=list(scratch),
        input_output_aliases=aliases or {},
        compiler_params=pltpu.CompilerParams(
            dimension_semantics=("arbitrary",) * len(grid), vmem_limit_bytes=VMEM_BYTES
        ),
        cost_estimate=pl.CostEstimate(flops=flops, transcendentals=0, bytes_accessed=nbytes),
    )


def sds(shape, dtype):
    return jax.ShapeDtypeStruct(shape, dtype)


def whole(shape, once=False):
    zeros = (0,) * len(shape)
    mode = dict(pipeline_mode=pl.Buffered(1)) if once else {}
    return pl.BlockSpec(shape, lambda *_: zeros, **mode)


def normalise(field):
    centre = jnp.mean(field, axis=-1, keepdims=True)
    centered = field - centre
    variance = jnp.mean(centered * centered, axis=-1, keepdims=True)
    inverse = lax.rsqrt(variance + EPS)
    return centered * inverse, inverse


def minus_row(field, row):
    return (field.reshape(-1, *row.shape) - row[None]).reshape(field.shape)


def swap_halves(field):
    lane = lax.broadcasted_iota(jnp.int32, field.shape, 1)
    first = (lane & (HD - 1)) < HD // 2
    return jnp.where(
        first, pltpu.roll(field, LANES - HD // 2, 1), pltpu.roll(field, HD // 2, 1)
    )


def fetch(weights, at, rows, target, sem, group=None, columns=slice(None)):
    order_ref, pieces = weights
    i = 0
    for piece in pieces:
        for slot in range(piece.shape[0]):
            device = order_ref[i]
            start = pl.multiple_of(device * rows, rows)
            pltpu.make_async_copy(
                piece.at[slot, pl.ds(at, rows), columns],
                target.at[pl.ds(start, rows), columns],
                sem if group is None else sem.at[device // group],
            ).start()
            i += 1


def arrive(target, sem):
    pltpu.make_async_copy(target, target, sem).wait()


def spans_of(columns, wide):
    return [slice(a, min(a + wide, columns)) for a in range(0, columns, wide)]


def grouping(weights, group):
    devices = weights[0].shape[0]
    return (group, devices // group) if devices % group == 0 else (devices, 1)


def arrive_in_time(target, sem, rows, groups, block, step):
    for g in groups:
        @pl.when(step == (g - groups[0]) * rows // block)
        def _(g=g):
            arrive(target.at[pl.ds(g * rows, rows), :], sem.at[g])


def fetching_call(
    kernel, weights, *, name, grid, in_specs, out_specs, out_shape, scratch=(), flops=0, nbytes=0
):
    number = len(weights)

    def run(*refs):
        orders, rest, sets = refs[:number], refs[number:], []
        for order, (_, pieces) in zip(orders, weights, strict=True):
            sets.append((order, rest[: len(pieces)]))
            rest = rest[len(pieces) :]
        kernel(*sets, *rest)

    pieces = [piece for _, some in weights for piece in some]
    made = pl.pallas_call(
        run,
        name=name,
        grid_spec=pltpu.PrefetchScalarGridSpec(
            num_scalar_prefetch=number,
            grid=grid,
            in_specs=[pl.BlockSpec(memory_space=pl.ANY)] * len(pieces) + in_specs,
            out_specs=out_specs,
            scratch_shapes=list(scratch),
        ),
        out_shape=out_shape,
        compiler_params=pltpu.CompilerParams(
            dimension_semantics=("arbitrary",) * len(grid), vmem_limit_bytes=VMEM_BYTES
        ),
        cost_estimate=pl.CostEstimate(flops=flops, transcendentals=0, bytes_accessed=nbytes),
    )
    return lambda *args: made(*[order for order, _ in weights], *pieces, *args)


def unpack_gains(rows_ref, number, out_ref):
    total, width = rows_ref.shape
    devices = total // 8
    owner = lax.broadcasted_iota(jnp.int32, (devices, total), 0)
    row = lax.broadcasted_iota(jnp.int32, (devices, total), 1)
    found = dot_nn((row == owner * 8).astype(BF16), rows_ref[:, :LANES]).astype(BF16)
    place_in = lax.broadcasted_iota(jnp.int32, (LANES, width), 0)
    lane = lax.broadcasted_iota(jnp.int32, (LANES, width), 1) & (number - 1)
    first = lax.broadcasted_iota(jnp.int32, (devices, width), 0) * number
    column = lax.broadcasted_iota(jnp.int32, (devices, width), 1)
    mine = (column >= first) & (column < first + number)
    for which in range(2):
        tiled = dot_nn(found, (place_in == lane + which * number).astype(BF16))
        out_ref[which : which + 1, :] = jnp.sum(jnp.where(mine, tiled, 0.0), axis=0, keepdims=True)


def project_kernel(rope_blocks, query_blocks, rows, given, group, groups, weights, tok_ref, cos_ref, sin_ref, *refs):
    if given:
        gains_in, out_ref, hid_ref, gains_ref, w_ref, sem = refs
    else:
        out_ref, hid_ref, gains_ref, w_ref, sem, rows_ref, rows_sem = refs
    step = pl.program_id(0)
    block = out_ref.shape[1]

    @pl.when(step == 0)
    def _():
        if given:
            gains_ref[...] = gains_in[...]
        else:
            fetch(weights, rows, 8, rows_ref, rows_sem)
        fetch(weights, 0, rows, w_ref, sem, group)
        if not given:
            arrive(rows_ref, rows_sem)
            unpack_gains(rows_ref, w_ref.shape[1] * 8 // rows_ref.shape[0], gains_ref)
        normed, _ = normalise(tok_ref[...].astype(F32))
        hid_ref[...] = (normed * gains_ref[:1, :]).astype(BF16)

    arrive_in_time(w_ref, sem, group * rows, range(groups), block, step)
    w_block = w_ref[pl.ds(pl.multiple_of(step * block, block), block), :]
    some = 256

    @pl.when(step < rope_blocks)
    def _():
        scale = jnp.where(step < query_blocks, 1.0 / math.sqrt(HD), 1.0).astype(F32)
        for r in range(hid_ref.shape[0] // some):
            at = slice(r * some, (r + 1) * some)
            acc = dot_nt(hid_ref[at, :], w_block)
            cosine, sine = cos_ref[at, :] * scale, sin_ref[at, :] * scale
            for s in range(block // LANES):
                part = acc[:, s * LANES : (s + 1) * LANES]
                out_ref[at, s * LANES : (s + 1) * LANES] = (part * cosine + swap_halves(part) * sine).astype(BF16)

    @pl.when(step >= rope_blocks)
    def _():
        for r in range(hid_ref.shape[0] // some):
            at = slice(r * some, (r + 1) * some)
            out_ref[at, :] = dot_nt(hid_ref[at, :], w_block).astype(BF16)


def project(tokens, cosine, sine, weights, rows, gains=None):
    count, width = tokens.shape
    total = 3 * width
    block = width
    given = gains is not None
    group, groups = grouping(weights, 4)
    own = [] if given else [pltpu.VMEM((weights[0].shape[0] * 8, width), BF16), pltpu.SemaphoreType.DMA]
    return fetching_call(
        functools.partial(project_kernel, 2 * width // block, width // block, rows, given, group, groups),
        [weights],
        name="norm_project",
        grid=(total // block,),
        in_specs=[whole((count, width)), whole((count, LANES)), whole((count, LANES))]
        + [whole((2, width))] * given,
        out_specs=[
            pl.BlockSpec((count, block), lambda j, *_: (0, j)),
            whole((count, width)),
            whole((2, width)),
        ],
        out_shape=[sds((count, total), BF16), sds((count, width), BF16), sds((2, width), F32)],
        scratch=[pltpu.VMEM((total, width), BF16), pltpu.SemaphoreType.DMA((groups,))] + own,
        flops=2 * count * width * total,
        nbytes=2 * (2 * count * width + total * width + total * count),
    )(tokens, cosine, sine, *([gains] if given else []))


def attend_kernel(q_ref, k_ref, v_ref, segc_ref, segr_ref, out_ref, lse_ref, vt_ref, ot_ref):
    count = q_ref.shape[0]
    vt_ref[...] = v_ref[...].T
    keys, query = k_ref[...], q_ref[...]
    lane = lax.broadcasted_iota(jnp.int32, query.shape, 1)
    allowed = jnp.concatenate([segc_ref[...]] * (count // LANES), axis=1) == segr_ref[...]
    for h in range(2):
        picked = jnp.where((lane >= h * HD) & (lane < (h + 1) * HD), query, jnp.zeros_like(query))
        scores = jnp.where(allowed, dot_nt(keys, picked), NEG)
        top = jnp.max(scores, axis=0, keepdims=True)
        powers = jnp.exp(scores - top)
        total = jnp.sum(powers, axis=0, keepdims=True)
        lse_ref[0, h : h + 1, :] = top + jnp.log(total)
        ot_ref[h * HD : (h + 1) * HD, :] = dot_nn(vt_ref[h * HD : (h + 1) * HD, :], powers.astype(BF16)) / total
    out_ref[...] = ot_ref[...].T.astype(BF16)


def attend(qkv, seg_column, seg_row, width, first, number, before=None):
    count = qkv.shape[0]
    pairs = width // LANES
    kept = () if before is None else tuple(before)

    def kernel(*refs):
        attend_kernel(*refs[:5], *refs[5 + len(kept) :])

    tall = lambda offset: pl.BlockSpec((count, LANES), lambda p: (0, offset + first + p))
    return call(
        kernel,
        name="attend",
        grid=(number,),
        in_specs=[tall(0), tall(pairs), tall(2 * pairs), whole((count, LANES)), whole((1, count))]
        + [pl.BlockSpec(memory_space=pl.ANY)] * len(kept),
        out_specs=[tall(0), pl.BlockSpec((1, 2, count), lambda p: (first + p, 0, 0))],
        out_shape=[sds((count, width), BF16), sds((pairs, 2, count), F32)],
        scratch=[pltpu.VMEM((LANES, count), BF16), pltpu.VMEM((LANES, count), F32)],
        flops=16 * count * count * LANES * number,
        nbytes=2 * 4 * count * LANES * number,
        aliases={5: 0, 6: 1} if kept else None,
    )(qkv, qkv, qkv, seg_column, seg_row, *kept)


def attend_back_kernel(
    chunk, q_ref, k_ref, v_ref, o_ref, g_ref, lse_ref, segc_ref, segr_ref, cos_ref, sin_ref,
    out_ref, kt_ref, dk_ref, dv_ref, dqt_ref, delta_ref, total_ref,
):
    count = q_ref.shape[0]
    kt_ref[...] = k_ref[...].T
    keys, values = k_ref[...], v_ref[...]
    product = (g_ref[...].astype(F32) * o_ref[...].astype(F32)).T
    for h in range(2):
        row = jnp.sum(product[h * HD : (h + 1) * HD, :], axis=0, keepdims=True)
        delta_ref[h] = jnp.broadcast_to(row, (8, count))
        total_ref[h] = jnp.broadcast_to(lse_ref[0, h : h + 1, :], (8, count))
    lane = lax.broadcasted_iota(jnp.int32, (chunk, LANES), 1)
    upper = lax.broadcasted_iota(jnp.int32, (LANES, chunk), 0) < HD
    for c in range(count // chunk):
        at = slice(c * chunk, (c + 1) * chunk)
        query, grad = q_ref[at, :], g_ref[at, :]
        allowed = jnp.concatenate([segc_ref[...]] * (chunk // LANES), axis=1) == segr_ref[:, at]
        grads = []
        for h in range(2):
            mine = (lane >= h * HD) & (lane < (h + 1) * HD)
            query_h = jnp.where(mine, query, jnp.zeros_like(query))
            grad_h = jnp.where(mine, grad, jnp.zeros_like(grad))
            scores = jnp.where(allowed, dot_nt(keys, query_h), NEG)
            weights = jnp.exp(minus_row(scores, total_ref[h, :, at]))
            grad_value = dot_nn(weights.astype(BF16), grad_h)
            spread = minus_row(dot_nt(values, grad_h), delta_ref[h, :, at])
            grad_scores = (weights * spread).astype(BF16)
            grads.append((dot_nn(grad_scores, query_h), grad_value, dot_nn(kt_ref[...], grad_scores)))
        (key_0, value_0, query_0), (key_1, value_1, query_1) = grads
        dqt_ref[:, at] = jnp.where(upper, query_0, query_1)
        if c == 0:
            dk_ref[...] = key_0 + key_1
            dv_ref[...] = value_0 + value_1
        else:
            dk_ref[...] += key_0 + key_1
            dv_ref[...] += value_0 + value_1

    cosine, sine = cos_ref[...], sin_ref[...]
    grad_query = dqt_ref[...].T * (1.0 / math.sqrt(HD))
    out_ref[0] = (grad_query * cosine - swap_halves(grad_query) * sine).astype(BF16)
    grad_key = dk_ref[...]
    out_ref[1] = (grad_key * cosine - swap_halves(grad_key) * sine).astype(BF16)
    out_ref[2] = dv_ref[...].astype(BF16)


def attend_back(qkv, attn_out, grad_heads, lse, seg_column, seg_row, cosine, sine, first, number, before=None):
    count, width = attn_out.shape
    pairs = width // LANES
    chunk = 256
    kept = () if before is None else (before,)

    def kernel(*refs):
        attend_back_kernel(chunk, *refs[:10], *refs[10 + len(kept) :])

    tall = lambda offset: pl.BlockSpec((count, LANES), lambda p: (0, offset + first + p))
    return call(
        kernel,
        name="attend_back",
        grid=(number,),
        in_specs=[
            tall(0),
            tall(pairs),
            tall(2 * pairs),
            tall(0),
            tall(0),
            pl.BlockSpec((1, 2, count), lambda p: (first + p, 0, 0)),
            whole((count, LANES)),
            whole((1, count)),
            whole((count, LANES)),
            whole((count, LANES)),
        ]
        + [pl.BlockSpec(memory_space=pl.ANY)] * len(kept),
        out_specs=pl.BlockSpec((3, count, LANES), lambda p: (0, 0, first + p)),
        out_shape=sds((3, count, width), BF16),
        scratch=[
            pltpu.VMEM((LANES, count), BF16),
            pltpu.VMEM((count, LANES), F32),
            pltpu.VMEM((count, LANES), F32),
            pltpu.VMEM((LANES, count), F32),
            pltpu.VMEM((2, 8, count), F32),
            pltpu.VMEM((2, 8, count), F32),
        ],
        flops=40 * count * count * LANES * number,
        nbytes=2 * 8 * count * LANES * number,
        aliases={10: 0} if kept else None,
    )(qkv, qkv, qkv, attn_out, grad_heads, lse, seg_column, seg_row, cosine, sine, *kept)


def ffn_kernel(
    rows_in, rows_out, rows_ff, group, groups, weights_in, weights_ff,
    tok_ref, attn_ref, cot_ref, gain_ref,
    resid_ref, mixed_ref, mid_ref, heads_ref, g_attn_ref, gnorm_ref, g_in_ref, g_out_ref,
    hid_ref, cot_t_ref, w_attn_ref, w_in_ref, w_ff_ref, sem_attn, sem_in, sem_ff,
):
    step = pl.program_id(0)
    count = resid_ref.shape[0]
    block = g_out_ref.shape[1]
    units = w_in_ref.shape[0] // 2
    width = hid_ref.shape[1]
    spans = spans_of(w_ff_ref.shape[1], width)
    some = 256

    @pl.when(step == 0)
    def _():
        fetch(weights_in, rows_in, rows_out, w_attn_ref, sem_attn)
        fetch(weights_ff, 0, rows_ff, w_ff_ref, sem_ff.at[0], columns=spans[0])
        fetch(weights_in, 0, rows_in, w_in_ref, sem_in, group)
        for b, span in enumerate(spans[1:], 1):
            fetch(weights_ff, 0, rows_ff, w_ff_ref, sem_ff.at[b], columns=span)
        cot_t_ref[...] = cot_ref[...].T
        mid_ref[...] = jnp.zeros_like(mid_ref)
        arrive(w_attn_ref, sem_attn)
        for i in range(count // some):
            at = slice(i * some, (i + 1) * some)
            resid = tok_ref[at, :].astype(F32) + dot_nt(attn_ref[at, :], w_attn_ref[...])
            resid_ref[at, :] = resid
            normed, _ = normalise(resid)
            hid_ref[at, :] = (normed * gain_ref[1:, :]).astype(BF16)

    half = max(groups // 2, 1)
    for some_groups in (range(half), range(half, groups)):
        if some_groups:
            arrive_in_time(w_in_ref, sem_in, group * rows_in, some_groups, block, step)
    for b, span in enumerate(spans):
        pl.when(step == span.start // block)(functools.partial(arrive, w_ff_ref.at[:, span], sem_ff.at[b]))
    hidden = hid_ref[...]
    w_pre = w_in_ref[pl.ds(pl.multiple_of(step * block, block), block), :]
    w_gate = w_in_ref[pl.ds(pl.multiple_of(units + step * block, block), block), :]
    w_out = w_ff_ref[:, pl.ds(pl.multiple_of(step * block, block), block)]
    pre = dot_nt(hidden, w_pre)
    gate = dot_nt(hidden, w_gate)
    grad_mixed = dot_nn(cot_ref[...], w_out)
    cdf = 0.5 * (1.0 + lax.erf(pre * 0.7071067811865476))
    density = jnp.exp(-0.5 * pre * pre) * 0.3989422804014327
    gelu = pre * cdf
    mixed = (gelu * gate).astype(BF16)
    mixed_ref[...] = mixed
    g_out_ref[...] = dot_nn(cot_t_ref[...], mixed).astype(BF16)
    grad_pre = (grad_mixed * gate * (cdf + pre * density)).astype(BF16)
    grad_gate = (grad_mixed * gelu).astype(BF16)
    g_in_ref[0] = dot_tn(grad_pre, hidden).astype(BF16)
    g_in_ref[1] = dot_tn(grad_gate, hidden).astype(BF16)
    mid_ref[...] += dot_nn(grad_pre, w_pre) + dot_nn(grad_gate, w_gate)

    @pl.when(step == pl.num_programs(0) - 1)
    def _():
        gnorm = jnp.zeros_like(gnorm_ref)
        for i in range(count // some):
            at = slice(i * some, (i + 1) * some)
            resid = resid_ref[at, :]
            normed, inverse = normalise(resid)
            grad = mid_ref[at, :]
            gnorm += jnp.sum(grad * normed, axis=0, keepdims=True)
            hat = grad * gain_ref[1:, :]
            first = jnp.mean(hat, axis=-1, keepdims=True)
            second = jnp.mean(hat * normed, axis=-1, keepdims=True)
            mid = cot_ref[at, :].astype(F32) + inverse * (hat - first - normed * second)
            mid_ref[at, :] = mid
            low = mid.astype(BF16)
            cot_t_ref[at, :] = low
            heads_ref[at, :] = dot_nn(low, w_attn_ref[...]).astype(BF16)
        gnorm_ref[...] = gnorm
        for i in range(width // some):
            at = slice(i * some, (i + 1) * some)
            g_attn_ref[at, :] = dot_tn(cot_t_ref[:, at], attn_ref[...]).astype(BF16)


def ffn(tokens, attn_out, cotangent, gains, w_in, w_ff, units, rows_in, rows_out, rows_ff):
    count, width = tokens.shape
    block = 256
    group, groups = grouping(w_in, 2)
    once = whole((count, width), once=True)
    return fetching_call(
        functools.partial(ffn_kernel, rows_in, rows_out, rows_ff, group, groups),
        [w_in, w_ff],
        name="ffn_forward_backward",
        grid=(units // block,),
        in_specs=[once, once, once, whole((2, width))],
        out_specs=[
            once,
            pl.BlockSpec((count, block), lambda j, *_: (0, j)),
            once,
            once,
            whole((width, width), once=True),
            whole((1, width)),
            pl.BlockSpec((2, block, width), lambda j, *_: (0, j, 0)),
            pl.BlockSpec((width, block), lambda j, *_: (0, j)),
        ],
        out_shape=[
            sds((count, width), F32),
            sds((count, units), BF16),
            sds((count, width), F32),
            sds((count, width), BF16),
            sds((width, width), BF16),
            sds((1, width), F32),
            sds((2, units, width), BF16),
            sds((width, units), BF16),
        ],
        scratch=[
            pltpu.VMEM((count, width), BF16),
            pltpu.VMEM((width, count), BF16),
            pltpu.VMEM((width, width), BF16),
            pltpu.VMEM((2 * units, width), BF16),
            pltpu.VMEM((width, units), BF16),
            pltpu.SemaphoreType.DMA,
            pltpu.SemaphoreType.DMA((groups,)),
            pltpu.SemaphoreType.DMA((len(spans_of(units, width)),)),
        ],
        flops=16 * count * width * units,
        nbytes=2 * (10 * count * width + 6 * units * width),
    )(tokens, attn_out, cotangent, gains)


def ffn_out_kernel(rows_ff, weights, resid_ref, mixed_ref, out_ref, w_ref, sem):
    spans = spans_of(mixed_ref.shape[1], out_ref.shape[1])

    @pl.when(pl.program_id(0) == 0)
    def _():
        for b, span in enumerate(spans):
            fetch(weights, 0, rows_ff, w_ref, sem.at[b], columns=span)

    out = resid_ref[...]
    for b, span in enumerate(spans):
        pl.when(pl.program_id(0) == 0)(functools.partial(arrive, w_ref.at[:, span], sem.at[b]))
        out = out + dot_nt(mixed_ref[:, span], w_ref[:, span])
    out_ref[...] = out.astype(BF16)


def ffn_out(resid, mixed, weights, rows_ff):
    count, width = resid.shape
    units = mixed.shape[1]
    rows = lambda columns: pl.BlockSpec((256, columns), lambda i, *_: (i, 0))
    return fetching_call(
        functools.partial(ffn_out_kernel, rows_ff),
        [weights],
        name="ffn_output",
        grid=(count // 256,),
        in_specs=[rows(width), rows(units)],
        out_specs=[rows(width)],
        out_shape=[sds((count, width), BF16)],
        scratch=[pltpu.VMEM((width, units), BF16), pltpu.SemaphoreType.DMA((len(spans_of(units, width)),))],
        flops=2 * count * width * units,
        nbytes=2 * (count * units + 3 * count * width + units * width),
    )(resid, mixed)[0]


def project_grad_kernel(gp_ref, hid_ref, out_ref):
    out_ref[...] = dot_tn(gp_ref[0], hid_ref[...]).astype(BF16)


def project_grad(grad_projected, hidden):
    count, width = hidden.shape
    block = 512
    per = width // block
    return call(
        project_grad_kernel,
        name="grad_qkv",
        grid=(3 * per,),
        in_specs=[pl.BlockSpec((1, count, block), lambda j: (j // per, 0, j % per)), whole((count, width))],
        out_specs=pl.BlockSpec((block, width), lambda j: (j, 0)),
        out_shape=sds((3 * width, width), BF16),
        flops=6 * count * width * width,
        nbytes=2 * 7 * count * width,
    )(grad_projected, hidden)


def project_grad_halves_kernel(rows, core_ref, gp_ref, hid_ref, stay_ref, go_ref, acc_ref):
    step = pl.program_id(0)
    block, width = acc_ref.shape

    def product(k):
        parts, at = [], k * block
        while at < (k + 1) * block:
            stop = min((k + 1) * block, (at // width + 1) * width)
            parts.append(gp_ref[at // width, :, at % width : at % width + stop - at])
            at = stop
        acc_ref[...] = dot_tn(jnp.concatenate(parts, axis=1), hid_ref[...])

    for k in range(gp_ref.shape[0] * width // block):
        pl.when(step == k)(functools.partial(product, k))
    mine = core_ref[0]
    for pair in range(block // (2 * rows)):
        to = slice(pair * rows, (pair + 1) * rows)
        for out, core in ((stay_ref, mine), (go_ref, 1 - mine)):
            start = pl.multiple_of((2 * pair + core) * rows, rows)
            out[to, :] = acc_ref[pl.ds(start, rows), :].astype(BF16)


def project_grad_halves(grad_projected, hidden, rows, core):
    count, width = hidden.shape
    total = 3 * width
    block = next(b for b in range(LANES, total + 1, LANES) if b % (2 * rows) == 0 and total % b == 0)
    half = pl.BlockSpec((block // 2, width), lambda j, _: (j, 0))
    return pl.pallas_call(
        functools.partial(project_grad_halves_kernel, rows),
        name="grad_qkv",
        grid_spec=pltpu.PrefetchScalarGridSpec(
            num_scalar_prefetch=1,
            grid=(total // block,),
            in_specs=[whole(grad_projected.shape, once=True), whole((count, width))],
            out_specs=[half, half],
            scratch_shapes=[pltpu.VMEM((block, width), F32)],
        ),
        out_shape=[sds((total // 2, width), BF16)] * 2,
        compiler_params=pltpu.CompilerParams(
            dimension_semantics=("arbitrary",), vmem_limit_bytes=VMEM_BYTES
        ),
        cost_estimate=pl.CostEstimate(
            flops=6 * count * width * width, transcendentals=0, bytes_accessed=14 * count * width
        ),
    )(core.reshape(1).astype(jnp.int32), grad_projected, hidden)


def hidden_back_kernel(rows_qkv, group, groups, weights, gp_ref, out_ref, w_ref, sem):
    step = pl.program_id(0)
    block = gp_ref.shape[2]

    @pl.when(step == 0)
    def _():
        fetch(weights, 0, rows_qkv, w_ref, sem, group)

    arrive_in_time(w_ref, sem, group * rows_qkv, range(groups), block, step)
    term = dot_nn(gp_ref[0], w_ref[pl.ds(pl.multiple_of(step * block, block), block), :])

    @pl.when(step == 0)
    def _():
        out_ref[...] = term

    @pl.when(step > 0)
    def _():
        out_ref[...] += term


def hidden_back(grad_projected, weights, rows_qkv):
    _, count, width = grad_projected.shape
    group, groups = grouping(weights, 4)
    return fetching_call(
        functools.partial(hidden_back_kernel, rows_qkv, group, groups),
        [weights],
        name="grad_hidden_one",
        grid=(3,),
        in_specs=[pl.BlockSpec((1, count, width), lambda j, *_: (j, 0, 0))],
        out_specs=[whole((count, width))],
        out_shape=[sds((count, width), F32)],
        scratch=[pltpu.VMEM((3 * width, width), BF16), pltpu.SemaphoreType.DMA((groups,))],
        flops=6 * count * width * width,
        nbytes=2 * 8 * count * width,
    )(grad_projected)[0]


def norm_back_kernel(grad_ref, tok_ref, mid_ref, gain_ref, out_ref, gnorm_ref):
    normed, inverse = normalise(tok_ref[...].astype(F32))
    grad = grad_ref[...]
    part = jnp.sum(grad * normed, axis=0, keepdims=True)
    hat = grad * gain_ref[:1, :]
    first = jnp.mean(hat, axis=-1, keepdims=True)
    second = jnp.mean(hat * normed, axis=-1, keepdims=True)
    out_ref[...] = mid_ref[...] + inverse * (hat - first - normed * second)

    @pl.when(pl.program_id(0) == 0)
    def _():
        gnorm_ref[...] = part

    @pl.when(pl.program_id(0) > 0)
    def _():
        gnorm_ref[...] += part


def norm_back(grad, tokens, mid, gain):
    count, width = tokens.shape
    rows = pl.BlockSpec((256, width), lambda i: (i, 0))
    return call(
        norm_back_kernel,
        name="grad_tokens",
        grid=(count // 256,),
        in_specs=[rows, rows, rows, whole((2, width))],
        out_specs=[rows, whole((1, width))],
        out_shape=[sds((count, width), F32), sds((1, width), F32)],
        flops=20 * count * width,
        nbytes=14 * count * width,
    )(grad, tokens, mid, gain)


Z, Y, X = 4, 2, 2
UP, DOWN, IN_Y, IN_X = (1, 0, 0), (-1, 0, 0), (0, 1, 0), (0, 0, 1)
CROSSED, LEVEL, UPRIGHT = ("planes", "lines"), ("planes", "planes"), ("lines", "lines")
SPREAD = {
    CROSSED: (((UP, IN_X), (DOWN, IN_Y), (UP, IN_Y)), ((IN_Y, UP), (IN_X, DOWN), (IN_X, UP))),
    LEVEL: (((UP, UP), (DOWN, DOWN), (UP, UP)), ((IN_Y, IN_X), (IN_X, IN_Y), (IN_X, IN_Y))),
    UPRIGHT: (((IN_X, IN_Y), (IN_Y, IN_X), (IN_Y, IN_X)), ((UP, UP), (DOWN, DOWN), (UP, UP))),
}
REDUCE = {
    CROSSED: (((IN_X, DOWN), (IN_X, UP), (IN_Y, DOWN)), ((DOWN, IN_Y), (UP, IN_Y), (DOWN, IN_X))),
    LEVEL: (((IN_X, IN_Y), (IN_X, IN_Y), (IN_Y, IN_X)), ((DOWN, DOWN), (UP, UP), (DOWN, DOWN))),
    UPRIGHT: (((DOWN, DOWN), (UP, UP), (DOWN, DOWN)), ((IN_Y, IN_X), (IN_Y, IN_X), (IN_X, IN_Y))),
}


def ident(z, y, x, c):
    return (((z % Z) * Y + y % Y) * X + x % X) * 2 + c


def plus(*moves):
    return tuple(sum(m[i] for m in moves) for i in range(3))


def minus(move):
    return tuple(-m for m in move)


def hop(array, axis, moves):
    pairs = [
        (ident(z, y, x, c), ident(z + m[0], y + m[1], x + m[2], c))
        for z in range(Z) for y in range(Y) for x in range(X)
        for c, m in enumerate(moves)
    ]
    return lax.ppermute(array, axis, pairs)


def swap_cores(array, axis):
    return lax.ppermute(array, axis, [(i, i ^ 1) for i in range(2 * Z * Y * X)])


def place(axis):
    me = lax.axis_index(axis)
    return (me // (2 * Y * X), me // (2 * X) % Y, me // 2 % X), me % 2


def by_core(c, zero, one):
    return jnp.where(c == 0, jnp.stack(zero), jnp.stack(one)).astype(jnp.int32)


def together(*places):
    values = lax.optimization_barrier(tuple(getattr(owner, name) for owner, name in places))
    for (owner, name), value in zip(places, values, strict=True):
        setattr(owner, name, value)


def tie(*values):
    return lax.optimization_barrier(values)


class Spread:
    def __init__(self, shard, axis, route):
        self.shard, self.axis, self.route = shard, axis, route

    def near(self):
        short, _ = SPREAD[self.route]
        self.first = hop(self.shard, self.axis, short[0])
        self.third = hop(self.shard, self.axis, short[1])

    def nearer(self):
        short, _ = SPREAD[self.route]
        second = hop(self.first, self.axis, short[2])
        self.block = jnp.stack([self.shard, self.first, second, self.third])

    def far_one(self):
        self.one = hop(self.block, self.axis, SPREAD[self.route][1][0])

    def far_three(self):
        self.three = hop(self.block, self.axis, SPREAD[self.route][1][1])

    def farther(self):
        _, far = SPREAD[self.route]
        self.two = hop(self.one, self.axis, far[2])

    def swap(self, *names):
        for name in names:
            setattr(self, "other_" + name, swap_cores(getattr(self, name), self.axis))

    def result(self):
        short, far = SPREAD[self.route]
        names = ("block", "one", "two", "three")
        pieces = tuple(getattr(self, kind + name) for kind in ("", "other_") for name in names)
        at, c = place(self.axis)
        froms = []
        for core in range(2):
            s, f = [m[core] for m in short], [m[core] for m in far]
            close = [(0, 0, 0), s[0], plus(s[0], s[2]), s[1]]
            long = [(0, 0, 0), f[0], plus(f[0], f[2]), f[1]]
            froms.append([ident(*plus(at, minus(a), minus(b)), core) for a in long for b in close])
        order = jnp.concatenate([by_core(c, *froms), by_core(c, *froms[::-1])])
        return order, pieces


def lay_out(grad, wide):
    spans = [(b, min(b + wide, grad.shape[2])) for b in range(0, grad.shape[2], wide)]
    return spans, grad.shape[1] * len(spans)


def gather_rows(mine, theirs, more, out, wide):
    at = 0
    for g, t in zip(mine, theirs, strict=True):
        rows = g.shape[1]
        for a, b in lay_out(g, wide)[0]:
            value = g[0, :, a:b].astype(F32) + t[0, :, a:b].astype(F32)
            for m in more:
                value = value + m[at : at + rows, : b - a].astype(F32)
            out[at : at + rows, : b - a] = value.astype(out.dtype)
            if b - a < wide:
                out[at : at + rows, b - a :] = jnp.zeros((rows, wide - (b - a)), out.dtype)
            at += rows


def collect_call(kernel, name, chosen, lines, splits, in_specs, out_specs, out_shape, nbytes, args):
    return pl.pallas_call(
        kernel,
        name=name,
        grid_spec=pltpu.PrefetchScalarGridSpec(
            num_scalar_prefetch=1, grid=(lines, splits), in_specs=in_specs, out_specs=out_specs
        ),
        out_shape=out_shape,
        compiler_params=pltpu.CompilerParams(
            dimension_semantics=("arbitrary", "arbitrary"), vmem_limit_bytes=VMEM_BYTES
        ),
        cost_estimate=pl.CostEstimate(flops=nbytes, transcendentals=0, bytes_accessed=nbytes),
    )(chosen, *args)


def collect(grads, twins, extras, chosen, lines, wide):
    four = chosen.shape[1]
    total = sum(lay_out(g, wide)[1] for g in grads)
    k, number = len(grads) * four, len(lines)
    splits, part = 1, wide

    def kernel(chosen_ref, *refs):
        mine, theirs, more, outs = refs[:k], refs[k : 2 * k], refs[2 * k : -number], refs[-number:]

        def fill(out):
            for i in range(four):
                gather_rows(mine[i::four], theirs[i::four], [m.at[i] for m in more], out.at[i], part)

        for j, out in enumerate(outs):
            pl.when(pl.program_id(0) == j)(functools.partial(fill, out))

    def by_device(g, i):
        def index(j, q, chosen_ref):
            device = chosen_ref[lines[0], i]
            for step, which in enumerate(lines[1:], 1):
                device = jnp.where(j == step, chosen_ref[which, i], device)
            return device, 0, q

        return pl.BlockSpec((1, g.shape[1], g.shape[2] // splits), index)

    def output(step):
        index = lambda j, q, _: (0, 0, jnp.where(j < step, 0, jnp.where(j > step, splits - 1, q)))
        return pl.BlockSpec((four, total, part), index)

    arrived = pl.BlockSpec((four, total, part), lambda j, q, _: (0, 0, q))
    devices = [by_device(g, i) for g in grads for i in range(four)]
    return collect_call(
        kernel,
        "collect_grads",
        chosen,
        number,
        splits,
        devices * 2 + [arrived] * len(extras),
        [output(j) for j in range(number)],
        [sds((four, total, wide), BF16)] * number,
        2 * number * four * total * wide * (3 + len(extras)),
        [*(g for g in (*grads, *twins) for _ in range(four)), *extras],
    )


def collect_last(grads, twins, extras, chosen, wide, direct):
    four = chosen.shape[1]
    total = sum(lay_out(g, wide)[1] for g in grads)
    k = len(grads) * four

    def kernel(chosen_ref, *refs):
        mine, theirs, more, outs = refs[:k], refs[k : 2 * k], refs[2 * k : -four], refs[-four:]
        for i, out in enumerate(outs):
            gather_rows(mine[i::four], theirs[i::four], [m.at[0] for m in more[i::four]], out, wide)

    def pick(shape, line, i):
        return pl.BlockSpec((1, *shape[1:]), lambda j, q, chosen_ref: (chosen_ref[line, i], 0, 0))

    devices = [pick(g.shape, 3, i) for g in grads for i in range(four)]
    places = [pick(m.shape, 4, i) for m in extras for i in range(four)]
    return collect_call(
        kernel,
        "collect_last_grads",
        chosen,
        1,
        1,
        devices * 2 + places,
        [whole((total, wide))] * four,
        [sds((total, wide), kind) for kind in (BF16, BF16, BF16 if direct else F32, F32)],
        2 * four * total * wide * (4 + len(extras)),
        [a for a in (*grads, *twins, *extras) for _ in range(four)],
    )


class Reduce:
    def __init__(self, axis, route, wide, halves=False, direct=False):
        self.axis, self.route, self.wide, self.halves, self.direct = axis, route, wide, halves, direct
        far, short = REDUCE[route]
        at, c = place(axis)
        both = lambda a, b: tuple(plus(i, j) for i, j in zip(a, b, strict=True))
        here = ((0, 0, 0), (0, 0, 0))

        def line(step):
            lists = []
            for core, kind in enumerate(route):
                z, y, x = plus(at, step[core])
                if kind == "planes":
                    lists.append([ident(k, y, x, core) for k in range(Z)])
                else:
                    lists.append([ident(z, j, k, core) for j in range(Y) for k in range(X)])
            return by_core(c, *lists)

        def slot(step):
            places = []
            for core, kind in enumerate(route):
                z, y, x = plus(at, step[core])
                places.append(z % Z if kind == "planes" else y % Y * X + x % X)
            return jnp.where(c == 0, places[0], places[1])

        ends = (both(short[0], short[2]), short[1], short[2], here)
        slots = jnp.stack([slot(step) for step in ends]).astype(jnp.int32)
        lines = [line(step) for step in (both(far[0], far[2]), far[1], far[2])]
        last = []
        for core in range(2):
            last.append([ident(*plus(at, step[core]), core) for step in ends])
        devices = jnp.stack([*lines, by_core(c, *last)])
        self.chosen = jnp.concatenate([devices // 2 if halves else devices, slots[None]])

    def pair(self, grads, go=None):
        self.grads = grads
        self.twins = tuple(swap_cores(g, self.axis) for g in (go if self.halves else grads))

    def pack(self):
        self.one, self.two = collect(self.grads, self.twins, (), self.chosen, (0, 1), self.wide)

    def far(self):
        far, _ = REDUCE[self.route]
        self.one, self.two = hop(self.one, self.axis, far[0]), hop(self.two, self.axis, far[1])

    def repack(self):
        (self.three,) = collect(self.grads, self.twins, (self.one,), self.chosen, (2,), self.wide)

    def farther(self):
        far, _ = REDUCE[self.route]
        self.three = hop(self.three, self.axis, far[2])

    def gather(self):
        self.one, self.two, self.three, self.rest = collect_last(
            self.grads, self.twins, (self.two, self.three), self.chosen, self.wide, self.direct
        )

    def near(self):
        _, short = REDUCE[self.route]
        first = short[0]
        if self.direct:
            first = tuple(plus(a, b) for a, b in zip(short[0], short[2], strict=True))
            self.three = hop(self.three, self.axis, short[2])
        self.one, self.two = hop(self.one, self.axis, first), hop(self.two, self.axis, short[1])

    def nearer(self):
        _, short = REDUCE[self.route]
        self.three = hop((self.three + self.one.astype(F32)).astype(BF16), self.axis, short[2])

    def result(self):
        total = self.rest + self.two.astype(F32) + self.three.astype(F32)
        return total + self.one.astype(F32) if self.direct else total


def tables(segment):
    count = segment.shape[0]
    slots = jnp.arange(count, dtype=jnp.int32)
    order = jnp.where(segment < 0, count, segment)
    starts = jnp.sum((order[None, :] < order[:, None]).astype(jnp.int32), axis=1)
    positions = (slots - starts).astype(F32)
    half = HD // 2
    freqs = THETA ** (-2.0 * jnp.arange(half, dtype=F32) / HD)
    angles = positions[:, None] * freqs[None, :]
    cosine, sine = jnp.cos(angles), jnp.sin(angles)
    cosine = jnp.concatenate([cosine] * 4, axis=1)
    sine = jnp.concatenate([-sine, sine] * 2, axis=1)
    group = jnp.where(segment < 0, -1 - slots, segment)
    return cosine, sine, jnp.broadcast_to(group[:, None], (count, LANES)), group[None, :]


def pad_units(w_ff_out, n, padded):
    units = w_ff_out.reshape(w_ff_out.shape[0], n // 2, -1)
    return jnp.pad(units, ((0, 0), (0, 0), (0, padded - units.shape[2]))).reshape(w_ff_out.shape[0], -1)


def drop_units(g_ff, n, padded, rows_in):
    return g_ff.reshape(-1, n // 2, padded)[:, :, :rows_in].reshape(-1, n // 2 * rows_in)


def sum_norms(n, axis, g_one, g_two):
    g_norms = jnp.stack([g_one.reshape(n, -1), g_two.reshape(n, -1)], axis=1)
    g_norms = jnp.sum(lax.all_to_all(g_norms, axis, 0, 0, tiled=True), axis=0)
    return g_norms


def by_collectives(tokens, cotangent, segment, w_qkv, w_attn_out, w_in, w_ff_out, gains, w_in_rows, padded, axis):
    n = lax.axis_size(axis)
    width = tokens.shape[1]
    units = n // 2 * padded
    pairs = width // LANES
    gather = lambda shard: lax.all_gather(shard, axis, axis=0, tiled=True)
    at_once = lambda matrix: (jnp.zeros((1,), jnp.int32), (matrix[None],))
    w_qkv, w_ff = at_once(gather(w_qkv)), at_once(gather(pad_units(w_ff_out, n, padded)))
    w_in = at_once(jnp.concatenate([gather(w_in), gather(w_attn_out)]))
    gains = gather(gains.reshape(1, 2, -1)).astype(F32).transpose(1, 0, 2).reshape(2, width)
    cosine, sine, seg_column, seg_row = tables(segment)
    qkv, hidden_one, gains = project(tokens, cosine, sine, w_qkv, 3 * width, gains)
    attn_out, lse = attend(qkv, seg_column, seg_row, width, 0, pairs)
    resid, mixed, mid, grad_heads, g_out, g_two, g_in, g_ff = ffn(
        tokens, attn_out, cotangent, gains, w_in, w_ff, units, 2 * units, width, width
    )
    output = ffn_out(resid, mixed, w_ff, width)
    grad_projected = attend_back(qkv, attn_out, grad_heads, lse, seg_column, seg_row, cosine, sine, 0, pairs)
    g_qkv = project_grad(grad_projected, hidden_one)
    grad_tokens, g_one = norm_back(hidden_back(grad_projected, w_qkv, 3 * width), tokens, mid, gains)
    scatter = lambda grad: lax.psum_scatter(grad, axis, scatter_dimension=0, tiled=True).astype(F32)
    g_in = g_in.reshape(2 * units, width)
    g_ff = drop_units(scatter(g_ff), n, padded, w_in_rows)
    return output, grad_tokens, scatter(g_qkv), scatter(g_out), scatter(g_in), g_ff, g_one, g_two


class Box:
    pass


def by_links(tokens, cotangent, segment, w_qkv, w_attn_out, w_in, w_ff_out, gains, w_in_rows, padded, axis):
    n = lax.axis_size(axis)
    width = tokens.shape[1]
    units = n // 2 * padded
    pairs = width // LANES
    rows_qkv, rows_out, rows_ff = w_qkv.shape[0], w_attn_out.shape[0], w_ff_out.shape[0]
    v = Box()
    gain_rows = jnp.pad(gains[None], ((0, 7), (0, width - gains.shape[0])))
    s_qkv = Spread(jnp.concatenate([w_qkv, gain_rows]), axis, LEVEL)
    s_in = Spread(jnp.concatenate([w_in, w_attn_out]), axis, LEVEL)
    s_qkv.shard, w_ff_out = tie(s_qkv.shard, w_ff_out)
    s_ff = Spread(pad_units(w_ff_out, n, padded), axis, UPRIGHT)
    r_ff = Reduce(axis, UPRIGHT, units, direct=True)
    r_in = Reduce(axis, LEVEL, width)
    r_qkv = Reduce(axis, LEVEL, width, halves=True, direct=True)
    v.cosine, v.sine, v.seg_column, v.seg_row = tables(segment)

    s_qkv.near()
    s_ff.near()
    s_qkv.nearer()
    together((s_qkv, "block"), (s_in, "shard"), (s_ff, "first"), (s_ff, "third"), *((v, k) for k in vars(v)))
    s_qkv.far_one()
    s_qkv.far_three()
    s_in.near()
    s_ff.nearer()
    together((s_qkv, "one"), (s_qkv, "three"), (s_qkv, "block"), (s_in, "first"), (s_in, "third"), (s_ff, "block"))
    s_qkv.farther()
    s_in.nearer()
    s_qkv.swap("block", "one", "three")
    together(
        (s_qkv, "two"), (s_qkv, "other_block"), (s_qkv, "other_three"), (s_qkv, "other_one"),
        (s_in, "block"), (s_ff, "block"),
    )
    s_in.far_one()
    s_in.far_three()
    s_ff.far_one()
    s_qkv.swap("two")
    s_ff.swap("block")
    w_qkv = s_qkv.result()
    v.qkv, v.hidden_one, v.gains = project(tokens, v.cosine, v.sine, w_qkv, rows_qkv)
    together((v, "qkv"), (s_ff, "one"), (s_ff, "block"), (s_in, "block"), (s_ff, "other_block"))
    s_ff.far_three()
    s_ff.swap("one")
    s_in.swap("block")
    attend_some = lambda first, number, done=None: attend(v.qkv, v.seg_column, v.seg_row, width, first, number, done)
    v.done = attend_some(0, pairs // 2)
    together(
        (v, "done"), (s_in, "one"), (s_in, "three"), (s_ff, "one"), (s_ff, "three"),
        (s_in, "other_block"), (s_ff, "other_one"),
    )
    s_in.farther()
    s_ff.farther()
    s_in.swap("one", "three")
    s_ff.swap("three")
    v.done = attend_some(pairs // 2, pairs // 2, v.done)
    together(
        (v, "done"), (s_in, "two"), (s_ff, "two"), (s_in, "other_one"), (s_in, "other_three"), (s_ff, "other_three")
    )
    s_in.swap("two")
    s_ff.swap("two")
    attn_out, lse = v.done
    w_in, w_ff = s_in.result(), s_ff.result()
    rows_of = lambda grad: grad.reshape(n, -1, grad.shape[-1])
    resid, v.mixed, mid, v.heads, v.g_out, g_two, v.g_in, g_ff = ffn(
        tokens, attn_out, cotangent, v.gains, w_in, w_ff, units, padded, rows_out, rows_ff
    )

    def back(first, number):
        v.some = attend_back(
            v.qkv, attn_out, v.heads, lse, v.seg_column, v.seg_row, v.cosine, v.sine,
            first * pairs // 8, number * pairs // 8, v.some,
        )

    v.some = None
    r_ff.pair((rows_of(g_ff),))
    back(0, 1)
    together((v, "some"), (r_ff, "twins"), (v, "g_in"), (v, "g_out"))
    r_in.pair((rows_of(v.g_in), rows_of(v.g_out)))
    r_ff.pack()
    together((v, "some"), (r_ff, "one"), (r_ff, "two"))
    r_ff.far()
    back(1, 2)
    together((v, "some"), (r_in, "twins"))
    r_in.pack()
    together((v, "some"), (r_in, "one"), (r_in, "two"))
    r_in.far()
    back(3, 2)
    together((v, "some"), (r_ff, "one"), (r_ff, "two"))
    r_ff.repack()
    together((v, "some"), (r_ff, "three"))
    r_ff.farther()
    back(5, 2)
    together((v, "some"), (r_in, "one"), (r_in, "two"), (r_ff, "three"))
    r_in.repack()
    together((v, "some"), (r_in, "three"), (r_ff, "three"))
    r_in.farther()
    back(7, 1)
    together((v, "some"), (r_ff, "three"))
    r_ff.gather()
    together((v, "some"), (r_ff, "one"), (r_ff, "two"))
    r_ff.near()
    v.stay, v.go = project_grad_halves(v.some, v.hidden_one, rows_qkv, place(axis)[1])
    together((v, "some"), (v, "stay"), (v, "go"), (r_in, "three"), (r_ff, "one"), (r_ff, "two"), (r_ff, "three"))
    half_of = lambda grad: grad.reshape(n // 2, -1, width)
    r_qkv.pair((half_of(v.stay),), (half_of(v.go),))
    r_in.gather()
    together((v, "some"), (r_qkv, "twins"), (r_in, "one"), (r_in, "two"))
    r_in.near()
    r_qkv.pack()
    together((v, "some"), (r_qkv, "one"), (r_qkv, "two"))
    r_qkv.far()
    v.hidden = hidden_back(v.some, w_qkv, rows_qkv)
    together(
        (v, "hidden"), (r_qkv, "one"), (r_qkv, "two"), (r_in, "one"), (r_in, "two"),
        (r_ff, "one"), (r_ff, "two"), (r_ff, "three"),
    )
    v.g_ff = drop_units(r_ff.result(), n, padded, w_in_rows)
    r_qkv.repack()
    together((v, "hidden"), (r_qkv, "three"))
    r_qkv.farther()
    r_in.nearer()
    v.grad_tokens, v.g_one = norm_back(v.hidden, tokens, mid, v.gains)
    together((v, "grad_tokens"), (v, "g_one"), (r_qkv, "three"), (r_in, "three"))
    r_qkv.gather()
    together((v, "mixed"), (r_qkv, "one"), (r_qkv, "two"), (r_qkv, "three"), (r_qkv, "rest"))
    r_qkv.near()
    v.output = ffn_out(resid, v.mixed, w_ff, rows_ff)
    together((v, "output"), (r_qkv, "one"), (r_qkv, "two"), (r_qkv, "three"), (r_in, "three"))
    rest = r_in.result()
    return v.output, v.grad_tokens, r_qkv.result(), rest[padded:], rest[:padded], v.g_ff, v.g_one, g_two


def body(tokens, cotangent, segment, w_qkv, w_attn_out, w_in, w_ff_out, norm_one, norm_two):
    axis = "fsdp"
    n = lax.axis_size(axis)
    rows_in = w_in.shape[0]
    padded = -(-rows_in // 16) * 16
    w_in = jnp.pad(w_in, ((0, padded - rows_in), (0, 0)))
    scales = norm_one.shape[0]
    aligned = not (any(w.shape[0] % 16 for w in (w_qkv, w_attn_out, w_ff_out)) or scales & (scales - 1))
    way = by_links if aligned and n == 2 * Z * Y * X else by_collectives
    output, grad_tokens, g_qkv, g_out, g_in, g_ff, g_one, g_two = way(
        tokens, cotangent, segment, w_qkv, w_attn_out, w_in, w_ff_out, jnp.concatenate([norm_one, norm_two]), rows_in, padded, axis
    )
    g_norms = sum_norms(n, axis, g_one, g_two)
    g_in = g_in[:rows_in]
    return (output, grad_tokens, g_qkv, g_out, g_in, g_ff, g_norms[0], g_norms[1])


def solution(mesh):
    rows, flat = P("fsdp", None), P("fsdp")
    return jax.shard_map(
        body,
        mesh=mesh,
        in_specs=(rows, rows, flat, rows, rows, rows, rows, flat, flat),
        out_specs=(rows, rows, rows, rows, rows, rows, flat, flat),
        check_vma=False,
    )
```

```python
import functools
import math

import jax
import jax.numpy as jnp
from jax import lax
from jax.experimental import pallas as pl
from jax.experimental.pallas import tpu as pltpu
from jax.sharding import PartitionSpec as P

HD = 64
EPS = 1e-05
THETA = 160000.0
NEG = -1e30
LANES = 128
F32 = jnp.float32
BF16 = jnp.bfloat16
VMEM_BYTES = 62 << 20


def dot_nt(left, right):
    return lax.dot_general(left, right, (((1,), (1,)), ((), ())), preferred_element_type=F32)


def dot_nn(left, right):
    return lax.dot_general(left, right, (((1,), (0,)), ((), ())), preferred_element_type=F32)


def dot_tn(left, right):
    return lax.dot_general(left, right, (((0,), (0,)), ((), ())), preferred_element_type=F32)


def call(kernel, *, name, grid, in_specs, out_specs, out_shape, scratch=(), flops=0, nbytes=0, aliases=None):
    return pl.pallas_call(
        kernel,
        name=name,
        grid=grid,
        in_specs=in_specs,
        out_specs=out_specs,
        out_shape=out_shape,
        scratch_shapes=list(scratch),
        input_output_aliases=aliases or {},
        compiler_params=pltpu.CompilerParams(
            dimension_semantics=("arbitrary",) * len(grid), vmem_limit_bytes=VMEM_BYTES
        ),
        cost_estimate=pl.CostEstimate(flops=flops, transcendentals=0, bytes_accessed=nbytes),
    )


def sds(shape, dtype):
    return jax.ShapeDtypeStruct(shape, dtype)


def whole(shape, once=False):
    zeros = (0,) * len(shape)
    mode = dict(pipeline_mode=pl.Buffered(1)) if once else {}
    return pl.BlockSpec(shape, lambda *_: zeros, **mode)


def normalise(field):
    centre = jnp.mean(field, axis=-1, keepdims=True)
    centered = field - centre
    variance = jnp.mean(centered * centered, axis=-1, keepdims=True)
    inverse = lax.rsqrt(variance + EPS)
    return centered * inverse, inverse


def minus_row(field, row):
    return (field.reshape(-1, *row.shape) - row[None]).reshape(field.shape)


def swap_halves(field):
    lane = lax.broadcasted_iota(jnp.int32, field.shape, 1)
    first = (lane & (HD - 1)) < HD // 2
    return jnp.where(
        first, pltpu.roll(field, LANES - HD // 2, 1), pltpu.roll(field, HD // 2, 1)
    )


def fetch(weights, at, rows, target, sem, group=None, columns=slice(None)):
    order_ref, pieces = weights
    i = 0
    for piece in pieces:
        for slot in range(piece.shape[0]):
            device = order_ref[i]
            start = pl.multiple_of(device * rows, rows)
            pltpu.make_async_copy(
                piece.at[slot, pl.ds(at, rows), columns],
                target.at[pl.ds(start, rows), columns],
                sem if group is None else sem.at[device // group],
            ).start()
            i += 1


def arrive(target, sem):
    pltpu.make_async_copy(target, target, sem).wait()


def spans_of(columns, wide):
    return [slice(a, min(a + wide, columns)) for a in range(0, columns, wide)]


def grouping(weights, group):
    devices = weights[0].shape[0]
    return (group, devices // group) if devices % group == 0 else (devices, 1)


def arrive_in_time(target, sem, rows, groups, block, step):
    for g in groups:
        @pl.when(step == (g - groups[0]) * rows // block)
        def _(g=g):
            arrive(target.at[pl.ds(g * rows, rows), :], sem.at[g])


def fetching_call(
    kernel, weights, *, name, grid, in_specs, out_specs, out_shape, scratch=(), flops=0, nbytes=0
):
    number = len(weights)

    def run(*refs):
        orders, rest, sets = refs[:number], refs[number:], []
        for order, (_, pieces) in zip(orders, weights, strict=True):
            sets.append((order, rest[: len(pieces)]))
            rest = rest[len(pieces) :]
        kernel(*sets, *rest)

    pieces = [piece for _, some in weights for piece in some]
    made = pl.pallas_call(
        run,
        name=name,
        grid_spec=pltpu.PrefetchScalarGridSpec(
            num_scalar_prefetch=number,
            grid=grid,
            in_specs=[pl.BlockSpec(memory_space=pl.ANY)] * len(pieces) + in_specs,
            out_specs=out_specs,
            scratch_shapes=list(scratch),
        ),
        out_shape=out_shape,
        compiler_params=pltpu.CompilerParams(
            dimension_semantics=("arbitrary",) * len(grid), vmem_limit_bytes=VMEM_BYTES
        ),
        cost_estimate=pl.CostEstimate(flops=flops, transcendentals=0, bytes_accessed=nbytes),
    )
    return lambda *args: made(*[order for order, _ in weights], *pieces, *args)


def unpack_gains(rows_ref, number, out_ref):
    total, width = rows_ref.shape
    devices = total // 8
    owner = lax.broadcasted_iota(jnp.int32, (devices, total), 0)
    row = lax.broadcasted_iota(jnp.int32, (devices, total), 1)
    found = dot_nn((row == owner * 8).astype(BF16), rows_ref[:, :LANES]).astype(BF16)
    place_in = lax.broadcasted_iota(jnp.int32, (LANES, width), 0)
    lane = lax.broadcasted_iota(jnp.int32, (LANES, width), 1) & (number - 1)
    first = lax.broadcasted_iota(jnp.int32, (devices, width), 0) * number
    column = lax.broadcasted_iota(jnp.int32, (devices, width), 1)
    mine = (column >= first) & (column < first + number)
    for which in range(2):
        tiled = dot_nn(found, (place_in == lane + which * number).astype(BF16))
        out_ref[which : which + 1, :] = jnp.sum(jnp.where(mine, tiled, 0.0), axis=0, keepdims=True)


def project_kernel(rope_blocks, query_blocks, rows, given, group, groups, weights, tok_ref, cos_ref, sin_ref, *refs):
    if given:
        gains_in, out_ref, hid_ref, gains_ref, w_ref, sem = refs
    else:
        out_ref, hid_ref, gains_ref, w_ref, sem, rows_ref, rows_sem = refs
    step = pl.program_id(0)
    block = out_ref.shape[1]

    @pl.when(step == 0)
    def _():
        if given:
            gains_ref[...] = gains_in[...]
        else:
            fetch(weights, rows, 8, rows_ref, rows_sem)
        fetch(weights, 0, rows, w_ref, sem, group)
        if not given:
            arrive(rows_ref, rows_sem)
            unpack_gains(rows_ref, w_ref.shape[1] * 8 // rows_ref.shape[0], gains_ref)
        normed, _ = normalise(tok_ref[...].astype(F32))
        hid_ref[...] = (normed * gains_ref[:1, :]).astype(BF16)

    arrive_in_time(w_ref, sem, group * rows, range(groups), block, step)
    w_block = w_ref[pl.ds(pl.multiple_of(step * block, block), block), :]
    some = 256

    @pl.when(step < rope_blocks)
    def _():
        scale = jnp.where(step < query_blocks, 1.0 / math.sqrt(HD), 1.0).astype(F32)
        for r in range(hid_ref.shape[0] // some):
            at = slice(r * some, (r + 1) * some)
            acc = dot_nt(hid_ref[at, :], w_block)
            cosine, sine = cos_ref[at, :] * scale, sin_ref[at, :] * scale
            for s in range(block // LANES):
                part = acc[:, s * LANES : (s + 1) * LANES]
                out_ref[at, s * LANES : (s + 1) * LANES] = (part * cosine + swap_halves(part) * sine).astype(BF16)

    @pl.when(step >= rope_blocks)
    def _():
        for r in range(hid_ref.shape[0] // some):
            at = slice(r * some, (r + 1) * some)
            out_ref[at, :] = dot_nt(hid_ref[at, :], w_block).astype(BF16)


def project(tokens, cosine, sine, weights, rows, gains=None):
    count, width = tokens.shape
    total = 3 * width
    block = width
    given = gains is not None
    group, groups = grouping(weights, 4)
    own = [] if given else [pltpu.VMEM((weights[0].shape[0] * 8, width), BF16), pltpu.SemaphoreType.DMA]
    return fetching_call(
        functools.partial(project_kernel, 2 * width // block, width // block, rows, given, group, groups),
        [weights],
        name="norm_project",
        grid=(total // block,),
        in_specs=[whole((count, width)), whole((count, LANES)), whole((count, LANES))]
        + [whole((2, width))] * given,
        out_specs=[
            pl.BlockSpec((count, block), lambda j, *_: (0, j)),
            whole((count, width)),
            whole((2, width)),
        ],
        out_shape=[sds((count, total), BF16), sds((count, width), BF16), sds((2, width), F32)],
        scratch=[pltpu.VMEM((total, width), BF16), pltpu.SemaphoreType.DMA((groups,))] + own,
        flops=2 * count * width * total,
        nbytes=2 * (2 * count * width + total * width + total * count),
    )(tokens, cosine, sine, *([gains] if given else []))


def attend_kernel(q_ref, k_ref, v_ref, segc_ref, segr_ref, out_ref, lse_ref, vt_ref, ot_ref):
    count = q_ref.shape[0]
    vt_ref[...] = v_ref[...].T
    keys, query = k_ref[...], q_ref[...]
    lane = lax.broadcasted_iota(jnp.int32, query.shape, 1)
    allowed = jnp.concatenate([segc_ref[...]] * (count // LANES), axis=1) == segr_ref[...]
    for h in range(2):
        picked = jnp.where((lane >= h * HD) & (lane < (h + 1) * HD), query, jnp.zeros_like(query))
        scores = jnp.where(allowed, dot_nt(keys, picked), NEG)
        top = jnp.max(scores, axis=0, keepdims=True)
        powers = jnp.exp(scores - top)
        total = jnp.sum(powers, axis=0, keepdims=True)
        lse_ref[0, h : h + 1, :] = top + jnp.log(total)
        ot_ref[h * HD : (h + 1) * HD, :] = dot_nn(vt_ref[h * HD : (h + 1) * HD, :], powers.astype(BF16)) / total
    out_ref[...] = ot_ref[...].T.astype(BF16)


def attend(qkv, seg_column, seg_row, width, first, number, before=None):
    count = qkv.shape[0]
    pairs = width // LANES
    kept = () if before is None else tuple(before)

    def kernel(*refs):
        attend_kernel(*refs[:5], *refs[5 + len(kept) :])

    tall = lambda offset: pl.BlockSpec((count, LANES), lambda p: (0, offset + first + p))
    return call(
        kernel,
        name="attend",
        grid=(number,),
        in_specs=[tall(0), tall(pairs), tall(2 * pairs), whole((count, LANES)), whole((1, count))]
        + [pl.BlockSpec(memory_space=pl.ANY)] * len(kept),
        out_specs=[tall(0), pl.BlockSpec((1, 2, count), lambda p: (first + p, 0, 0))],
        out_shape=[sds((count, width), BF16), sds((pairs, 2, count), F32)],
        scratch=[pltpu.VMEM((LANES, count), BF16), pltpu.VMEM((LANES, count), F32)],
        flops=16 * count * count * LANES * number,
        nbytes=2 * 4 * count * LANES * number,
        aliases={5: 0, 6: 1} if kept else None,
    )(qkv, qkv, qkv, seg_column, seg_row, *kept)


def attend_back_kernel(
    chunk, q_ref, k_ref, v_ref, o_ref, g_ref, lse_ref, segc_ref, segr_ref, cos_ref, sin_ref,
    out_ref, kt_ref, dk_ref, dv_ref, dqt_ref, delta_ref, total_ref,
):
    count = q_ref.shape[0]
    kt_ref[...] = k_ref[...].T
    keys, values = k_ref[...], v_ref[...]
    product = (g_ref[...].astype(F32) * o_ref[...].astype(F32)).T
    for h in range(2):
        row = jnp.sum(product[h * HD : (h + 1) * HD, :], axis=0, keepdims=True)
        delta_ref[h] = jnp.broadcast_to(row, (8, count))
        total_ref[h] = jnp.broadcast_to(lse_ref[0, h : h + 1, :], (8, count))
    lane = lax.broadcasted_iota(jnp.int32, (chunk, LANES), 1)
    upper = lax.broadcasted_iota(jnp.int32, (LANES, chunk), 0) < HD
    for c in range(count // chunk):
        at = slice(c * chunk, (c + 1) * chunk)
        query, grad = q_ref[at, :], g_ref[at, :]
        allowed = jnp.concatenate([segc_ref[...]] * (chunk // LANES), axis=1) == segr_ref[:, at]
        grads = []
        for h in range(2):
            mine = (lane >= h * HD) & (lane < (h + 1) * HD)
            query_h = jnp.where(mine, query, jnp.zeros_like(query))
            grad_h = jnp.where(mine, grad, jnp.zeros_like(grad))
            scores = jnp.where(allowed, dot_nt(keys, query_h), NEG)
            weights = jnp.exp(minus_row(scores, total_ref[h, :, at]))
            grad_value = dot_nn(weights.astype(BF16), grad_h)
            spread = minus_row(dot_nt(values, grad_h), delta_ref[h, :, at])
            grad_scores = (weights * spread).astype(BF16)
            grads.append((dot_nn(grad_scores, query_h), grad_value, dot_nn(kt_ref[...], grad_scores)))
        (key_0, value_0, query_0), (key_1, value_1, query_1) = grads
        dqt_ref[:, at] = jnp.where(upper, query_0, query_1)
        if c == 0:
            dk_ref[...] = key_0 + key_1
            dv_ref[...] = value_0 + value_1
        else:
            dk_ref[...] += key_0 + key_1
            dv_ref[...] += value_0 + value_1

    cosine, sine = cos_ref[...], sin_ref[...]
    grad_query = dqt_ref[...].T * (1.0 / math.sqrt(HD))
    out_ref[0] = (grad_query * cosine - swap_halves(grad_query) * sine).astype(BF16)
    grad_key = dk_ref[...]
    out_ref[1] = (grad_key * cosine - swap_halves(grad_key) * sine).astype(BF16)
    out_ref[2] = dv_ref[...].astype(BF16)


def attend_back(qkv, attn_out, grad_heads, lse, seg_column, seg_row, cosine, sine, first, number, before=None):
    count, width = attn_out.shape
    pairs = width // LANES
    chunk = 256
    kept = () if before is None else (before,)

    def kernel(*refs):
        attend_back_kernel(chunk, *refs[:10], *refs[10 + len(kept) :])

    tall = lambda offset: pl.BlockSpec((count, LANES), lambda p: (0, offset + first + p))
    return call(
        kernel,
        name="attend_back",
        grid=(number,),
        in_specs=[
            tall(0),
            tall(pairs),
            tall(2 * pairs),
            tall(0),
            tall(0),
            pl.BlockSpec((1, 2, count), lambda p: (first + p, 0, 0)),
            whole((count, LANES)),
            whole((1, count)),
            whole((count, LANES)),
            whole((count, LANES)),
        ]
        + [pl.BlockSpec(memory_space=pl.ANY)] * len(kept),
        out_specs=pl.BlockSpec((3, count, LANES), lambda p: (0, 0, first + p)),
        out_shape=sds((3, count, width), BF16),
        scratch=[
            pltpu.VMEM((LANES, count), BF16),
            pltpu.VMEM((count, LANES), F32),
            pltpu.VMEM((count, LANES), F32),
            pltpu.VMEM((LANES, count), F32),
            pltpu.VMEM((2, 8, count), F32),
            pltpu.VMEM((2, 8, count), F32),
        ],
        flops=40 * count * count * LANES * number,
        nbytes=2 * 8 * count * LANES * number,
        aliases={10: 0} if kept else None,
    )(qkv, qkv, qkv, attn_out, grad_heads, lse, seg_column, seg_row, cosine, sine, *kept)


def ffn_kernel(
    rows_in, rows_out, rows_ff, group, groups, weights_in, weights_ff,
    tok_ref, attn_ref, cot_ref, gain_ref,
    resid_ref, mixed_ref, mid_ref, heads_ref, g_attn_ref, gnorm_ref, g_in_ref, g_out_ref,
    hid_ref, cot_t_ref, w_attn_ref, w_in_ref, w_ff_ref, sem_attn, sem_in, sem_ff,
):
    step = pl.program_id(0)
    count = resid_ref.shape[0]
    block = g_out_ref.shape[1]
    units = w_in_ref.shape[0] // 2
    width = hid_ref.shape[1]
    spans = spans_of(w_ff_ref.shape[1], width)
    some = 256

    @pl.when(step == 0)
    def _():
        fetch(weights_in, rows_in, rows_out, w_attn_ref, sem_attn)
        fetch(weights_ff, 0, rows_ff, w_ff_ref, sem_ff.at[0], columns=spans[0])
        fetch(weights_in, 0, rows_in, w_in_ref, sem_in, group)
        for b, span in enumerate(spans[1:], 1):
            fetch(weights_ff, 0, rows_ff, w_ff_ref, sem_ff.at[b], columns=span)
        cot_t_ref[...] = cot_ref[...].T
        mid_ref[...] = jnp.zeros_like(mid_ref)
        arrive(w_attn_ref, sem_attn)
        for i in range(count // some):
            at = slice(i * some, (i + 1) * some)
            resid = tok_ref[at, :].astype(F32) + dot_nt(attn_ref[at, :], w_attn_ref[...])
            resid_ref[at, :] = resid
            normed, _ = normalise(resid)
            hid_ref[at, :] = (normed * gain_ref[1:, :]).astype(BF16)

    half = max(groups // 2, 1)
    for some_groups in (range(half), range(half, groups)):
        if some_groups:
            arrive_in_time(w_in_ref, sem_in, group * rows_in, some_groups, block, step)
    for b, span in enumerate(spans):
        pl.when(step == span.start // block)(functools.partial(arrive, w_ff_ref.at[:, span], sem_ff.at[b]))
    hidden = hid_ref[...]
    w_pre = w_in_ref[pl.ds(pl.multiple_of(step * block, block), block), :]
    w_gate = w_in_ref[pl.ds(pl.multiple_of(units + step * block, block), block), :]
    w_out = w_ff_ref[:, pl.ds(pl.multiple_of(step * block, block), block)]
    pre = dot_nt(hidden, w_pre)
    gate = dot_nt(hidden, w_gate)
    grad_mixed = dot_nn(cot_ref[...], w_out)
    cdf = 0.5 * (1.0 + lax.erf(pre * 0.7071067811865476))
    density = jnp.exp(-0.5 * pre * pre) * 0.3989422804014327
    gelu = pre * cdf
    mixed = (gelu * gate).astype(BF16)
    mixed_ref[...] = mixed
    g_out_ref[...] = dot_nn(cot_t_ref[...], mixed).astype(BF16)
    grad_pre = (grad_mixed * gate * (cdf + pre * density)).astype(BF16)
    grad_gate = (grad_mixed * gelu).astype(BF16)
    g_in_ref[0] = dot_tn(grad_pre, hidden).astype(BF16)
    g_in_ref[1] = dot_tn(grad_gate, hidden).astype(BF16)
    mid_ref[...] += dot_nn(grad_pre, w_pre) + dot_nn(grad_gate, w_gate)

    @pl.when(step == pl.num_programs(0) - 1)
    def _():
        gnorm = jnp.zeros_like(gnorm_ref)
        for i in range(count // some):
            at = slice(i * some, (i + 1) * some)
            resid = resid_ref[at, :]
            normed, inverse = normalise(resid)
            grad = mid_ref[at, :]
            gnorm += jnp.sum(grad * normed, axis=0, keepdims=True)
            hat = grad * gain_ref[1:, :]
            first = jnp.mean(hat, axis=-1, keepdims=True)
            second = jnp.mean(hat * normed, axis=-1, keepdims=True)
            mid = cot_ref[at, :].astype(F32) + inverse * (hat - first - normed * second)
            mid_ref[at, :] = mid
            low = mid.astype(BF16)
            cot_t_ref[at, :] = low
            heads_ref[at, :] = dot_nn(low, w_attn_ref[...]).astype(BF16)
        gnorm_ref[...] = gnorm
        for i in range(width // some):
            at = slice(i * some, (i + 1) * some)
            g_attn_ref[at, :] = dot_tn(cot_t_ref[:, at], attn_ref[...]).astype(BF16)


def ffn(tokens, attn_out, cotangent, gains, w_in, w_ff, units, rows_in, rows_out, rows_ff):
    count, width = tokens.shape
    block = 256
    group, groups = grouping(w_in, 2)
    once = whole((count, width), once=True)
    return fetching_call(
        functools.partial(ffn_kernel, rows_in, rows_out, rows_ff, group, groups),
        [w_in, w_ff],
        name="ffn_forward_backward",
        grid=(units // block,),
        in_specs=[once, once, once, whole((2, width))],
        out_specs=[
            once,
            pl.BlockSpec((count, block), lambda j, *_: (0, j)),
            once,
            once,
            whole((width, width), once=True),
            whole((1, width)),
            pl.BlockSpec((2, block, width), lambda j, *_: (0, j, 0)),
            pl.BlockSpec((width, block), lambda j, *_: (0, j)),
        ],
        out_shape=[
            sds((count, width), F32),
            sds((count, units), BF16),
            sds((count, width), F32),
            sds((count, width), BF16),
            sds((width, width), BF16),
            sds((1, width), F32),
            sds((2, units, width), BF16),
            sds((width, units), BF16),
        ],
        scratch=[
            pltpu.VMEM((count, width), BF16),
            pltpu.VMEM((width, count), BF16),
            pltpu.VMEM((width, width), BF16),
            pltpu.VMEM((2 * units, width), BF16),
            pltpu.VMEM((width, units), BF16),
            pltpu.SemaphoreType.DMA,
            pltpu.SemaphoreType.DMA((groups,)),
            pltpu.SemaphoreType.DMA((len(spans_of(units, width)),)),
        ],
        flops=16 * count * width * units,
        nbytes=2 * (10 * count * width + 6 * units * width),
    )(tokens, attn_out, cotangent, gains)


def ffn_out_kernel(rows_ff, weights, resid_ref, mixed_ref, out_ref, w_ref, sem):
    spans = spans_of(mixed_ref.shape[1], out_ref.shape[1])

    @pl.when(pl.program_id(0) == 0)
    def _():
        for b, span in enumerate(spans):
            fetch(weights, 0, rows_ff, w_ref, sem.at[b], columns=span)

    out = resid_ref[...]
    for b, span in enumerate(spans):
        pl.when(pl.program_id(0) == 0)(functools.partial(arrive, w_ref.at[:, span], sem.at[b]))
        out = out + dot_nt(mixed_ref[:, span], w_ref[:, span])
    out_ref[...] = out.astype(BF16)


def ffn_out(resid, mixed, weights, rows_ff):
    count, width = resid.shape
    units = mixed.shape[1]
    rows = lambda columns: pl.BlockSpec((256, columns), lambda i, *_: (i, 0))
    return fetching_call(
        functools.partial(ffn_out_kernel, rows_ff),
        [weights],
        name="ffn_output",
        grid=(count // 256,),
        in_specs=[rows(width), rows(units)],
        out_specs=[rows(width)],
        out_shape=[sds((count, width), BF16)],
        scratch=[pltpu.VMEM((width, units), BF16), pltpu.SemaphoreType.DMA((len(spans_of(units, width)),))],
        flops=2 * count * width * units,
        nbytes=2 * (count * units + 3 * count * width + units * width),
    )(resid, mixed)[0]


def project_grad_kernel(gp_ref, hid_ref, out_ref):
    out_ref[...] = dot_tn(gp_ref[0], hid_ref[...]).astype(BF16)


def project_grad(grad_projected, hidden):
    count, width = hidden.shape
    block = 512
    per = width // block
    return call(
        project_grad_kernel,
        name="grad_qkv",
        grid=(3 * per,),
        in_specs=[pl.BlockSpec((1, count, block), lambda j: (j // per, 0, j % per)), whole((count, width))],
        out_specs=pl.BlockSpec((block, width), lambda j: (j, 0)),
        out_shape=sds((3 * width, width), BF16),
        flops=6 * count * width * width,
        nbytes=2 * 7 * count * width,
    )(grad_projected, hidden)


def project_grad_halves_kernel(rows, core_ref, gp_ref, hid_ref, stay_ref, go_ref, acc_ref):
    step = pl.program_id(0)
    block, width = acc_ref.shape

    def product(k):
        parts, at = [], k * block
        while at < (k + 1) * block:
            stop = min((k + 1) * block, (at // width + 1) * width)
            parts.append(gp_ref[at // width, :, at % width : at % width + stop - at])
            at = stop
        acc_ref[...] = dot_tn(jnp.concatenate(parts, axis=1), hid_ref[...])

    for k in range(gp_ref.shape[0] * width // block):
        pl.when(step == k)(functools.partial(product, k))
    mine = core_ref[0]
    for pair in range(block // (2 * rows)):
        to = slice(pair * rows, (pair + 1) * rows)
        for out, core in ((stay_ref, mine), (go_ref, 1 - mine)):
            start = pl.multiple_of((2 * pair + core) * rows, rows)
            out[to, :] = acc_ref[pl.ds(start, rows), :].astype(BF16)


def project_grad_halves(grad_projected, hidden, rows, core):
    count, width = hidden.shape
    total = 3 * width
    block = next(b for b in range(LANES, total + 1, LANES) if b % (2 * rows) == 0 and total % b == 0)
    half = pl.BlockSpec((block // 2, width), lambda j, _: (j, 0))
    return pl.pallas_call(
        functools.partial(project_grad_halves_kernel, rows),
        name="grad_qkv",
        grid_spec=pltpu.PrefetchScalarGridSpec(
            num_scalar_prefetch=1,
            grid=(total // block,),
            in_specs=[whole(grad_projected.shape, once=True), whole((count, width))],
            out_specs=[half, half],
            scratch_shapes=[pltpu.VMEM((block, width), F32)],
        ),
        out_shape=[sds((total // 2, width), BF16)] * 2,
        compiler_params=pltpu.CompilerParams(
            dimension_semantics=("arbitrary",), vmem_limit_bytes=VMEM_BYTES
        ),
        cost_estimate=pl.CostEstimate(
            flops=6 * count * width * width, transcendentals=0, bytes_accessed=14 * count * width
        ),
    )(core.reshape(1).astype(jnp.int32), grad_projected, hidden)


def hidden_back_kernel(rows_qkv, group, groups, weights, gp_ref, out_ref, w_ref, sem):
    step = pl.program_id(0)
    block = gp_ref.shape[2]

    @pl.when(step == 0)
    def _():
        fetch(weights, 0, rows_qkv, w_ref, sem, group)

    arrive_in_time(w_ref, sem, group * rows_qkv, range(groups), block, step)
    term = dot_nn(gp_ref[0], w_ref[pl.ds(pl.multiple_of(step * block, block), block), :])

    @pl.when(step == 0)
    def _():
        out_ref[...] = term

    @pl.when(step > 0)
    def _():
        out_ref[...] += term


def hidden_back(grad_projected, weights, rows_qkv):
    _, count, width = grad_projected.shape
    group, groups = grouping(weights, 4)
    return fetching_call(
        functools.partial(hidden_back_kernel, rows_qkv, group, groups),
        [weights],
        name="grad_hidden_one",
        grid=(3,),
        in_specs=[pl.BlockSpec((1, count, width), lambda j, *_: (j, 0, 0))],
        out_specs=[whole((count, width))],
        out_shape=[sds((count, width), F32)],
        scratch=[pltpu.VMEM((3 * width, width), BF16), pltpu.SemaphoreType.DMA((groups,))],
        flops=6 * count * width * width,
        nbytes=2 * 8 * count * width,
    )(grad_projected)[0]


def norm_back_kernel(grad_ref, tok_ref, mid_ref, gain_ref, out_ref, gnorm_ref):
    normed, inverse = normalise(tok_ref[...].astype(F32))
    grad = grad_ref[...]
    part = jnp.sum(grad * normed, axis=0, keepdims=True)
    hat = grad * gain_ref[:1, :]
    first = jnp.mean(hat, axis=-1, keepdims=True)
    second = jnp.mean(hat * normed, axis=-1, keepdims=True)
    out_ref[...] = mid_ref[...] + inverse * (hat - first - normed * second)

    @pl.when(pl.program_id(0) == 0)
    def _():
        gnorm_ref[...] = part

    @pl.when(pl.program_id(0) > 0)
    def _():
        gnorm_ref[...] += part


def norm_back(grad, tokens, mid, gain):
    count, width = tokens.shape
    rows = pl.BlockSpec((512, width), lambda i: (i, 0))
    return call(
        norm_back_kernel,
        name="grad_tokens",
        grid=(count // 512,),
        in_specs=[rows, rows, rows, whole((2, width))],
        out_specs=[rows, whole((1, width))],
        out_shape=[sds((count, width), F32), sds((1, width), F32)],
        flops=20 * count * width,
        nbytes=14 * count * width,
    )(grad, tokens, mid, gain)


Z, Y, X = 4, 2, 2
UP, DOWN, IN_Y, IN_X = (1, 0, 0), (-1, 0, 0), (0, 1, 0), (0, 0, 1)
CROSSED, LEVEL, UPRIGHT = ("planes", "lines"), ("planes", "planes"), ("lines", "lines")
SPREAD = {
    CROSSED: (((UP, IN_X), (DOWN, IN_Y), (UP, IN_Y)), ((IN_Y, UP), (IN_X, DOWN), (IN_X, UP))),
    LEVEL: (((UP, UP), (DOWN, DOWN), (UP, UP)), ((IN_Y, IN_X), (IN_X, IN_Y), (IN_X, IN_Y))),
    UPRIGHT: (((IN_X, IN_Y), (IN_Y, IN_X), (IN_Y, IN_X)), ((UP, UP), (DOWN, DOWN), (UP, UP))),
}
REDUCE = {
    CROSSED: (((IN_X, DOWN), (IN_X, UP), (IN_Y, DOWN)), ((DOWN, IN_Y), (UP, IN_Y), (DOWN, IN_X))),
    LEVEL: (((IN_X, IN_Y), (IN_X, IN_Y), (IN_Y, IN_X)), ((DOWN, DOWN), (UP, UP), (DOWN, DOWN))),
    UPRIGHT: (((DOWN, DOWN), (UP, UP), (DOWN, DOWN)), ((IN_Y, IN_X), (IN_Y, IN_X), (IN_X, IN_Y))),
}


def ident(z, y, x, c):
    return (((z % Z) * Y + y % Y) * X + x % X) * 2 + c


def plus(*moves):
    return tuple(sum(m[i] for m in moves) for i in range(3))


def minus(move):
    return tuple(-m for m in move)


def hop(array, axis, moves):
    pairs = [
        (ident(z, y, x, c), ident(z + m[0], y + m[1], x + m[2], c))
        for z in range(Z) for y in range(Y) for x in range(X)
        for c, m in enumerate(moves)
    ]
    return lax.ppermute(array, axis, pairs)


def swap_cores(array, axis):
    return lax.ppermute(array, axis, [(i, i ^ 1) for i in range(2 * Z * Y * X)])


def place(axis):
    me = lax.axis_index(axis)
    return (me // (2 * Y * X), me // (2 * X) % Y, me // 2 % X), me % 2


def by_core(c, zero, one):
    return jnp.where(c == 0, jnp.stack(zero), jnp.stack(one)).astype(jnp.int32)


def together(*places):
    values = lax.optimization_barrier(tuple(getattr(owner, name) for owner, name in places))
    for (owner, name), value in zip(places, values, strict=True):
        setattr(owner, name, value)


def tie(*values):
    return lax.optimization_barrier(values)


class Spread:
    def __init__(self, shard, axis, route):
        self.shard, self.axis, self.route = shard, axis, route

    def near(self):
        short, _ = SPREAD[self.route]
        self.first = hop(self.shard, self.axis, short[0])
        self.third = hop(self.shard, self.axis, short[1])

    def nearer(self):
        short, _ = SPREAD[self.route]
        second = hop(self.first, self.axis, short[2])
        self.block = jnp.stack([self.shard, self.first, second, self.third])

    def far_one(self):
        self.one = hop(self.block, self.axis, SPREAD[self.route][1][0])

    def far_three(self):
        self.three = hop(self.block, self.axis, SPREAD[self.route][1][1])

    def farther(self):
        _, far = SPREAD[self.route]
        self.two = hop(self.one, self.axis, far[2])

    def swap(self, *names):
        for name in names:
            setattr(self, "other_" + name, swap_cores(getattr(self, name), self.axis))

    def result(self):
        short, far = SPREAD[self.route]
        names = ("block", "one", "two", "three")
        pieces = tuple(getattr(self, kind + name) for kind in ("", "other_") for name in names)
        at, c = place(self.axis)
        froms = []
        for core in range(2):
            s, f = [m[core] for m in short], [m[core] for m in far]
            close = [(0, 0, 0), s[0], plus(s[0], s[2]), s[1]]
            long = [(0, 0, 0), f[0], plus(f[0], f[2]), f[1]]
            froms.append([ident(*plus(at, minus(a), minus(b)), core) for a in long for b in close])
        order = jnp.concatenate([by_core(c, *froms), by_core(c, *froms[::-1])])
        return order, pieces


def lay_out(grad, wide):
    spans = [(b, min(b + wide, grad.shape[2])) for b in range(0, grad.shape[2], wide)]
    return spans, grad.shape[1] * len(spans)


def gather_rows(mine, theirs, more, out, wide):
    at = 0
    for g, t in zip(mine, theirs, strict=True):
        rows = g.shape[1]
        for a, b in lay_out(g, wide)[0]:
            value = g[0, :, a:b].astype(F32) + t[0, :, a:b].astype(F32)
            for m in more:
                value = value + m[at : at + rows, : b - a].astype(F32)
            out[at : at + rows, : b - a] = value.astype(out.dtype)
            if b - a < wide:
                out[at : at + rows, b - a :] = jnp.zeros((rows, wide - (b - a)), out.dtype)
            at += rows


def collect_call(kernel, name, chosen, lines, splits, in_specs, out_specs, out_shape, nbytes, args):
    return pl.pallas_call(
        kernel,
        name=name,
        grid_spec=pltpu.PrefetchScalarGridSpec(
            num_scalar_prefetch=1, grid=(lines, splits), in_specs=in_specs, out_specs=out_specs
        ),
        out_shape=out_shape,
        compiler_params=pltpu.CompilerParams(
            dimension_semantics=("arbitrary", "arbitrary"), vmem_limit_bytes=VMEM_BYTES
        ),
        cost_estimate=pl.CostEstimate(flops=nbytes, transcendentals=0, bytes_accessed=nbytes),
    )(chosen, *args)


def collect(grads, twins, extras, chosen, lines, wide):
    four = chosen.shape[1]
    total = sum(lay_out(g, wide)[1] for g in grads)
    k, number = len(grads) * four, len(lines)
    splits, part = 1, wide

    def kernel(chosen_ref, *refs):
        mine, theirs, more, outs = refs[:k], refs[k : 2 * k], refs[2 * k : -number], refs[-number:]

        def fill(out):
            for i in range(four):
                gather_rows(mine[i::four], theirs[i::four], [m.at[i] for m in more], out.at[i], part)

        for j, out in enumerate(outs):
            pl.when(pl.program_id(0) == j)(functools.partial(fill, out))

    def by_device(g, i):
        def index(j, q, chosen_ref):
            device = chosen_ref[lines[0], i]
            for step, which in enumerate(lines[1:], 1):
                device = jnp.where(j == step, chosen_ref[which, i], device)
            return device, 0, q

        return pl.BlockSpec((1, g.shape[1], g.shape[2] // splits), index)

    def output(step):
        index = lambda j, q, _: (0, 0, jnp.where(j < step, 0, jnp.where(j > step, splits - 1, q)))
        return pl.BlockSpec((four, total, part), index)

    arrived = pl.BlockSpec((four, total, part), lambda j, q, _: (0, 0, q))
    devices = [by_device(g, i) for g in grads for i in range(four)]
    return collect_call(
        kernel,
        "collect_grads",
        chosen,
        number,
        splits,
        devices * 2 + [arrived] * len(extras),
        [output(j) for j in range(number)],
        [sds((four, total, wide), BF16)] * number,
        2 * number * four * total * wide * (3 + len(extras)),
        [*(g for g in (*grads, *twins) for _ in range(four)), *extras],
    )


def collect_last(grads, twins, extras, chosen, wide, direct):
    four = chosen.shape[1]
    total = sum(lay_out(g, wide)[1] for g in grads)
    k = len(grads) * four

    def kernel(chosen_ref, *refs):
        mine, theirs, more, outs = refs[:k], refs[k : 2 * k], refs[2 * k : -four], refs[-four:]
        for i, out in enumerate(outs):
            gather_rows(mine[i::four], theirs[i::four], [m.at[0] for m in more[i::four]], out, wide)

    def pick(shape, line, i):
        return pl.BlockSpec((1, *shape[1:]), lambda j, q, chosen_ref: (chosen_ref[line, i], 0, 0))

    devices = [pick(g.shape, 3, i) for g in grads for i in range(four)]
    places = [pick(m.shape, 4, i) for m in extras for i in range(four)]
    return collect_call(
        kernel,
        "collect_last_grads",
        chosen,
        1,
        1,
        devices * 2 + places,
        [whole((total, wide))] * four,
        [sds((total, wide), kind) for kind in (BF16, BF16, BF16 if direct else F32, F32)],
        2 * four * total * wide * (4 + len(extras)),
        [a for a in (*grads, *twins, *extras) for _ in range(four)],
    )


class Reduce:
    def __init__(self, axis, route, wide, halves=False, direct=False):
        self.axis, self.route, self.wide, self.halves, self.direct = axis, route, wide, halves, direct
        far, short = REDUCE[route]
        at, c = place(axis)
        both = lambda a, b: tuple(plus(i, j) for i, j in zip(a, b, strict=True))
        here = ((0, 0, 0), (0, 0, 0))

        def line(step):
            lists = []
            for core, kind in enumerate(route):
                z, y, x = plus(at, step[core])
                if kind == "planes":
                    lists.append([ident(k, y, x, core) for k in range(Z)])
                else:
                    lists.append([ident(z, j, k, core) for j in range(Y) for k in range(X)])
            return by_core(c, *lists)

        def slot(step):
            places = []
            for core, kind in enumerate(route):
                z, y, x = plus(at, step[core])
                places.append(z % Z if kind == "planes" else y % Y * X + x % X)
            return jnp.where(c == 0, places[0], places[1])

        ends = (both(short[0], short[2]), short[1], short[2], here)
        slots = jnp.stack([slot(step) for step in ends]).astype(jnp.int32)
        lines = [line(step) for step in (both(far[0], far[2]), far[1], far[2])]
        last = []
        for core in range(2):
            last.append([ident(*plus(at, step[core]), core) for step in ends])
        devices = jnp.stack([*lines, by_core(c, *last)])
        self.chosen = jnp.concatenate([devices // 2 if halves else devices, slots[None]])

    def pair(self, grads, go=None):
        self.grads = grads
        self.twins = tuple(swap_cores(g, self.axis) for g in (go if self.halves else grads))

    def pack(self):
        self.one, self.two = collect(self.grads, self.twins, (), self.chosen, (0, 1), self.wide)

    def far(self):
        far, _ = REDUCE[self.route]
        self.one, self.two = hop(self.one, self.axis, far[0]), hop(self.two, self.axis, far[1])

    def repack(self):
        (self.three,) = collect(self.grads, self.twins, (self.one,), self.chosen, (2,), self.wide)

    def farther(self):
        far, _ = REDUCE[self.route]
        self.three = hop(self.three, self.axis, far[2])

    def gather(self):
        self.one, self.two, self.three, self.rest = collect_last(
            self.grads, self.twins, (self.two, self.three), self.chosen, self.wide, self.direct
        )

    def near(self):
        _, short = REDUCE[self.route]
        first = short[0]
        if self.direct:
            first = tuple(plus(a, b) for a, b in zip(short[0], short[2], strict=True))
            self.three = hop(self.three, self.axis, short[2])
        self.one, self.two = hop(self.one, self.axis, first), hop(self.two, self.axis, short[1])

    def nearer(self):
        _, short = REDUCE[self.route]
        self.three = hop((self.three + self.one.astype(F32)).astype(BF16), self.axis, short[2])

    def result(self):
        total = self.rest + self.two.astype(F32) + self.three.astype(F32)
        return total + self.one.astype(F32) if self.direct else total


def tables(segment):
    count = segment.shape[0]
    slots = jnp.arange(count, dtype=jnp.int32)
    order = jnp.where(segment < 0, count, segment)
    starts = jnp.sum((order[None, :] < order[:, None]).astype(jnp.int32), axis=1)
    positions = (slots - starts).astype(F32)
    half = HD // 2
    freqs = THETA ** (-2.0 * jnp.arange(half, dtype=F32) / HD)
    angles = positions[:, None] * freqs[None, :]
    cosine, sine = jnp.cos(angles), jnp.sin(angles)
    cosine = jnp.concatenate([cosine] * 4, axis=1)
    sine = jnp.concatenate([-sine, sine] * 2, axis=1)
    group = jnp.where(segment < 0, -1 - slots, segment)
    return cosine, sine, jnp.broadcast_to(group[:, None], (count, LANES)), group[None, :]


def pad_units(w_ff_out, n, padded):
    units = w_ff_out.reshape(w_ff_out.shape[0], n // 2, -1)
    return jnp.pad(units, ((0, 0), (0, 0), (0, padded - units.shape[2]))).reshape(w_ff_out.shape[0], -1)


def drop_units(g_ff, n, padded, rows_in):
    return g_ff.reshape(-1, n // 2, padded)[:, :, :rows_in].reshape(-1, n // 2 * rows_in)


def sum_norms(n, axis, g_one, g_two):
    g_norms = jnp.stack([g_one.reshape(n, -1), g_two.reshape(n, -1)], axis=1)
    g_norms = jnp.sum(lax.all_to_all(g_norms, axis, 0, 0, tiled=True), axis=0)
    return g_norms


def by_collectives(tokens, cotangent, segment, w_qkv, w_attn_out, w_in, w_ff_out, gains, w_in_rows, padded, axis):
    n = lax.axis_size(axis)
    width = tokens.shape[1]
    units = n // 2 * padded
    pairs = width // LANES
    gather = lambda shard: lax.all_gather(shard, axis, axis=0, tiled=True)
    at_once = lambda matrix: (jnp.zeros((1,), jnp.int32), (matrix[None],))
    w_qkv, w_ff = at_once(gather(w_qkv)), at_once(gather(pad_units(w_ff_out, n, padded)))
    w_in = at_once(jnp.concatenate([gather(w_in), gather(w_attn_out)]))
    gains = gather(gains.reshape(1, 2, -1)).astype(F32).transpose(1, 0, 2).reshape(2, width)
    cosine, sine, seg_column, seg_row = tables(segment)
    qkv, hidden_one, gains = project(tokens, cosine, sine, w_qkv, 3 * width, gains)
    attn_out, lse = attend(qkv, seg_column, seg_row, width, 0, pairs)
    resid, mixed, mid, grad_heads, g_out, g_two, g_in, g_ff = ffn(
        tokens, attn_out, cotangent, gains, w_in, w_ff, units, 2 * units, width, width
    )
    output = ffn_out(resid, mixed, w_ff, width)
    grad_projected = attend_back(qkv, attn_out, grad_heads, lse, seg_column, seg_row, cosine, sine, 0, pairs)
    g_qkv = project_grad(grad_projected, hidden_one)
    grad_tokens, g_one = norm_back(hidden_back(grad_projected, w_qkv, 3 * width), tokens, mid, gains)
    scatter = lambda grad: lax.psum_scatter(grad, axis, scatter_dimension=0, tiled=True).astype(F32)
    g_in = g_in.reshape(2 * units, width)
    g_ff = drop_units(scatter(g_ff), n, padded, w_in_rows)
    return output, grad_tokens, scatter(g_qkv), scatter(g_out), scatter(g_in), g_ff, g_one, g_two


class Box:
    pass


def by_links(tokens, cotangent, segment, w_qkv, w_attn_out, w_in, w_ff_out, gains, w_in_rows, padded, axis):
    n = lax.axis_size(axis)
    width = tokens.shape[1]
    units = n // 2 * padded
    pairs = width // LANES
    rows_qkv, rows_out, rows_ff = w_qkv.shape[0], w_attn_out.shape[0], w_ff_out.shape[0]
    v = Box()
    gain_rows = jnp.pad(gains[None], ((0, 7), (0, width - gains.shape[0])))
    s_qkv = Spread(jnp.concatenate([w_qkv, gain_rows]), axis, LEVEL)
    s_in = Spread(jnp.concatenate([w_in, w_attn_out]), axis, LEVEL)
    s_qkv.shard, w_ff_out = tie(s_qkv.shard, w_ff_out)
    s_ff = Spread(pad_units(w_ff_out, n, padded), axis, UPRIGHT)
    r_ff = Reduce(axis, UPRIGHT, units, direct=True)
    r_in = Reduce(axis, LEVEL, width)
    r_qkv = Reduce(axis, LEVEL, width, halves=True, direct=True)
    v.cosine, v.sine, v.seg_column, v.seg_row = tables(segment)

    s_qkv.near()
    s_ff.near()
    s_qkv.nearer()
    together((s_qkv, "block"), (s_in, "shard"), (s_ff, "first"), (s_ff, "third"), *((v, k) for k in vars(v)))
    s_qkv.far_one()
    s_qkv.far_three()
    s_in.near()
    s_ff.nearer()
    together((s_qkv, "one"), (s_qkv, "three"), (s_qkv, "block"), (s_in, "first"), (s_in, "third"), (s_ff, "block"))
    s_qkv.farther()
    s_in.nearer()
    s_qkv.swap("block", "one", "three")
    together(
        (s_qkv, "two"), (s_qkv, "other_block"), (s_qkv, "other_three"), (s_qkv, "other_one"),
        (s_in, "block"), (s_ff, "block"),
    )
    s_in.far_one()
    s_in.far_three()
    s_ff.far_one()
    s_qkv.swap("two")
    s_ff.swap("block")
    w_qkv = s_qkv.result()
    v.qkv, v.hidden_one, v.gains = project(tokens, v.cosine, v.sine, w_qkv, rows_qkv)
    together((v, "qkv"), (s_ff, "one"), (s_ff, "block"), (s_in, "block"), (s_ff, "other_block"))
    s_ff.far_three()
    s_ff.swap("one")
    s_in.swap("block")
    attend_some = lambda first, number, done=None: attend(v.qkv, v.seg_column, v.seg_row, width, first, number, done)
    v.done = attend_some(0, pairs // 2)
    together(
        (v, "done"), (s_in, "one"), (s_in, "three"), (s_ff, "one"), (s_ff, "three"),
        (s_in, "other_block"), (s_ff, "other_one"),
    )
    s_in.farther()
    s_ff.farther()
    s_in.swap("one", "three")
    s_ff.swap("three")
    v.done = attend_some(pairs // 2, pairs // 2, v.done)
    together(
        (v, "done"), (s_in, "two"), (s_ff, "two"), (s_in, "other_one"), (s_in, "other_three"), (s_ff, "other_three")
    )
    s_in.swap("two")
    s_ff.swap("two")
    attn_out, lse = v.done
    w_in, w_ff = s_in.result(), s_ff.result()
    rows_of = lambda grad: grad.reshape(n, -1, grad.shape[-1])
    resid, v.mixed, mid, v.heads, v.g_out, g_two, v.g_in, g_ff = ffn(
        tokens, attn_out, cotangent, v.gains, w_in, w_ff, units, padded, rows_out, rows_ff
    )

    def back(first, number):
        v.some = attend_back(
            v.qkv, attn_out, v.heads, lse, v.seg_column, v.seg_row, v.cosine, v.sine,
            first * pairs // 8, number * pairs // 8, v.some,
        )

    v.some = None
    r_ff.pair((rows_of(g_ff),))
    back(0, 1)
    together((v, "some"), (r_ff, "twins"), (v, "g_in"), (v, "g_out"))
    r_in.pair((rows_of(v.g_in), rows_of(v.g_out)))
    r_ff.pack()
    together((v, "some"), (r_ff, "one"), (r_ff, "two"))
    r_ff.far()
    back(1, 2)
    together((v, "some"), (r_in, "twins"))
    r_in.pack()
    together((v, "some"), (r_in, "one"), (r_in, "two"))
    r_in.far()
    back(3, 2)
    together((v, "some"), (r_ff, "one"), (r_ff, "two"))
    r_ff.repack()
    together((v, "some"), (r_ff, "three"))
    r_ff.farther()
    back(5, 2)
    together((v, "some"), (r_in, "one"), (r_in, "two"), (r_ff, "three"))
    r_in.repack()
    together((v, "some"), (r_in, "three"), (r_ff, "three"))
    r_in.farther()
    back(7, 1)
    together((v, "some"), (r_ff, "three"))
    r_ff.gather()
    together((v, "some"), (r_ff, "one"), (r_ff, "two"))
    r_ff.near()
    v.stay, v.go = project_grad_halves(v.some, v.hidden_one, rows_qkv, place(axis)[1])
    together((v, "some"), (v, "stay"), (v, "go"), (r_in, "three"), (r_ff, "one"), (r_ff, "two"), (r_ff, "three"))
    half_of = lambda grad: grad.reshape(n // 2, -1, width)
    r_qkv.pair((half_of(v.stay),), (half_of(v.go),))
    r_in.gather()
    together((v, "some"), (r_qkv, "twins"), (r_in, "one"), (r_in, "two"))
    r_in.near()
    r_qkv.pack()
    together((v, "some"), (r_qkv, "one"), (r_qkv, "two"))
    r_qkv.far()
    v.hidden = hidden_back(v.some, w_qkv, rows_qkv)
    together((v, "hidden"), (r_in, "one"), (r_in, "two"))
    r_in.nearer()
    together((v, "hidden"), (r_qkv, "one"), (r_qkv, "two"), (r_ff, "one"), (r_ff, "two"), (r_ff, "three"))
    v.g_ff = drop_units(r_ff.result(), n, padded, w_in_rows)
    r_qkv.repack()
    together((v, "hidden"), (r_qkv, "three"))
    r_qkv.farther()
    v.grad_tokens, v.g_one = norm_back(v.hidden, tokens, mid, v.gains)
    together((v, "grad_tokens"), (v, "g_one"), (r_qkv, "three"), (r_in, "three"))
    r_qkv.gather()
    together((v, "mixed"), (r_qkv, "one"), (r_qkv, "two"), (r_qkv, "three"), (r_qkv, "rest"))
    r_qkv.near()
    v.output = ffn_out(resid, v.mixed, w_ff, rows_ff)
    together((v, "output"), (r_qkv, "one"), (r_qkv, "two"), (r_qkv, "three"), (r_in, "three"))
    rest = r_in.result()
    return v.output, v.grad_tokens, r_qkv.result(), rest[padded:], rest[:padded], v.g_ff, v.g_one, g_two


def body(tokens, cotangent, segment, w_qkv, w_attn_out, w_in, w_ff_out, norm_one, norm_two):
    axis = "fsdp"
    n = lax.axis_size(axis)
    rows_in = w_in.shape[0]
    padded = -(-rows_in // 16) * 16
    w_in = jnp.pad(w_in, ((0, padded - rows_in), (0, 0)))
    scales = norm_one.shape[0]
    aligned = not (any(w.shape[0] % 16 for w in (w_qkv, w_attn_out, w_ff_out)) or scales & (scales - 1))
    way = by_links if aligned and n == 2 * Z * Y * X else by_collectives
    output, grad_tokens, g_qkv, g_out, g_in, g_ff, g_one, g_two = way(
        tokens, cotangent, segment, w_qkv, w_attn_out, w_in, w_ff_out, jnp.concatenate([norm_one, norm_two]), rows_in, padded, axis
    )
    g_norms = sum_norms(n, axis, g_one, g_two)
    g_in = g_in[:rows_in]
    return (output, grad_tokens, g_qkv, g_out, g_in, g_ff, g_norms[0], g_norms[1])


def solution(mesh):
    rows, flat = P("fsdp", None), P("fsdp")
    return jax.shard_map(
        body,
        mesh=mesh,
        in_specs=(rows, rows, flat, rows, rows, rows, rows, flat, flat),
        out_specs=(rows, rows, rows, rows, rows, rows, flat, flat),
        check_vma=False,
    )
```
